256 devices in a mesh: tile: 128 (over z_hi, x, y, core), member: 2 (over z_lo).
Axes of the slice: x: 4, y: 4, z: 8 (z_hi: 4, z_lo: 2; z = z_hi * 2 + z_lo), core: 2. Of those that a mesh axis runs over, the one named last changes fastest.
Arguments:
- fields: bfloat16 [2, 128, 2, 32, 32, 128], P('member', 'tile'), may hold values from -6 to 6
- cotangent: bfloat16 [2, 128, 2, 32, 32, 128], P('member', 'tile'), may hold values from -6 to 6
- edge_map: int32 [128, 4, 2], P('tile'), may hold values from 0 to 3, as said below
- w_first: bfloat16 [3, 3, 128, 128], replicated, may hold values from -0.1875 to 0.1875
- b_first: float32 [128], replicated, may hold values from -3 to 3
- w_second: bfloat16 [3, 3, 128, 128], replicated, may hold values from -0.1875 to 0.1875
- b_second: float32 [128], replicated, may hold values from -3 to 3
Outputs:
- response: bfloat16 [2, 128, 2, 32, 32, 128], P('member', 'tile')
- field_grad: bfloat16 [2, 128, 2, 32, 32, 128], P('member', 'tile')
- first_kernel_grad: float32 [3, 3, 128, 128], replicated
- first_bias_grad: float32 [128], replicated
- second_kernel_grad: float32 [3, 3, 128, 128], replicated
- second_bias_grad: float32 [128], replicated
The draws below stay inside these ranges and needn't reach their ends.
Inputs may be any that keep to these rules, and one draw needn't show every extreme that they name: Each tile t is its own grid turned by r quarter turns: edge_map[t, g, 0] = (g - r) mod 4, and edge_map[t, g, 1] is 1 exactly when r = 2, or r = 1 and g is even, or r = 3 and g is odd.
All inputs are finite; a program needn't handle non-finite values.
Results may differ from the reference program's by a relative error of at most 0.0065.
Values may be sent and summed in bfloat16 or wider, within the bound.
A program may use at most 64 MiB of HBM per device.

```python
import jax
import jax.numpy as jnp
from jax import lax

CHANNELS = 128
TILE_SIDE = 32
FRAMES = 2
ROW_TILES = 8
ALL_TILES = 128
MEMBERS = 2
SAMPLES = 524288


def draw_edge_map(key, part):
    quarter_turns = jax.random.randint(key, (ALL_TILES,), 0, 4, dtype=jnp.int32)
    directions = jnp.arange(4, dtype=jnp.int32)
    side_ids = (directions[None, :] - quarter_turns[:, None]) % 4
    parity = directions[None, :] % 2
    turned = quarter_turns[:, None]
    against = (turned == 2) | (turned == 1) & (parity == 0) | (turned == 3) & (parity == 1)
    return jnp.stack([side_ids, against.astype(jnp.int32)], axis=2).astype(jnp.int32)


def shard_levels(stream_key, dims, cuts, low, largest):
    level, own = 1.0, jax.random.fold_in(stream_key, 6)
    for axis_at, blocks in cuts:
        draws = jnp.exp(jax.random.uniform(jax.random.fold_in(own, axis_at), (blocks,), jnp.float32, low / len(cuts), largest / len(cuts)))
        level = level * jnp.repeat(draws, dims[axis_at] // blocks).reshape([-1 if axis == axis_at else 1 for axis in range(len(dims))])
    return level


def scatter_about(stream_key, dims, width, bound, cuts=(), held_as=jnp.bfloat16):
    values = width * jax.random.normal(stream_key, dims, jnp.float32)
    if cuts:
        values = values * shard_levels(stream_key, dims, cuts, -0.22, 0.18)
    return jnp.clip(values, -bound, bound).astype(held_as)


def setup_inputs(seed: int = 0) -> dict:
    key_of = jax.random.split(jax.random.key(seed), 8)
    return {
        "fields": scatter_about(key_of[0], (MEMBERS, ALL_TILES, FRAMES, TILE_SIDE, TILE_SIDE, CHANNELS), 1.0, 6.0, ((0, 2), (1, 128))),
        "cotangent": scatter_about(key_of[1], (MEMBERS, ALL_TILES, FRAMES, TILE_SIDE, TILE_SIDE, CHANNELS), 1.0, 6.0, ((0, 2), (1, 128))),
        "edge_map": draw_edge_map(jax.random.fold_in(key_of[7], 71), 0),
        "w_first": scatter_about(key_of[3], (3, 3, CHANNELS, CHANNELS), (9 * CHANNELS) ** -0.5, 0.1875),
        "b_first": scatter_about(key_of[4], (CHANNELS,), 0.5, 3.0, (), jnp.float32),
        "w_second": scatter_about(key_of[5], (3, 3, CHANNELS, CHANNELS), (9 * CHANNELS) ** -0.5, 0.1875),
        "b_second": scatter_about(key_of[6], (CHANNELS,), 0.5, 3.0, (), jnp.float32),
    }


ROOT_HALF = 0.7071067811865476
INV_ROOT_TAU = 0.3989422804014327


def gelu_value(inputs):
    return 0.5 * inputs * (1.0 + jax.scipy.special.erf(inputs * ROOT_HALF))


def gelu_slope(inputs):
    return 0.5 * (1.0 + jax.scipy.special.erf(inputs * ROOT_HALF)) + inputs * jnp.exp(-0.5 * inputs * inputs) * INV_ROOT_TAU


def patches(padded):
    out_rows = padded.shape[-3] - 2
    out_cols = padded.shape[-2] - 2
    pieces = [padded[..., row_off:row_off + out_rows, col_off:col_off + out_cols, :] for row_off in range(3) for col_off in range(3)]
    joined = jnp.concatenate(pieces, axis=-1)
    return joined.reshape(-1, joined.shape[-1])


def rim_strips(tile_data):
    return jnp.stack([tile_data[..., 0, :, :], tile_data[..., :, -1, :], tile_data[..., -1, :, :], tile_data[..., :, 0, :]], axis=-4)


def orient(strips, chosen_ids, flip_ids):
    shaped_ids = chosen_ids.reshape(chosen_ids.shape + (1, 1, 1))
    shaped_flips = flip_ids.reshape(flip_ids.shape + (1, 1, 1))
    chosen = jnp.zeros_like(strips)
    for candidate in range(4):
        chosen = jnp.where(shaped_ids == candidate, jnp.expand_dims(strips[..., candidate, :, :, :], -4), chosen)
    flipped = chosen[..., ::-1, :]
    return jnp.where(shaped_flips == 1, flipped, chosen)


def assemble(tile_data, placed):
    top_rim = placed[..., 0, :, :, :]
    right_rim = placed[..., 1, :, :, :]
    bottom_rim = placed[..., 2, :, :, :]
    left_rim = placed[..., 3, :, :, :]
    kind = tile_data.dtype
    top_left = (0.5 * (top_rim[..., 0, :].astype(jnp.float32) + left_rim[..., 0, :].astype(jnp.float32))).astype(kind)
    top_right = (0.5 * (top_rim[..., -1, :].astype(jnp.float32) + right_rim[..., 0, :].astype(jnp.float32))).astype(kind)
    low_left = (0.5 * (bottom_rim[..., 0, :].astype(jnp.float32) + left_rim[..., -1, :].astype(jnp.float32))).astype(kind)
    low_right = (0.5 * (bottom_rim[..., -1, :].astype(jnp.float32) + right_rim[..., -1, :].astype(jnp.float32))).astype(kind)
    top_row = jnp.concatenate([top_left[..., None, :], top_rim, top_right[..., None, :]], axis=-2)
    bottom_row = jnp.concatenate([low_left[..., None, :], bottom_rim, low_right[..., None, :]], axis=-2)
    middle = jnp.concatenate([left_rim[..., :, None, :], tile_data, right_rim[..., :, None, :]], axis=-2)
    return jnp.concatenate([top_row[..., None, :, :], middle, bottom_row[..., None, :, :]], axis=-3)


def fold_rims(grad_pad):
    interior = grad_pad[..., 1:-1, 1:-1, :]
    top_left = 0.5 * grad_pad[..., 0, 0, :]
    top_right = 0.5 * grad_pad[..., 0, -1, :]
    low_left = 0.5 * grad_pad[..., -1, 0, :]
    low_right = 0.5 * grad_pad[..., -1, -1, :]
    top_rim = grad_pad[..., 0, 1:-1, :].at[..., 0, :].add(top_left).at[..., -1, :].add(top_right)
    right_rim = grad_pad[..., 1:-1, -1, :].at[..., 0, :].add(top_right).at[..., -1, :].add(low_right)
    bottom_rim = grad_pad[..., -1, 1:-1, :].at[..., 0, :].add(low_left).at[..., -1, :].add(low_right)
    left_rim = grad_pad[..., 1:-1, 0, :].at[..., 0, :].add(top_left).at[..., -1, :].add(low_left)
    return interior, jnp.stack([top_rim, right_rim, bottom_rim, left_rim], axis=-4)


def spread(interior, edge_grads):
    interior = interior.at[..., 0, :, :].add(edge_grads[..., 0, :, :, :])
    interior = interior.at[..., :, -1, :].add(edge_grads[..., 1, :, :, :])
    interior = interior.at[..., -1, :, :].add(edge_grads[..., 2, :, :, :])
    return interior.at[..., :, 0, :].add(edge_grads[..., 3, :, :, :])


def route_rims(outgoing):
    tile_ids = jnp.arange(ALL_TILES)
    sources = [(tile_ids - ROW_TILES) % ALL_TILES, (tile_ids + 1) % ALL_TILES, (tile_ids + ROW_TILES) % ALL_TILES, (tile_ids - 1) % ALL_TILES]
    return jnp.stack([outgoing[:, sources[direction], (direction + 2) % 4] for direction in range(4)], axis=2)


def pad_all(tile_data, tables):
    side_ids, flip_marks, inverse, inverse_marks = tables
    outgoing = orient(rim_strips(tile_data), side_ids, flip_marks)
    incoming = route_rims(outgoing)
    return assemble(tile_data, orient(incoming, inverse, inverse_marks))


def unpad_all(grad_pad, tables):
    side_ids, flip_marks, inverse, inverse_marks = tables
    interior, placed = fold_rims(grad_pad)
    outgoing = orient(placed, side_ids, flip_marks)
    incoming = route_rims(outgoing)
    return spread(interior, orient(incoming, inverse, inverse_marks))


def conv_tiles(padded, weights_cat):
    leading = padded.shape[:2]
    flattened = padded.reshape((-1,) + padded.shape[2:])

    def one_tile(tile_pad):
        product = jnp.dot(patches(tile_pad), weights_cat, preferred_element_type=jnp.float32)
        return product.reshape(tile_pad.shape[0], tile_pad.shape[1] - 2, tile_pad.shape[2] - 2, -1)

    result = lax.map(one_tile, flattened)
    return result.reshape(leading + result.shape[1:])


def weight_total(padded, grad_data):
    flat_pad = padded.reshape((-1,) + padded.shape[2:])
    flat_grad = grad_data.reshape((-1,) + grad_data.shape[2:])

    def accumulate(running, tile_pair):
        tile_pad, tile_grad = tile_pair
        tile_term = lax.dot_general(patches(tile_pad), tile_grad.reshape(-1, tile_grad.shape[-1]), (((0,), (0,)), ((), ())), preferred_element_type=jnp.float32)
        return running + tile_term, None

    start_sum = jnp.zeros((9 * CHANNELS, CHANNELS), jnp.float32)
    total, ignored = lax.scan(accumulate, start_sum, (flat_pad, flat_grad))
    return total.reshape(3, 3, CHANNELS, CHANNELS)


def back_conv(grad_data, weights_flip):
    zero_pad = jnp.pad(grad_data, ((0, 0), (0, 0), (0, 0), (2, 2), (2, 2), (0, 0)))
    return conv_tiles(zero_pad, weights_flip)


def reference(fields, cotangent, edge_map, w_first, b_first, w_second, b_second):
    side_ids = edge_map[:, :, 0]
    flip_marks = edge_map[:, :, 1]
    directions = jnp.arange(4, dtype=jnp.int32)
    inverse = jnp.sum(directions[None, None, :] * (side_ids[:, None, :] == directions[None, :, None]), axis=2).astype(jnp.int32)
    inverse_marks = jnp.take_along_axis(flip_marks, inverse, axis=1)
    tables = (side_ids, flip_marks, inverse, inverse_marks)
    first_cat = w_first.reshape(9 * CHANNELS, CHANNELS)
    second_cat = w_second.reshape(9 * CHANNELS, CHANNELS)
    first_flip = w_first[::-1, ::-1].transpose(0, 1, 3, 2).reshape(9 * CHANNELS, CHANNELS)
    second_flip = w_second[::-1, ::-1].transpose(0, 1, 3, 2).reshape(9 * CHANNELS, CHANNELS)
    pad_first = pad_all(fields, tables)
    hidden_one = conv_tiles(pad_first, first_cat) + b_first
    activity = gelu_value(hidden_one).astype(jnp.bfloat16)
    pad_second = pad_all(activity, tables)
    hidden_two = conv_tiles(pad_second, second_cat) + b_second
    response = gelu_value(hidden_two).astype(jnp.bfloat16)
    grad_second = (cotangent.astype(jnp.float32) * gelu_slope(hidden_two)).astype(jnp.bfloat16)
    norm_scale = float(SAMPLES) ** -0.5
    kernel_two = weight_total(pad_second, grad_second) * norm_scale
    bias_two = jnp.sum(grad_second.astype(jnp.float32), axis=(0, 1, 2, 3, 4)) * norm_scale
    grad_act = unpad_all(back_conv(grad_second, second_flip), tables)
    grad_first = (grad_act * gelu_slope(hidden_one)).astype(jnp.bfloat16)
    kernel_one = weight_total(pad_first, grad_first) * norm_scale
    bias_one = jnp.sum(grad_first.astype(jnp.float32), axis=(0, 1, 2, 3, 4)) * norm_scale
    field_grad = unpad_all(back_conv(grad_first, first_flip), tables).astype(jnp.bfloat16)
    return (response, field_grad, kernel_one, bias_one, kernel_two, bias_two)
```

```python
import functools

import jax
import jax.numpy as jnp
from jax import lax
from jax.experimental import pallas as pl
from jax.experimental.pallas import tpu as pltpu
from jax.sharding import PartitionSpec as P

ROW_TILES = 8


ROOT_HALF = 0.7071067811865476
INV_ROOT_TAU = 0.3989422804014327


def shifted(value, axis, steps):
    count = lax.axis_size(axis)
    pairs = [(source, (source + steps) % count) for source in range(count)]
    return lax.ppermute(value, axis, pairs)


PLANE = 16
DEPTH = 8
PIECE = 5
PART_ROWS = 2 * PLANE * PIECE * 8


def coordinates():
    tile = lax.axis_index("tile")
    member = lax.axis_index("member")
    core = lax.rem(tile, 2)
    spot = lax.rem(tile // 2, PLANE)
    floor = tile // (2 * PLANE)
    return tile, member, core, spot, floor


def sum_partners():
    tile, member, core, spot, floor = coordinates()
    mate = (tile - core + (1 - core), member)
    plane = [
        ((floor * PLANE + lax.rem(spot + step, PLANE)) * 2 + core, member)
        for step in range(1, PLANE)
    ]
    level = floor * 2 + member
    column = []
    for step in range(1, DEPTH):
        other = lax.rem(level + step, DEPTH)
        column.append((((other // 2) * PLANE + spot) * 2 + core, lax.rem(other, 2)))
    return mate, plane, column


def remote(source, target, send_sem, recv_sem, device):
    return pltpu.make_async_remote_copy(
        src_ref=source,
        dst_ref=target,
        send_sem=send_sem,
        recv_sem=recv_sem,
        device_id=device,
        device_id_type=pl.DeviceIdType.MESH,
    )


def sum_scratch():
    dma = pltpu.SemaphoreType.DMA
    return [
        pltpu.VMEM((2, PLANE, PIECE, 8, 128), jnp.float32),
        pltpu.VMEM((2, PLANE, PIECE, 8, 128), jnp.bfloat16),
        pltpu.VMEM((PLANE, PIECE, 8, 128), jnp.bfloat16),
        pltpu.VMEM((PLANE, PIECE, 8, 128), jnp.float32),
        pltpu.VMEM((PLANE, PIECE, 8, 128), jnp.bfloat16),
        pltpu.VMEM((PLANE, PIECE, 8, 128), jnp.bfloat16),
        pltpu.VMEM((DEPTH, PIECE, 8, 128), jnp.bfloat16),
        pltpu.VMEM((2, PLANE, PIECE, 8, 128), jnp.bfloat16),
        dma((2,)),
        dma((2, PLANE)),
        dma((2, DEPTH)),
        dma((2, PLANE)),
        dma((2, PLANE)),
    ]


class GradientSum:
    def __init__(self, refs):
        (
            self.own,
            self.halves,
            self.from_mate,
            self.total,
            self.pieces,
            self.from_plane,
            self.from_column,
            self.gathered,
            self.mate_sem,
            self.plane_sem,
            self.column_sem,
            self.gather_sem,
            self.forward_sem,
        ) = refs
        tile, member, core, spot, floor = coordinates()
        self.core, self.spot, self.level = core, spot, floor * 2 + member
        self.mate, self.plane, self.column = sum_partners()

    def to_mate(self):
        return remote(
            self.halves.at[1 - self.core],
            self.from_mate,
            self.mate_sem.at[0],
            self.mate_sem.at[1],
            self.mate,
        )

    def to_plane(self, step):
        target = lax.rem(self.spot + step, PLANE)
        return remote(
            self.pieces.at[target],
            self.from_plane.at[self.spot],
            self.plane_sem.at[0, step],
            self.plane_sem.at[1, step],
            self.plane[step - 1],
        )

    def to_column(self, step):
        return remote(
            self.from_column.at[self.level],
            self.from_column.at[self.level],
            self.column_sem.at[0, step],
            self.column_sem.at[1, step],
            self.column[step - 1],
        )

    def to_gather(self, step):
        return remote(
            self.gathered.at[self.core, self.spot],
            self.gathered.at[self.core, self.spot],
            self.gather_sem.at[0, step],
            self.gather_sem.at[1, step],
            self.plane[step - 1],
        )

    def to_forward(self, step):
        origin = lax.rem(self.spot + PLANE - step, PLANE)
        return remote(
            self.gathered.at[self.core, origin],
            self.gathered.at[self.core, origin],
            self.forward_sem.at[0, step],
            self.forward_sem.at[1, step],
            self.mate,
        )

    def start(self):
        self.halves[...] = self.own[...].astype(jnp.bfloat16)
        self.to_mate().start()

    def spread_plane(self):
        self.to_mate().wait_recv()
        total = self.own[self.core] + self.from_mate[...].astype(jnp.float32)
        self.total[...] = total
        self.pieces[...] = total.astype(jnp.bfloat16)
        for step in range(1, PLANE):
            self.to_plane(step).start()

    def spread_column(self):
        value = self.total[self.spot]
        for step in range(1, PLANE):
            self.to_plane(step).wait_recv()
            origin = lax.rem(self.spot + PLANE - step, PLANE)
            value = value + self.from_plane[origin].astype(jnp.float32)
        self.from_column[self.level] = value.astype(jnp.bfloat16)
        for step in range(1, DEPTH):
            self.to_column(step).start()

    def gather_plane(self):
        for step in range(1, DEPTH):
            self.to_column(step).wait_recv()
        value = jnp.zeros((PIECE, 8, 128), jnp.float32)
        for level in range(DEPTH):
            value = value + self.from_column[level].astype(jnp.float32)
        self.gathered[self.core, self.spot] = value.astype(jnp.bfloat16)
        for step in range(1, PLANE):
            self.to_gather(step).start()
        self.to_forward(0).start()

    def forward(self):
        for step in range(1, PLANE):
            self.to_gather(step).wait_recv()
            self.to_forward(step).start()

    def finish(self):
        for step in range(PLANE):
            self.to_forward(step).wait_recv()

    def drain(self):
        self.to_mate().wait_send()
        for step in range(1, PLANE):
            self.to_plane(step).wait_send()
            self.to_gather(step).wait_send()
        for step in range(1, DEPTH):
            self.to_column(step).wait_send()
        for step in range(PLANE):
            self.to_forward(step).wait_send()


def greet(partners):
    barrier = pltpu.get_barrier_semaphore()
    for device in partners:
        pl.semaphore_signal(
            barrier, inc=1, device_id=device, device_id_type=pl.DeviceIdType.MESH
        )
    pl.semaphore_wait(barrier, len(partners))


def sum_kernel(scale, kernel_one, bias_one, kernel_two, bias_two, kernel_one_out, bias_one_out,
               kernel_two_out, bias_two_out, *scratch):
    count = len(sum_scratch())
    sums = (GradientSum(scratch[:count]), GradientSum(scratch[count:]))
    mate, plane, column = sum_partners()
    greet([mate, *plane, *column])
    sources = ((kernel_one, bias_one), (kernel_two, bias_two))
    targets = ((kernel_one_out, bias_one_out), (kernel_two_out, bias_two_out))
    for one, (kernel, bias) in zip(sums, sources):
        extra = jnp.concatenate(
            [bias[...], jnp.zeros((PART_ROWS - kernel.shape[0] - 1, 128), jnp.float32)], axis=0
        )
        full = jnp.concatenate([kernel[...], extra], axis=0)
        one.own[...] = full.reshape(one.own.shape)
        one.start()
    for one in sums:
        one.spread_plane()
    for one in sums:
        one.spread_column()
    for one in sums:
        one.gather_plane()
    for one in sums:
        one.forward()
    for one, (kernel, bias) in zip(sums, targets):
        one.finish()
        full = one.gathered[...].astype(jnp.float32).reshape(PART_ROWS, 128) * scale
        kernel[...] = full[: kernel.shape[0]]
        bias[...] = full[kernel.shape[0] : kernel.shape[0] + 1]
    for one in sums:
        one.drain()


def sum_gradients(scale, kernel_one, bias_one, kernel_two, bias_two):
    channels = kernel_one.shape[-1]
    flat = (
        kernel_one.reshape(-1, channels),
        bias_one.reshape(1, channels),
        kernel_two.reshape(-1, channels),
        bias_two.reshape(1, channels),
    )
    outs = pl.pallas_call(
        functools.partial(sum_kernel, scale),
        out_shape=[jax.ShapeDtypeStruct(x.shape, x.dtype) for x in flat],
        in_specs=[pl.BlockSpec(memory_space=pltpu.VMEM)] * 4,
        out_specs=[pl.BlockSpec(memory_space=pltpu.VMEM)] * 4,
        scratch_shapes=sum_scratch() + sum_scratch(),
        compiler_params=pltpu.CompilerParams(collective_id=0, has_side_effects=True),
    )(*flat)
    return (
        outs[0].reshape(kernel_one.shape),
        outs[1].reshape(bias_one.shape),
        outs[2].reshape(kernel_two.shape),
        outs[3].reshape(bias_two.shape),
    )


def gelu_value(inputs):
    return 0.5 * inputs * (1.0 + jax.scipy.special.erf(inputs * ROOT_HALF))


def gelu_slope(inputs):
    return (
        0.5 * (1.0 + jax.scipy.special.erf(inputs * ROOT_HALF))
        + inputs * jnp.exp(-0.5 * inputs * inputs) * INV_ROOT_TAU
    )


def patches(padded):
    out_rows = padded.shape[-3] - 2
    out_cols = padded.shape[-2] - 2
    pieces = [
        padded[..., row_off : row_off + out_rows, col_off : col_off + out_cols, :]
        for row_off in range(3)
        for col_off in range(3)
    ]
    joined = jnp.concatenate(pieces, axis=-1)
    return joined.reshape(-1, joined.shape[-1])


def rim_strips(tile_data):
    return jnp.stack(
        [
            tile_data[..., 0, :, :],
            tile_data[..., :, -1, :],
            tile_data[..., -1, :, :],
            tile_data[..., :, 0, :],
        ],
        axis=-4,
    )


def orient(strips, chosen_ids, flip_ids):
    shaped_ids = chosen_ids.reshape(chosen_ids.shape + (1, 1, 1))
    shaped_flips = flip_ids.reshape(flip_ids.shape + (1, 1, 1))
    chosen = jnp.zeros_like(strips)
    for candidate in range(4):
        chosen = jnp.where(
            shaped_ids == candidate, jnp.expand_dims(strips[..., candidate, :, :, :], -4), chosen
        )
    flipped = chosen[..., ::-1, :]
    return jnp.where(shaped_flips == 1, flipped, chosen)


def assemble(tile_data, placed):
    top_rim = placed[..., 0, :, :, :]
    right_rim = placed[..., 1, :, :, :]
    bottom_rim = placed[..., 2, :, :, :]
    left_rim = placed[..., 3, :, :, :]
    kind = tile_data.dtype
    top_left = (
        0.5 * (top_rim[..., 0, :].astype(jnp.float32) + left_rim[..., 0, :].astype(jnp.float32))
    ).astype(kind)
    top_right = (
        0.5 * (top_rim[..., -1, :].astype(jnp.float32) + right_rim[..., 0, :].astype(jnp.float32))
    ).astype(kind)
    low_left = (
        0.5 * (bottom_rim[..., 0, :].astype(jnp.float32) + left_rim[..., -1, :].astype(jnp.float32))
    ).astype(kind)
    low_right = (
        0.5
        * (bottom_rim[..., -1, :].astype(jnp.float32) + right_rim[..., -1, :].astype(jnp.float32))
    ).astype(kind)
    top_row = jnp.concatenate([top_left[..., None, :], top_rim, top_right[..., None, :]], axis=-2)
    bottom_row = jnp.concatenate(
        [low_left[..., None, :], bottom_rim, low_right[..., None, :]], axis=-2
    )
    middle = jnp.concatenate(
        [left_rim[..., :, None, :], tile_data, right_rim[..., :, None, :]], axis=-2
    )
    return jnp.concatenate([top_row[..., None, :, :], middle, bottom_row[..., None, :, :]], axis=-3)


def fold_rims(grad_pad):
    interior = grad_pad[..., 1:-1, 1:-1, :]
    top_left = 0.5 * grad_pad[..., 0, 0, :]
    top_right = 0.5 * grad_pad[..., 0, -1, :]
    low_left = 0.5 * grad_pad[..., -1, 0, :]
    low_right = 0.5 * grad_pad[..., -1, -1, :]
    top_rim = grad_pad[..., 0, 1:-1, :].at[..., 0, :].add(top_left).at[..., -1, :].add(top_right)
    right_rim = (
        grad_pad[..., 1:-1, -1, :].at[..., 0, :].add(top_right).at[..., -1, :].add(low_right)
    )
    bottom_rim = (
        grad_pad[..., -1, 1:-1, :].at[..., 0, :].add(low_left).at[..., -1, :].add(low_right)
    )
    left_rim = grad_pad[..., 1:-1, 0, :].at[..., 0, :].add(top_left).at[..., -1, :].add(low_left)
    return (interior, jnp.stack([top_rim, right_rim, bottom_rim, left_rim], axis=-4))


def spread(interior, edge_grads):
    interior = interior.at[..., 0, :, :].add(edge_grads[..., 0, :, :, :])
    interior = interior.at[..., :, -1, :].add(edge_grads[..., 1, :, :, :])
    interior = interior.at[..., -1, :, :].add(edge_grads[..., 2, :, :, :])
    return interior.at[..., :, 0, :].add(edge_grads[..., 3, :, :, :])


def trade_rims(outgoing):
    offsets = (ROW_TILES, -1, -ROW_TILES, 1)
    received = []
    for direction in range(4):
        received.append(shifted(outgoing[(direction + 2) % 4], "tile", offsets[direction]))
    return jnp.stack(received)


def trade_grads(outgoing):
    offsets = (ROW_TILES, -1, -ROW_TILES, 1)
    received = []
    for direction in range(4):
        received.append(
            shifted(
                outgoing[(direction + 2) % 4].astype(jnp.bfloat16), "tile", offsets[direction]
            ).astype(jnp.float32)
        )
    return jnp.stack(received)


def pad_tile(tile_data, tables):
    side_ids, flip_marks, inverse, inverse_marks = tables
    outgoing = orient(rim_strips(tile_data), side_ids, flip_marks)
    incoming = trade_rims(outgoing)
    return assemble(tile_data, orient(incoming, inverse, inverse_marks))


def unpad_tile(grad_pad, tables):
    side_ids, flip_marks, inverse, inverse_marks = tables
    interior, placed = fold_rims(grad_pad)
    outgoing = orient(placed, side_ids, flip_marks)
    incoming = trade_grads(outgoing)
    return spread(interior, orient(incoming, inverse, inverse_marks))


def apply_cat(padded, weights_cat, out_rows, out_cols):
    product = jnp.dot(patches(padded), weights_cat, preferred_element_type=jnp.float32)
    return product.reshape(padded.shape[0], out_rows, out_cols, -1)


def forward_conv(tile_data, weights_cat, tables):
    tile_side = tile_data.shape[1]
    padded = pad_tile(tile_data, tables)
    result = apply_cat(padded, weights_cat, tile_side, tile_side)
    return (result, padded)


def back_conv(grad_data, weights_flip):
    tile_side = grad_data.shape[1]
    zero_pad = jnp.pad(grad_data, ((0, 0), (2, 2), (2, 2), (0, 0)))
    return apply_cat(zero_pad, weights_flip, tile_side + 2, tile_side + 2)


def kernel_term(padded, grad_data):
    channels = grad_data.shape[-1]
    total = lax.dot_general(
        patches(padded),
        grad_data.reshape(-1, channels),
        (((0,), (0,)), ((), ())),
        preferred_element_type=jnp.float32,
    )
    return total.reshape(3, 3, channels, channels)


def per_device(fields, cotangent, edge_map, w_first, b_first, w_second, b_second):
    frames, tile_side, channels = (fields.shape[2], fields.shape[3], fields.shape[5])
    source = fields.reshape(fields.shape[2:])
    upstream = cotangent.reshape(cotangent.shape[2:])
    side_ids = edge_map[0, :, 0]
    flip_marks = edge_map[0, :, 1]
    directions = jnp.arange(4, dtype=jnp.int32)
    inverse = jnp.sum(directions[None, :] * (side_ids[None, :] == directions[:, None]), axis=1)
    inverse_marks = jnp.take(flip_marks, inverse)
    tables = (side_ids, flip_marks, inverse, inverse_marks)
    first_cat = w_first.reshape(9 * channels, channels)
    second_cat = w_second.reshape(9 * channels, channels)
    first_flip = w_first[::-1, ::-1].transpose(0, 1, 3, 2).reshape(9 * channels, channels)
    second_flip = w_second[::-1, ::-1].transpose(0, 1, 3, 2).reshape(9 * channels, channels)
    norm_scale = float(
        lax.axis_size("tile") * lax.axis_size("member") * frames * tile_side * tile_side
    ) ** (-0.5)
    pre_one, pad_first = forward_conv(source, first_cat, tables)
    hidden_one = pre_one + b_first
    activity = gelu_value(hidden_one).astype(jnp.bfloat16)
    pre_two, pad_second = forward_conv(activity, second_cat, tables)
    hidden_two = pre_two + b_second
    response = gelu_value(hidden_two).astype(jnp.bfloat16)
    grad_second = (upstream.astype(jnp.float32) * gelu_slope(hidden_two)).astype(jnp.bfloat16)
    kernel_two = kernel_term(pad_second, grad_second)
    bias_two = jnp.sum(grad_second.astype(jnp.float32), axis=(0, 1, 2))
    grad_act = unpad_tile(back_conv(grad_second, second_flip), tables)
    grad_first = (grad_act * gelu_slope(hidden_one)).astype(jnp.bfloat16)
    kernel_one = kernel_term(pad_first, grad_first)
    bias_one = jnp.sum(grad_first.astype(jnp.float32), axis=(0, 1, 2))
    field_grad = unpad_tile(back_conv(grad_first, first_flip), tables).astype(jnp.bfloat16)
    kernel_one, bias_one, kernel_two, bias_two = sum_gradients(
        norm_scale, kernel_one, bias_one, kernel_two, bias_two
    )
    return (
        response.reshape(fields.shape),
        field_grad.reshape(fields.shape),
        kernel_one,
        bias_one,
        kernel_two,
        bias_two,
    )


def solution(mesh):
    in_specs = (
        P("member", "tile", None, None, None, None),
        P("member", "tile", None, None, None, None),
        P("tile", None, None),
        P(),
        P(),
        P(),
        P(),
    )
    out_specs = (
        P("member", "tile", None, None, None, None),
        P("member", "tile", None, None, None, None),
        P(),
        P(),
        P(),
        P(),
    )
    return jax.shard_map(
        per_device, mesh=mesh, in_specs=in_specs, out_specs=out_specs, check_vma=False
    )
```

```python
import functools

import jax
import jax.numpy as jnp
from jax import lax
from jax.experimental import pallas as pl
from jax.experimental.pallas import tpu as pltpu
from jax.sharding import PartitionSpec as P

ROW_TILES = 8
ROOT_HALF = 0.7071067811865476
INV_ROOT_TAU = 0.3989422804014327
BF16 = jnp.bfloat16
F32 = jnp.float32

PLANE = 16
DEPTH = 8
PIECE = 5
HALF = PLANE * PIECE
PART_ROWS = 2 * HALF * 8


def coordinates():
    tile = lax.axis_index("tile")
    member = lax.axis_index("member")
    core = lax.rem(tile, 2)
    spot = lax.rem(tile // 2, PLANE)
    floor = tile // (2 * PLANE)
    return tile, member, core, spot, floor


def sum_partners():
    tile, member, core, spot, floor = coordinates()
    mate = (tile - core + (1 - core), member)
    plane = [
        ((floor * PLANE + lax.rem(spot + step, PLANE)) * 2 + core, member)
        for step in range(1, PLANE)
    ]
    level = floor * 2 + member
    column = []
    for step in range(1, DEPTH):
        other = lax.rem(level + step, DEPTH)
        column.append((((other // 2) * PLANE + spot) * 2 + core, lax.rem(other, 2)))
    return mate, plane, column


def remote(source, target, send_sem, recv_sem, device):
    return pltpu.make_async_remote_copy(
        src_ref=source,
        dst_ref=target,
        send_sem=send_sem,
        recv_sem=recv_sem,
        device_id=device,
        device_id_type=pl.DeviceIdType.MESH,
    )


def sum_scratch():
    dma = pltpu.SemaphoreType.DMA
    return [
        pltpu.VMEM((2 * HALF, 8, 128), jnp.float32),
        pltpu.VMEM((2 * HALF, 8, 128), jnp.bfloat16),
        pltpu.VMEM((HALF, 8, 128), jnp.bfloat16),
        pltpu.VMEM((PLANE, PIECE, 8, 128), jnp.float32),
        pltpu.VMEM((PLANE, PIECE, 8, 128), jnp.bfloat16),
        pltpu.VMEM((PLANE, PIECE, 8, 128), jnp.bfloat16),
        pltpu.VMEM((DEPTH, PIECE, 8, 128), jnp.bfloat16),
        pltpu.VMEM((2, PLANE, PIECE, 8, 128), jnp.bfloat16),
        dma((2,)),
        dma((2, PLANE)),
        dma((2, DEPTH)),
        dma((2, PLANE)),
        dma((2, PLANE)),
    ]


class GradientSum:
    def __init__(self, refs):
        (
            self.own,
            self.halves,
            self.from_mate,
            self.total,
            self.pieces,
            self.from_plane,
            self.from_column,
            self.gathered,
            self.mate_sem,
            self.plane_sem,
            self.column_sem,
            self.gather_sem,
            self.forward_sem,
        ) = refs
        tile, member, core, spot, floor = coordinates()
        self.core, self.spot, self.level = core, spot, floor * 2 + member
        self.mate, self.plane, self.column = sum_partners()

    def to_mate(self):
        return remote(
            self.halves.at[pl.ds((1 - self.core) * HALF, HALF)],
            self.from_mate,
            self.mate_sem.at[0],
            self.mate_sem.at[1],
            self.mate,
        )

    def to_plane(self, step):
        target = lax.rem(self.spot + step, PLANE)
        return remote(
            self.pieces.at[target],
            self.from_plane.at[self.spot],
            self.plane_sem.at[0, step],
            self.plane_sem.at[1, step],
            self.plane[step - 1],
        )

    def to_column(self, step):
        return remote(
            self.from_column.at[self.level],
            self.from_column.at[self.level],
            self.column_sem.at[0, step],
            self.column_sem.at[1, step],
            self.column[step - 1],
        )

    def to_gather(self, step):
        return remote(
            self.gathered.at[self.core, self.spot],
            self.gathered.at[self.core, self.spot],
            self.gather_sem.at[0, step],
            self.gather_sem.at[1, step],
            self.plane[step - 1],
        )

    def to_forward(self, step):
        origin = lax.rem(self.spot + PLANE - step, PLANE)
        return remote(
            self.gathered.at[self.core, origin],
            self.gathered.at[self.core, origin],
            self.forward_sem.at[0, step],
            self.forward_sem.at[1, step],
            self.mate,
        )

    def start(self):
        self.halves[...] = self.own[...].astype(jnp.bfloat16)
        self.to_mate().start()

    def spread_plane(self):
        self.to_mate().wait_recv()
        total = self.own[pl.ds(self.core * HALF, HALF)] + self.from_mate[...].astype(jnp.float32)
        total = total.reshape(PLANE, PIECE, 8, 128)
        self.total[...] = total
        self.pieces[...] = total.astype(jnp.bfloat16)
        for step in range(1, PLANE):
            self.to_plane(step).start()

    def spread_column(self):
        value = self.total[self.spot]
        for step in range(1, PLANE):
            self.to_plane(step).wait_recv()
            origin = lax.rem(self.spot + PLANE - step, PLANE)
            value = value + self.from_plane[origin].astype(jnp.float32)
        self.from_column[self.level] = value.astype(jnp.bfloat16)
        for step in range(1, DEPTH):
            self.to_column(step).start()

    def gather_plane(self):
        for step in range(1, DEPTH):
            self.to_column(step).wait_recv()
        value = jnp.zeros((PIECE, 8, 128), jnp.float32)
        for level in range(DEPTH):
            value = value + self.from_column[level].astype(jnp.float32)
        self.gathered[self.core, self.spot] = value.astype(jnp.bfloat16)
        for step in range(1, PLANE):
            self.to_gather(step).start()
        self.to_forward(0).start()

    def forward(self):
        for step in range(1, PLANE):
            self.to_gather(step).wait_recv()
            self.to_forward(step).start()

    def finish(self):
        for step in range(PLANE):
            self.to_forward(step).wait_recv()

    def drain(self):
        self.to_mate().wait_send()
        for step in range(1, PLANE):
            self.to_plane(step).wait_send()
            self.to_gather(step).wait_send()
        for step in range(1, DEPTH):
            self.to_column(step).wait_send()
        for step in range(PLANE):
            self.to_forward(step).wait_send()


def dot(left, right):
    return jnp.dot(left, right, preferred_element_type=F32)


def dot_nt(left, right):
    return lax.dot_general(left, right, (((1,), (1,)), ((), ())), preferred_element_type=F32)


def dot_tn(left, right):
    return lax.dot_general(left, right, (((0,), (0,)), ((), ())), preferred_element_type=F32)


def iota(shape, axis):
    return lax.broadcasted_iota(jnp.int32, shape, axis)


def ones_where(mask):
    return jnp.where(mask, 1.0, 0.0).astype(BF16)


def border_pixel(side, place):
    return jnp.where(
        side == 0,
        place,
        jnp.where(side == 1, place * 32 + 31, jnp.where(side == 2, place + 992, place * 32)),
    )


def facing(edge_map, index):
    direction, place = index >> 5, index & 31
    side = jnp.zeros_like(index)
    flip = jnp.zeros_like(index)
    for candidate in range(4):
        side = jnp.where(direction == candidate, edge_map[candidate, 0], side)
        flip = jnp.where(direction == candidate, edge_map[candidate, 1], flip)
    return side, jnp.where(flip == 1, 31 - place, place)


def ring_taps(tap):
    row, lane = iota((128, 128), 0), iota((128, 128), 1)
    side, place = row >> 5, row & 31
    halo_side, halo_place = lane >> 5, lane & 31
    wanted = place + (tap - 1)
    whole = (halo_side == side) & (halo_place == wanted)
    along = (side == 0) | (side == 2)
    end = jnp.where(side == 0, 0, 31)
    low = ((halo_side == side) & (halo_place == 0)) | ((halo_side == 3) & (halo_place == end))
    high = ((halo_side == side) & (halo_place == 31)) | ((halo_side == 1) & (halo_place == end))
    half = along & (((wanted == -1) & low) | ((wanted == 32) & high))
    return jnp.where(whole, 1.0, jnp.where(half, 0.5, 0.0)).astype(BF16)


def side_tap(side, tap):
    return ((0, tap), (tap, 2), (2, tap), (tap, 0))[side]


def split_float(value):
    high = value.astype(BF16)
    low = (value - high.astype(F32)).astype(BF16)
    return jnp.concatenate([high, low], axis=0)


def make_tables(edge_map, t):
    row, lane = iota((128, 128), 0), iota((128, 128), 1)
    side, place = facing(edge_map, row)
    pixel = border_pixel(side, place)
    plain = border_pixel(row >> 5, row & 31)
    turn = ones_where(lane == side * 32 + place)
    for block in range(8):
        here = lane + block * 128
        t.pick[:, block * 128 : (block + 1) * 128] = ones_where(here == pixel)
        t.border[:, block * 128 : (block + 1) * 128] = ones_where(here == plain)
    lane_side, lane_place = facing(edge_map, lane)
    lane_pixel = border_pixel(lane_side, lane_place)
    lane_plain = border_pixel(lane >> 5, lane & 31)
    for block in range(8):
        here = row + block * 128
        rows = slice(block * 128, (block + 1) * 128)
        t.put_in[rows, :] = ones_where(here == lane_pixel)
        marks = ones_where(here == lane_plain)
        t.put[rows, 0:128] = marks
        t.put[rows, 128:256] = marks
    for tap in range(3):
        taps = ring_taps(tap)
        t.ring[tap * 128 : (tap + 1) * 128, :] = dot_nt(taps, turn).astype(BF16)
        back = dot_nt(turn, taps).astype(BF16)
        t.ring_back[:, tap * 128 : (tap + 1) * 128] = back
        t.ring_back[:, 384 + tap * 128 : 384 + (tap + 1) * 128] = back


def lay_weights(target, block):
    empty = jnp.zeros((384, 128), BF16)
    target[0, :, 128:256] = empty
    target[3, :, 0:128] = empty
    for row in range(3):
        for col in range(3):
            part = block(row, col)
            target[row, col * 128 : (col + 1) * 128, 0:128] = part
            target[row + 1, col * 128 : (col + 1) * 128, 128:256] = part


def lay_shifted(target, frame, pair, value):
    col = iota((64, 128), 0) & 31
    before = jnp.where(col == 0, 0.0, pltpu.roll(value, 1, 0))
    after = jnp.where(col == 31, 0.0, pltpu.roll(value, 63, 0))
    for tap, part in enumerate((before, value, after)):
        target[frame, pl.ds(1 + 2 * pair, 2), :, tap * 128 : (tap + 1) * 128] = part.astype(
            BF16
        ).reshape(2, 32, 128)


def lay_rows(target, frame, pair, value):
    part = value.reshape(2, 32, 128)
    for tap in range(3):
        target[frame, pl.ds(2 * pair + tap, 2), :, tap * 128 : (tap + 1) * 128] = part


def clear_rims(shifted):
    for frame in range(2):
        shifted[frame, 0] = jnp.zeros((32, 384), BF16)
        shifted[frame, 33] = jnp.zeros((32, 384), BF16)
        shifted[frame, 34] = jnp.zeros((32, 384), BF16)


def tile_conv(shifted, weights, result):
    for frame in range(2):
        total = None
        for row in range(4):
            rows = shifted[frame, row : row + 32].reshape(16, 2, 32, 384)[:, 0].reshape(512, 384)
            part = dot(rows, weights[row])
            total = part if total is None else total + part
        pairs = slice(frame * 16, (frame + 1) * 16)
        result[pairs, 0:32, :] = total[:, 0:128].reshape(16, 32, 128)
        result[pairs, 32:64, :] = total[:, 128:256].reshape(16, 32, 128)


def transpose_shifted(shifted, target):
    for frame in range(2):
        for tap in range(3):
            lanes = slice(tap * 128, (tap + 1) * 128)
            target[lanes, frame * 1024 : (frame + 1) * 1024] = (
                shifted[frame, 1:33, :, lanes].reshape(1024, 128).T
            )


def picked(table, image):
    parts = [
        dot(table[...], image[frame * 16 : (frame + 1) * 16].reshape(1024, 128))
        for frame in range(2)
    ]
    return jnp.concatenate(parts, axis=1).astype(BF16)


def halo_share(t, arrived, weights, ring_rows, share):
    around = dot(t.ring[...], arrived[...].reshape(128, 256)).astype(BF16)
    parts = []
    for side in range(4):
        for frame in range(2):
            lanes = slice(frame * 128, (frame + 1) * 128)
            ring_rows[side, frame * 32 : (frame + 1) * 32, :] = jnp.concatenate(
                [
                    around[tap * 128 + side * 32 : tap * 128 + (side + 1) * 32, lanes]
                    for tap in range(3)
                ],
                axis=1,
            )
        taps = jnp.concatenate([weights[side_tap(side, tap)] for tap in range(3)], axis=0)
        value = dot(ring_rows[side], taps)
        parts.append(jnp.concatenate([value[0:32], value[32:64]], axis=1))
    both = split_float(jnp.concatenate(parts, axis=0))
    share[...] = dot(t.put[...], both).reshape(16, 64, 256)


def ring_gradient(t, image, weights, border_rows, leaving):
    border = picked(t.border, image)
    rows = [[None] * 4 for tap in range(3)]
    for side in range(4):
        here = border[side * 32 : (side + 1) * 32]
        border_rows[side] = jnp.concatenate([here[:, 0:128], here[:, 128:256]], axis=0)
        for tap in range(3):
            value = dot_nt(border_rows[side], weights[side_tap(side, tap)])
            rows[tap][side] = jnp.concatenate([value[0:32], value[32:64]], axis=1)
    stacked = jnp.concatenate([rows[tap][side] for tap in range(3) for side in range(4)], axis=0)
    leaving[...] = dot(t.ring_back[...], split_float(stacked)).astype(BF16).reshape(4, 32, 256)


def kernel_gradient(turned, spread_rows, ring_rows, border_rows, bias, block, own):
    total = None
    for frame in range(2):
        part = dot(
            turned[:, frame * 1024 : (frame + 1) * 1024],
            spread_rows[frame, 1:33].reshape(1024, 384),
        )
        total = part if total is None else total + part
    block[...] = total
    for side in range(4):
        part = dot_tn(ring_rows[side], border_rows[side])
        for tap in range(3):
            row, col = side_tap(side, tap)
            at = (slice(col * 128, (col + 1) * 128), slice(row * 128, (row + 1) * 128))
            block[at] += part[tap * 128 : (tap + 1) * 128]
    for row in range(3):
        for col in range(3):
            first = (row * 3 + col) * 16
            own[first : first + 16] = block[
                col * 128 : (col + 1) * 128, row * 128 : (row + 1) * 128
            ].reshape(16, 8, 128)
    own[144] = jnp.concatenate([bias, jnp.zeros((7, 128), F32)], axis=0)
    own[145:160] = jnp.zeros((15, 8, 128), F32)


def halo_partners():
    tile, member, core, spot, floor = coordinates()
    count = 2 * PLANE * (DEPTH // 2)
    steps = (count - ROW_TILES, 1, ROW_TILES, count - 1)
    return [(lax.rem(tile + step, count), member) for step in steps]


class Halo:
    def __init__(self, leaving, arrived, send_sem, recv_sem):
        self.leaving, self.arrived = leaving, arrived
        self.send_sem, self.recv_sem = send_sem, recv_sem
        self.partners = halo_partners()

    def copies(self, turn):
        return [
            remote(
                self.leaving.at[turn, way],
                self.arrived.at[turn, (way + 2) % 4],
                self.send_sem.at[turn, way],
                self.recv_sem.at[turn, (way + 2) % 4],
                self.partners[way],
            )
            for way in range(4)
        ]

    def start(self, turn):
        for copy in self.copies(turn):
            copy.start()

    def wait(self, turn):
        for copy in self.copies(turn):
            copy.wait_recv()

    def drain(self):
        for turn in range(4):
            for copy in self.copies(turn):
                copy.wait_send()


TABLES = {
    "pick": (128, 1024),
    "border": (128, 1024),
    "put_in": (1024, 128),
    "put": (1024, 256),
    "ring": (384, 128),
    "ring_back": (128, 768),
}
IMAGE = (32, 64, 128)
SHIFTED = (2, 36, 32, 384)
BUFFERS = {
    "source": (IMAGE, BF16),
    "upstream": (IMAGE, BF16),
    "first": ((3, 3, 128, 128), BF16),
    "second": ((3, 3, 128, 128), BF16),
    "first_fwd": ((4, 384, 256), BF16),
    "first_back": ((4, 384, 256), BF16),
    "second_fwd": ((4, 384, 256), BF16),
    "second_back": ((4, 384, 256), BF16),
    "shift_one": (SHIFTED, BF16),
    "shift_two": (SHIFTED, BF16),
    "shift_grad": (SHIFTED, BF16),
    "row_grad": ((2, 34, 32, 384), BF16),
    "turned_one": ((384, 2048), BF16),
    "turned_two": ((384, 2048), BF16),
    "hidden": (IMAGE, F32),
    "share": ((16, 64, 256), F32),
    "slope": (IMAGE, F32),
    "act": (IMAGE, BF16),
    "response": (IMAGE, BF16),
    "grad": (IMAGE, BF16),
    "field_grad": (IMAGE, BF16),
    "ring_one": ((4, 64, 384), BF16),
    "ring_two": ((4, 64, 384), BF16),
    "border_grad": ((4, 64, 128), BF16),
    "block": ((384, 384), F32),
    "leaving": ((4, 4, 32, 256), BF16),
    "arrived": ((4, 4, 32, 256), BF16),
}


class Names:
    def __init__(self, names, refs):
        for name, ref in zip(names, refs):
            setattr(self, name, ref)


def step_scratch():
    dma = pltpu.SemaphoreType.DMA
    return (
        [pltpu.VMEM(shape, BF16) for shape in TABLES.values()]
        + [pltpu.VMEM(shape, kind) for shape, kind in BUFFERS.values()]
        + [dma((4, 4)), dma((4, 4)), dma((6,))]
        + sum_scratch()
        + sum_scratch()
    )


def gelu_parts(hidden):
    bell = 0.5 * (1.0 + lax.erf(hidden * ROOT_HALF))
    return hidden * bell, bell + hidden * jnp.exp(-0.5 * hidden * hidden) * INV_ROOT_TAU


def each_pair(body, start=0):
    def step(pair, carry):
        for frame in range(2):
            carry = body(frame, pair, frame * 16 + pair, slice(frame * 128, (frame + 1) * 128), carry)
        return carry

    return lax.fori_loop(0, 16, step, start)


def fold_rows(value):
    return jnp.sum(value.reshape(8, 8, 128), axis=0)


def step_kernel(scale, edge_map, fields, cotangent, w_first, b_first, w_second, b_second,
                response_out, field_grad_out, kernel_one_out, bias_one_out, kernel_two_out,
                bias_two_out, *scratch):
    tables, scratch = Names(TABLES, scratch), scratch[len(TABLES) :]
    v, scratch = Names(BUFFERS, scratch), scratch[len(BUFFERS) :]
    halo = Halo(v.leaving, v.arrived, scratch[0], scratch[1])
    local_sem, scratch = scratch[2], scratch[3:]
    count = len(sum_scratch())
    sum_one, sum_two = GradientSum(scratch[:count]), GradientSum(scratch[count:])

    loads = [
        pltpu.make_async_copy(source, target, local_sem.at[index])
        for index, (source, target) in enumerate(
            ((fields, v.source), (w_first, v.first), (w_second, v.second), (cotangent, v.upstream))
        )
    ]
    for load in loads:
        load.start()
    mate, plane, column = sum_partners()
    partners = [*halo_partners(), mate, *plane, *column]
    barrier = pltpu.get_barrier_semaphore()
    for device in partners:
        pl.semaphore_signal(
            barrier, inc=1, device_id=device, device_id_type=pl.DeviceIdType.MESH
        )
    make_tables(edge_map, tables)
    loads[0].wait()
    v.leaving[0] = picked(tables.pick, v.source).reshape(4, 32, 256)
    pl.semaphore_wait(barrier, len(partners))
    halo.start(0)

    for shifted in (v.shift_one, v.shift_two, v.shift_grad):
        clear_rims(shifted)
    for frame in range(2):
        v.row_grad[frame, 32:34, :, 0:128] = jnp.zeros((2, 32, 128), BF16)
        v.row_grad[frame, 0:2, :, 256:384] = jnp.zeros((2, 32, 128), BF16)

    def shift_source(frame, pair, index, lanes, carry):
        lay_shifted(v.shift_one, frame, pair, v.source[index].astype(F32))
        return carry

    each_pair(shift_source)
    loads[1].wait()
    lay_weights(v.first_fwd, lambda row, col: v.first[row, col])
    tile_conv(v.shift_one, v.first_fwd, v.hidden)
    loads[2].wait()
    lay_weights(v.second_fwd, lambda row, col: v.second[row, col])
    halo.wait(0)
    halo_share(tables, v.arrived.at[0], v.first, v.ring_one, v.share)

    def activate(frame, pair, index, lanes, carry):
        hidden = v.hidden[index] + v.share[pair, :, lanes] + b_first[...]
        value, slope = gelu_parts(hidden)
        v.slope[index] = slope
        v.act[index] = value.astype(BF16)
        lay_shifted(v.shift_two, frame, pair, value)
        return carry

    each_pair(activate)
    v.leaving[1] = picked(tables.pick, v.act).reshape(4, 32, 256)
    halo.start(1)
    tile_conv(v.shift_two, v.second_fwd, v.hidden)
    lay_weights(v.second_back, lambda row, col: v.second[2 - row, 2 - col].T)
    lay_weights(v.first_back, lambda row, col: v.first[2 - row, 2 - col].T)
    loads[3].wait()
    halo.wait(1)
    halo_share(tables, v.arrived.at[1], v.second, v.ring_two, v.share)

    def respond(frame, pair, index, lanes, carry):
        hidden = v.hidden[index] + v.share[pair, :, lanes] + b_second[...]
        value, slope = gelu_parts(hidden)
        v.response[index] = value.astype(BF16)
        grad = (v.upstream[index].astype(F32) * slope).astype(BF16)
        v.grad[index] = grad
        wide = grad.astype(F32)
        lay_shifted(v.shift_grad, frame, pair, wide)
        lay_rows(v.row_grad, frame, pair, grad)
        return carry + fold_rows(wide)

    bias = each_pair(respond, jnp.zeros((8, 128), F32))
    bias = jnp.sum(bias, axis=0, keepdims=True)
    response_store = pltpu.make_async_copy(v.response, response_out, local_sem.at[4])
    response_store.start()
    ring_gradient(tables, v.grad, v.second, v.border_grad, v.leaving.at[2])
    halo.start(2)
    transpose_shifted(v.shift_two, v.turned_two)
    kernel_gradient(
        v.turned_two, v.row_grad, v.ring_two, v.border_grad, bias, v.block, sum_two.own
    )
    sum_two.start()
    tile_conv(v.shift_grad, v.second_back, v.hidden)
    transpose_shifted(v.shift_one, v.turned_one)
    sum_two.spread_plane()
    halo.wait(2)
    v.share[...] = dot(tables.put_in[...], v.arrived[2].reshape(128, 256)).reshape(16, 64, 256)

    def descend(frame, pair, index, lanes, carry):
        grad = ((v.hidden[index] + v.share[pair, :, lanes]) * v.slope[index]).astype(BF16)
        v.grad[index] = grad
        wide = grad.astype(F32)
        lay_shifted(v.shift_grad, frame, pair, wide)
        lay_rows(v.row_grad, frame, pair, grad)
        return carry + fold_rows(wide)

    bias = each_pair(descend, jnp.zeros((8, 128), F32))
    bias = jnp.sum(bias, axis=0, keepdims=True)
    ring_gradient(tables, v.grad, v.first, v.border_grad, v.leaving.at[3])
    halo.start(3)
    kernel_gradient(
        v.turned_one, v.row_grad, v.ring_one, v.border_grad, bias, v.block, sum_one.own
    )
    sum_one.start()
    sum_two.spread_column()
    sum_one.spread_plane()
    tile_conv(v.shift_grad, v.first_back, v.hidden)
    sum_two.gather_plane()
    sum_one.spread_column()
    halo.wait(3)
    v.share[...] = dot(tables.put_in[...], v.arrived[3].reshape(128, 256)).reshape(16, 64, 256)

    def finish(frame, pair, index, lanes, carry):
        v.field_grad[index] = (v.hidden[index] + v.share[pair, :, lanes]).astype(BF16)
        return carry

    each_pair(finish)
    field_grad_store = pltpu.make_async_copy(v.field_grad, field_grad_out, local_sem.at[5])
    field_grad_store.start()
    sum_two.forward()
    sum_one.gather_plane()
    sum_one.forward()
    for one, kernel_out, bias_out in (
        (sum_two, kernel_two_out, bias_two_out),
        (sum_one, kernel_one_out, bias_one_out),
    ):
        one.finish()
        full = one.gathered[...].reshape(PART_ROWS, 128)
        rows = kernel_out.shape[0]
        kernel_out[...] = full[:rows].astype(F32) * scale
        bias_out[...] = full[rows : rows + 8].astype(F32)[0:1] * scale
    response_store.wait()
    field_grad_store.wait()
    halo.drain()
    sum_one.drain()
    sum_two.drain()


def per_device(fields, cotangent, edge_map, w_first, b_first, w_second, b_second):
    frames, tile_side, channels = (fields.shape[2], fields.shape[3], fields.shape[5])
    samples = lax.axis_size("tile") * lax.axis_size("member") * frames * tile_side * tile_side
    kernel = jax.ShapeDtypeStruct((9 * channels, channels), F32)
    bias = jax.ShapeDtypeStruct((1, channels), F32)
    image = jax.ShapeDtypeStruct(IMAGE, BF16)
    anywhere = pl.BlockSpec(memory_space=pl.ANY)
    local = pl.BlockSpec(memory_space=pltpu.VMEM)
    outs = pl.pallas_call(
        functools.partial(step_kernel, float(samples) ** -0.5),
        out_shape=[image, image, kernel, bias, kernel, bias],
        in_specs=[
            pl.BlockSpec(memory_space=pltpu.SMEM),
            anywhere,
            anywhere,
            anywhere,
            local,
            anywhere,
            local,
        ],
        out_specs=[anywhere, anywhere, local, local, local, local],
        scratch_shapes=step_scratch(),
        compiler_params=pltpu.CompilerParams(collective_id=0, has_side_effects=True),
    )(
        edge_map.reshape(4, 2),
        fields.reshape(IMAGE),
        cotangent.reshape(IMAGE),
        w_first,
        b_first.reshape(1, channels),
        w_second,
        b_second.reshape(1, channels),
    )
    return (
        outs[0].reshape(fields.shape),
        outs[1].reshape(fields.shape),
        outs[2].reshape(w_first.shape),
        outs[3].reshape(b_first.shape),
        outs[4].reshape(w_second.shape),
        outs[5].reshape(b_second.shape),
    )


def solution(mesh):
    in_specs = (
        P("member", "tile", None, None, None, None),
        P("member", "tile", None, None, None, None),
        P("tile", None, None),
        P(),
        P(),
        P(),
        P(),
    )
    out_specs = (
        P("member", "tile", None, None, None, None),
        P("member", "tile", None, None, None, None),
        P(),
        P(),
        P(),
        P(),
    )
    return jax.shard_map(
        per_device, mesh=mesh, in_specs=in_specs, out_specs=out_specs, check_vma=False
    )
```

```python
import functools

import jax
import jax.numpy as jnp
from jax import lax
from jax.experimental import pallas as pl
from jax.experimental.pallas import tpu as pltpu
from jax.sharding import PartitionSpec as P

ROW_TILES = 8
ROOT_HALF = 0.7071067811865476
INV_ROOT_TAU = 0.3989422804014327
BF16 = jnp.bfloat16
F32 = jnp.float32

PLANE = 16
DEPTH = 8
PIECE = 5
HALF = PLANE * PIECE
PART_ROWS = 2 * HALF * 8


def coordinates():
    tile = lax.axis_index("tile")
    member = lax.axis_index("member")
    core = lax.rem(tile, 2)
    spot = lax.rem(tile // 2, PLANE)
    floor = tile // (2 * PLANE)
    return tile, member, core, spot, floor


def sum_partners():
    tile, member, core, spot, floor = coordinates()
    mate = (tile - core + (1 - core), member)
    plane = [
        ((floor * PLANE + lax.rem(spot + step, PLANE)) * 2 + core, member)
        for step in range(1, PLANE)
    ]
    level = floor * 2 + member
    column = []
    for step in range(1, DEPTH):
        other = lax.rem(level + step, DEPTH)
        column.append((((other // 2) * PLANE + spot) * 2 + core, lax.rem(other, 2)))
    return mate, plane, column


def remote(source, target, send_sem, recv_sem, device):
    return pltpu.make_async_remote_copy(
        src_ref=source,
        dst_ref=target,
        send_sem=send_sem,
        recv_sem=recv_sem,
        device_id=device,
        device_id_type=pl.DeviceIdType.MESH,
    )


def sum_scratch():
    dma = pltpu.SemaphoreType.DMA
    return [
        pltpu.VMEM((2 * HALF, 8, 128), jnp.float32),
        pltpu.VMEM((2 * HALF, 8, 128), jnp.bfloat16),
        pltpu.VMEM((HALF, 8, 128), jnp.bfloat16),
        pltpu.VMEM((PLANE, PIECE, 8, 128), jnp.float32),
        pltpu.VMEM((PLANE, PIECE, 8, 128), jnp.bfloat16),
        pltpu.VMEM((PLANE, PIECE, 8, 128), jnp.bfloat16),
        pltpu.VMEM((DEPTH, PIECE, 8, 128), jnp.bfloat16),
        pltpu.VMEM((2, PLANE, PIECE, 8, 128), jnp.bfloat16),
        dma((2,)),
        dma((2, PLANE)),
        dma((2, DEPTH)),
        dma((2, PLANE)),
        dma((2, PLANE)),
    ]


class GradientSum:
    def __init__(self, refs):
        (
            self.own,
            self.halves,
            self.from_mate,
            self.total,
            self.pieces,
            self.from_plane,
            self.from_column,
            self.gathered,
            self.mate_sem,
            self.plane_sem,
            self.column_sem,
            self.gather_sem,
            self.forward_sem,
        ) = refs
        tile, member, core, spot, floor = coordinates()
        self.core, self.spot, self.level = core, spot, floor * 2 + member
        self.mate, self.plane, self.column = sum_partners()

    def to_mate(self):
        return remote(
            self.halves.at[pl.ds((1 - self.core) * HALF, HALF)],
            self.from_mate,
            self.mate_sem.at[0],
            self.mate_sem.at[1],
            self.mate,
        )

    def to_plane(self, step):
        target = lax.rem(self.spot + step, PLANE)
        return remote(
            self.pieces.at[target],
            self.from_plane.at[self.spot],
            self.plane_sem.at[0, step],
            self.plane_sem.at[1, step],
            self.plane[step - 1],
        )

    def to_column(self, step):
        return remote(
            self.from_column.at[self.level],
            self.from_column.at[self.level],
            self.column_sem.at[0, step],
            self.column_sem.at[1, step],
            self.column[step - 1],
        )

    def to_gather(self, step):
        return remote(
            self.gathered.at[self.core, self.spot],
            self.gathered.at[self.core, self.spot],
            self.gather_sem.at[0, step],
            self.gather_sem.at[1, step],
            self.plane[step - 1],
        )

    def to_forward(self, step):
        origin = lax.rem(self.spot + PLANE - step, PLANE)
        return remote(
            self.gathered.at[self.core, origin],
            self.gathered.at[self.core, origin],
            self.forward_sem.at[0, step],
            self.forward_sem.at[1, step],
            self.mate,
        )

    def start(self):
        self.halves[...] = self.own[...].astype(jnp.bfloat16)
        self.to_mate().start()

    def spread_plane(self):
        self.to_mate().wait_recv()
        total = self.own[pl.ds(self.core * HALF, HALF)] + self.from_mate[...].astype(jnp.float32)
        total = total.reshape(PLANE, PIECE, 8, 128)
        self.total[...] = total
        self.pieces[...] = total.astype(jnp.bfloat16)
        for step in range(1, PLANE):
            self.to_plane(step).start()

    def spread_column(self):
        value = self.total[self.spot]
        for step in range(1, PLANE):
            self.to_plane(step).wait_recv()
            origin = lax.rem(self.spot + PLANE - step, PLANE)
            value = value + self.from_plane[origin].astype(jnp.float32)
        self.from_column[self.level] = value.astype(jnp.bfloat16)
        for step in range(1, DEPTH):
            self.to_column(step).start()

    def gather_plane(self):
        for step in range(1, DEPTH):
            self.to_column(step).wait_recv()
        value = jnp.zeros((PIECE, 8, 128), jnp.float32)
        for level in range(DEPTH):
            value = value + self.from_column[level].astype(jnp.float32)
        self.gathered[self.core, self.spot] = value.astype(jnp.bfloat16)
        for step in range(1, PLANE):
            self.to_gather(step).start()
        self.to_forward(0).start()

    def forward(self):
        for step in range(1, PLANE):
            self.to_gather(step).wait_recv()
            self.to_forward(step).start()

    def finish(self):
        for step in range(PLANE):
            self.to_forward(step).wait_recv()

    def drain(self):
        self.to_mate().wait_send()
        for step in range(1, PLANE):
            self.to_plane(step).wait_send()
            self.to_gather(step).wait_send()
        for step in range(1, DEPTH):
            self.to_column(step).wait_send()
        for step in range(PLANE):
            self.to_forward(step).wait_send()


def dot(left, right):
    return jnp.dot(left, right, preferred_element_type=F32)


def dot_nt(left, right):
    return lax.dot_general(left, right, (((1,), (1,)), ((), ())), preferred_element_type=F32)


def dot_tn(left, right):
    return lax.dot_general(left, right, (((0,), (0,)), ((), ())), preferred_element_type=F32)


def iota(shape, axis):
    return lax.broadcasted_iota(jnp.int32, shape, axis)


def ones_where(mask):
    return jnp.where(mask, 1.0, 0.0).astype(BF16)


def border_pixel(side, place):
    return jnp.where(
        side == 0,
        place,
        jnp.where(side == 1, place * 32 + 31, jnp.where(side == 2, place + 992, place * 32)),
    )


def facing(edge_map, index):
    direction, place = index >> 5, index & 31
    side = jnp.zeros_like(index)
    flip = jnp.zeros_like(index)
    for candidate in range(4):
        side = jnp.where(direction == candidate, edge_map[0, candidate], side)
        flip = jnp.where(direction == candidate, edge_map[1, candidate], flip)
    return side, jnp.where(flip == 1, 31 - place, place)


def ring_taps(tap):
    row, lane = iota((128, 128), 0), iota((128, 128), 1)
    side, place = row >> 5, row & 31
    halo_side, halo_place = lane >> 5, lane & 31
    wanted = place + (tap - 1)
    whole = (halo_side == side) & (halo_place == wanted)
    along = (side == 0) | (side == 2)
    end = jnp.where(side == 0, 0, 31)
    low = ((halo_side == side) & (halo_place == 0)) | ((halo_side == 3) & (halo_place == end))
    high = ((halo_side == side) & (halo_place == 31)) | ((halo_side == 1) & (halo_place == end))
    half = along & (((wanted == -1) & low) | ((wanted == 32) & high))
    return jnp.where(whole, 1.0, jnp.where(half, 0.5, 0.0)).astype(BF16)


def side_tap(side, tap):
    return ((0, tap), (tap, 2), (2, tap), (tap, 0))[side]


def split_float(value):
    high = value.astype(BF16)
    low = (value - high.astype(F32)).astype(BF16)
    return jnp.concatenate([high, low], axis=0)


def make_tables(edge_map, t):
    row, lane = iota((128, 128), 0), iota((128, 128), 1)
    side, place = facing(edge_map, row)
    pixel = border_pixel(side, place)
    plain = border_pixel(row >> 5, row & 31)
    turn = ones_where(lane == side * 32 + place)
    for block in range(8):
        here = lane + block * 128
        t.pick[:, block * 128 : (block + 1) * 128] = ones_where(here == pixel)
        t.border[:, block * 128 : (block + 1) * 128] = ones_where(here == plain)
    lane_side, lane_place = facing(edge_map, lane)
    lane_pixel = border_pixel(lane_side, lane_place)
    lane_plain = border_pixel(lane >> 5, lane & 31)
    for block in range(8):
        here = row + block * 128
        rows = slice(block * 128, (block + 1) * 128)
        t.put_in[rows, :] = ones_where(here == lane_pixel)
        marks = ones_where(here == lane_plain)
        t.put[rows, 0:128] = marks
        t.put[rows, 128:256] = marks
    for tap in range(3):
        taps = ring_taps(tap)
        t.ring[tap * 128 : (tap + 1) * 128, :] = dot_nt(taps, turn).astype(BF16)
        back = dot_nt(turn, taps).astype(BF16)
        t.ring_back[:, tap * 128 : (tap + 1) * 128] = back
        t.ring_back[:, 384 + tap * 128 : 384 + (tap + 1) * 128] = back


def lay_weights(target, block):
    empty = jnp.zeros((384, 128), BF16)
    target[0, :, 128:256] = empty
    target[3, :, 0:128] = empty
    for row in range(3):
        for col in range(3):
            part = block(row, col)
            target[row, col * 128 : (col + 1) * 128, 0:128] = part
            target[row + 1, col * 128 : (col + 1) * 128, 128:256] = part


def lay_shifted(target, frame, pair, value):
    col = iota((64, 128), 0) & 31
    before = jnp.where(col == 0, 0.0, pltpu.roll(value, 1, 0))
    after = jnp.where(col == 31, 0.0, pltpu.roll(value, 63, 0))
    for tap, part in enumerate((before, value, after)):
        target[frame, pl.ds(1 + 2 * pair, 2), :, tap * 128 : (tap + 1) * 128] = part.astype(
            BF16
        ).reshape(2, 32, 128)


def lay_rows(target, frame, pair, value):
    part = value.reshape(2, 32, 128)
    for tap in range(3):
        target[frame, pl.ds(2 * pair + tap, 2), :, tap * 128 : (tap + 1) * 128] = part


def clear_rims(shifted):
    for frame in range(2):
        shifted[frame, 0] = jnp.zeros((32, 384), BF16)
        shifted[frame, 33] = jnp.zeros((32, 384), BF16)
        shifted[frame, 34] = jnp.zeros((32, 384), BF16)


def tile_conv(shifted, weights, result):
    for frame in range(2):
        total = None
        for row in range(4):
            rows = shifted[frame, row : row + 32].reshape(16, 2, 32, 384)[:, 0].reshape(512, 384)
            part = dot(rows, weights[row])
            total = part if total is None else total + part
        pairs = slice(frame * 16, (frame + 1) * 16)
        result[pairs, 0:32, :] = total[:, 0:128].reshape(16, 32, 128)
        result[pairs, 32:64, :] = total[:, 128:256].reshape(16, 32, 128)


def transpose_shifted(shifted, target):
    for frame in range(2):
        for tap in range(3):
            lanes = slice(tap * 128, (tap + 1) * 128)
            target[lanes, frame * 1024 : (frame + 1) * 1024] = (
                shifted[frame, 1:33, :, lanes].reshape(1024, 128).T
            )


def picked(table, image):
    parts = [
        dot(table[...], image[frame * 16 : (frame + 1) * 16].reshape(1024, 128))
        for frame in range(2)
    ]
    return jnp.concatenate(parts, axis=1).astype(BF16)


def halo_share(t, arrived, weights, ring_rows, share):
    around = dot(t.ring[...], arrived[...].reshape(128, 256)).astype(BF16)
    parts = []
    for side in range(4):
        for frame in range(2):
            lanes = slice(frame * 128, (frame + 1) * 128)
            ring_rows[side, frame * 32 : (frame + 1) * 32, :] = jnp.concatenate(
                [
                    around[tap * 128 + side * 32 : tap * 128 + (side + 1) * 32, lanes]
                    for tap in range(3)
                ],
                axis=1,
            )
        taps = jnp.concatenate([weights[side_tap(side, tap)] for tap in range(3)], axis=0)
        value = dot(ring_rows[side], taps)
        parts.append(jnp.concatenate([value[0:32], value[32:64]], axis=1))
    both = split_float(jnp.concatenate(parts, axis=0))
    share[...] = dot(t.put[...], both).reshape(16, 64, 256)


def ring_gradient(t, image, weights, border_rows, leaving):
    border = picked(t.border, image)
    rows = [[None] * 4 for tap in range(3)]
    for side in range(4):
        here = border[side * 32 : (side + 1) * 32]
        border_rows[side] = jnp.concatenate([here[:, 0:128], here[:, 128:256]], axis=0)
        for tap in range(3):
            value = dot_nt(border_rows[side], weights[side_tap(side, tap)])
            rows[tap][side] = jnp.concatenate([value[0:32], value[32:64]], axis=1)
    stacked = jnp.concatenate([rows[tap][side] for tap in range(3) for side in range(4)], axis=0)
    leaving[...] = dot(t.ring_back[...], split_float(stacked)).astype(BF16).reshape(4, 32, 256)


def kernel_gradient(turned, spread_rows, ring_rows, border_rows, bias, block, own):
    total = None
    for frame in range(2):
        part = dot(
            turned[:, frame * 1024 : (frame + 1) * 1024],
            spread_rows[frame, 1:33].reshape(1024, 384),
        )
        total = part if total is None else total + part
    block[...] = total
    for side in range(4):
        part = dot_tn(ring_rows[side], border_rows[side])
        for tap in range(3):
            row, col = side_tap(side, tap)
            at = (slice(col * 128, (col + 1) * 128), slice(row * 128, (row + 1) * 128))
            block[at] += part[tap * 128 : (tap + 1) * 128]
    for row in range(3):
        for col in range(3):
            first = (row * 3 + col) * 16
            own[first : first + 16] = block[
                col * 128 : (col + 1) * 128, row * 128 : (row + 1) * 128
            ].reshape(16, 8, 128)
    own[144] = jnp.concatenate([bias, jnp.zeros((7, 128), F32)], axis=0)
    own[145:160] = jnp.zeros((15, 8, 128), F32)


def halo_partners():
    tile, member, core, spot, floor = coordinates()
    count = 2 * PLANE * (DEPTH // 2)
    steps = (count - ROW_TILES, 1, ROW_TILES, count - 1)
    return [(lax.rem(tile + step, count), member) for step in steps]


class Halo:
    def __init__(self, leaving, arrived, send_sem, recv_sem):
        self.leaving, self.arrived = leaving, arrived
        self.send_sem, self.recv_sem = send_sem, recv_sem
        self.partners = halo_partners()

    def copies(self, turn):
        return [
            remote(
                self.leaving.at[turn, way],
                self.arrived.at[turn, (way + 2) % 4],
                self.send_sem.at[turn, way],
                self.recv_sem.at[turn, (way + 2) % 4],
                self.partners[way],
            )
            for way in range(4)
        ]

    def start(self, turn):
        for copy in self.copies(turn):
            copy.start()

    def wait(self, turn):
        for copy in self.copies(turn):
            copy.wait_recv()

    def drain(self):
        for turn in range(4):
            for copy in self.copies(turn):
                copy.wait_send()


TABLES = {
    "pick": (128, 1024),
    "border": (128, 1024),
    "put_in": (1024, 128),
    "put": (1024, 256),
    "ring": (384, 128),
    "ring_back": (128, 768),
}
IMAGE = (32, 64, 128)
SHIFTED = (2, 36, 32, 384)
BUFFERS = {
    "source": (IMAGE, BF16),
    "upstream": (IMAGE, BF16),
    "first": ((3, 3, 128, 128), BF16),
    "second": ((3, 3, 128, 128), BF16),
    "first_fwd": ((4, 384, 256), BF16),
    "first_back": ((4, 384, 256), BF16),
    "second_fwd": ((4, 384, 256), BF16),
    "second_back": ((4, 384, 256), BF16),
    "shift_one": (SHIFTED, BF16),
    "shift_two": (SHIFTED, BF16),
    "shift_grad": (SHIFTED, BF16),
    "row_grad": ((2, 34, 32, 384), BF16),
    "turned_one": ((384, 2048), BF16),
    "turned_two": ((384, 2048), BF16),
    "hidden": (IMAGE, F32),
    "share": ((16, 64, 256), F32),
    "slope": (IMAGE, F32),
    "act": (IMAGE, BF16),
    "grad": (IMAGE, BF16),
    "ring_one": ((4, 64, 384), BF16),
    "ring_two": ((4, 64, 384), BF16),
    "border_grad": ((4, 64, 128), BF16),
    "block": ((384, 384), F32),
    "leaving": ((4, 4, 32, 256), BF16),
    "arrived": ((4, 4, 32, 256), BF16),
}


class Names:
    def __init__(self, names, refs):
        for name, ref in zip(names, refs):
            setattr(self, name, ref)


def step_scratch():
    dma = pltpu.SemaphoreType.DMA
    return (
        [pltpu.VMEM(shape, BF16) for shape in TABLES.values()]
        + [pltpu.VMEM(shape, kind) for shape, kind in BUFFERS.values()]
        + [dma((4, 4)), dma((4, 4)), dma((4,))]
        + sum_scratch()
        + sum_scratch()
    )


def gelu_parts(hidden):
    bell = 0.5 * (1.0 + lax.erf(hidden * ROOT_HALF))
    return hidden * bell, bell + hidden * jnp.exp(-0.5 * hidden * hidden) * INV_ROOT_TAU


def each_pair(body, start=0):
    def step(pair, carry):
        for frame in range(2):
            carry = body(frame, pair, frame * 16 + pair, slice(frame * 128, (frame + 1) * 128), carry)
        return carry

    return lax.fori_loop(0, 16, step, start)


def fold_rows(value):
    return jnp.sum(value.reshape(8, 8, 128), axis=0)


def step_kernel(edge_map, fields, cotangent, w_first, b_first, w_second, b_second,
                response_out, field_grad_out, sum_one_out, sum_two_out, *scratch):
    tables, scratch = Names(TABLES, scratch), scratch[len(TABLES) :]
    v, scratch = Names(BUFFERS, scratch), scratch[len(BUFFERS) :]
    halo = Halo(v.leaving, v.arrived, scratch[0], scratch[1])
    local_sem, scratch = scratch[2], scratch[3:]
    count = len(sum_scratch())
    sum_one, sum_two = GradientSum(scratch[:count]), GradientSum(scratch[count:])

    loads = [
        pltpu.make_async_copy(source, target, local_sem.at[index])
        for index, (source, target) in enumerate(
            ((fields, v.source), (w_first, v.first), (w_second, v.second), (cotangent, v.upstream))
        )
    ]
    for load in loads:
        load.start()
    mate, plane, column = sum_partners()
    partners = [*halo_partners(), mate, *plane, *column]
    barrier = pltpu.get_barrier_semaphore()
    for device in partners:
        pl.semaphore_signal(
            barrier, inc=1, device_id=device, device_id_type=pl.DeviceIdType.MESH
        )
    make_tables(edge_map, tables)
    loads[0].wait()
    v.leaving[0] = picked(tables.pick, v.source).reshape(4, 32, 256)
    pl.semaphore_wait(barrier, len(partners))
    halo.start(0)

    for shifted in (v.shift_one, v.shift_two, v.shift_grad):
        clear_rims(shifted)
    for frame in range(2):
        v.row_grad[frame, 32:34, :, 0:128] = jnp.zeros((2, 32, 128), BF16)
        v.row_grad[frame, 0:2, :, 256:384] = jnp.zeros((2, 32, 128), BF16)

    def shift_source(frame, pair, index, lanes, carry):
        lay_shifted(v.shift_one, frame, pair, v.source[index].astype(F32))
        return carry

    each_pair(shift_source)
    loads[1].wait()
    lay_weights(v.first_fwd, lambda row, col: v.first[row, col])
    tile_conv(v.shift_one, v.first_fwd, v.hidden)
    loads[2].wait()
    lay_weights(v.second_fwd, lambda row, col: v.second[row, col])
    halo.wait(0)
    halo_share(tables, v.arrived.at[0], v.first, v.ring_one, v.share)

    def activate(frame, pair, index, lanes, carry):
        hidden = v.hidden[index] + v.share[pair, :, lanes] + b_first[...]
        value, slope = gelu_parts(hidden)
        v.slope[index] = slope
        v.act[index] = value.astype(BF16)
        lay_shifted(v.shift_two, frame, pair, value)
        return carry

    each_pair(activate)
    v.leaving[1] = picked(tables.pick, v.act).reshape(4, 32, 256)
    halo.start(1)
    tile_conv(v.shift_two, v.second_fwd, v.hidden)
    lay_weights(v.second_back, lambda row, col: v.second[2 - row, 2 - col].T)
    lay_weights(v.first_back, lambda row, col: v.first[2 - row, 2 - col].T)
    loads[3].wait()
    halo.wait(1)
    halo_share(tables, v.arrived.at[1], v.second, v.ring_two, v.share)

    def respond(frame, pair, index, lanes, carry):
        hidden = v.hidden[index] + v.share[pair, :, lanes] + b_second[...]
        value, slope = gelu_parts(hidden)
        response_out[index] = value.astype(BF16)
        grad = (v.upstream[index].astype(F32) * slope).astype(BF16)
        v.grad[index] = grad
        wide = grad.astype(F32)
        lay_shifted(v.shift_grad, frame, pair, wide)
        lay_rows(v.row_grad, frame, pair, grad)
        return carry + fold_rows(wide)

    bias = each_pair(respond, jnp.zeros((8, 128), F32))
    bias = jnp.sum(bias, axis=0, keepdims=True)
    ring_gradient(tables, v.grad, v.second, v.border_grad, v.leaving.at[2])
    halo.start(2)
    transpose_shifted(v.shift_two, v.turned_two)
    kernel_gradient(
        v.turned_two, v.row_grad, v.ring_two, v.border_grad, bias, v.block, sum_two.own
    )
    sum_two.start()
    tile_conv(v.shift_grad, v.second_back, v.hidden)
    transpose_shifted(v.shift_one, v.turned_one)
    sum_two.spread_plane()
    halo.wait(2)
    v.share[...] = dot(tables.put_in[...], v.arrived[2].reshape(128, 256)).reshape(16, 64, 256)

    def descend(frame, pair, index, lanes, carry):
        grad = ((v.hidden[index] + v.share[pair, :, lanes]) * v.slope[index]).astype(BF16)
        v.grad[index] = grad
        wide = grad.astype(F32)
        lay_shifted(v.shift_grad, frame, pair, wide)
        lay_rows(v.row_grad, frame, pair, grad)
        return carry + fold_rows(wide)

    bias = each_pair(descend, jnp.zeros((8, 128), F32))
    bias = jnp.sum(bias, axis=0, keepdims=True)
    ring_gradient(tables, v.grad, v.first, v.border_grad, v.leaving.at[3])
    halo.start(3)
    kernel_gradient(
        v.turned_one, v.row_grad, v.ring_one, v.border_grad, bias, v.block, sum_one.own
    )
    sum_one.start()
    sum_two.spread_column()
    sum_one.spread_plane()
    tile_conv(v.shift_grad, v.first_back, v.hidden)
    sum_two.gather_plane()
    sum_one.spread_column()
    halo.wait(3)
    v.share[...] = dot(tables.put_in[...], v.arrived[3].reshape(128, 256)).reshape(16, 64, 256)

    def finish(frame, pair, index, lanes, carry):
        field_grad_out[index] = (v.hidden[index] + v.share[pair, :, lanes]).astype(BF16)
        return carry

    each_pair(finish)
    sum_two.forward()
    sum_one.gather_plane()
    sum_one.forward()
    for one, out in ((sum_two, sum_two_out), (sum_one, sum_one_out)):
        one.finish()
        out[...] = one.gathered[...].reshape(2 * HALF, 8, 128)
    halo.drain()
    sum_one.drain()
    sum_two.drain()


def store_kernel(scale, response, field_grad, sum_one, sum_two, response_out, field_grad_out,
                 kernel_one_out, bias_one_out, kernel_two_out, bias_two_out, kernel_one,
                 bias_one, kernel_two, bias_two, sems):
    stores = [
        pltpu.make_async_copy(response, response_out, sems.at[0]),
        pltpu.make_async_copy(field_grad, field_grad_out, sems.at[1]),
    ]
    for store in stores:
        store.start()
    for total, kernel, bias, kernel_out, bias_out in (
        (sum_one, kernel_one, bias_one, kernel_one_out, bias_one_out),
        (sum_two, kernel_two, bias_two, kernel_two_out, bias_two_out),
    ):
        kernel[...] = total[0:144].astype(F32) * scale
        bias[...] = total[144].astype(F32)[0:1] * scale
        for source, target in ((kernel, kernel_out), (bias, bias_out)):
            stores.append(pltpu.make_async_copy(source, target, sems.at[len(stores)]))
            stores[-1].start()
    for store in stores:
        store.wait()


def per_device(fields, cotangent, edge_map, w_first, b_first, w_second, b_second):
    frames, tile_side, channels = (fields.shape[2], fields.shape[3], fields.shape[5])
    samples = lax.axis_size("tile") * lax.axis_size("member") * frames * tile_side * tile_side
    kernel = jax.ShapeDtypeStruct((9 * channels // 8, 8, channels), F32)
    bias = jax.ShapeDtypeStruct((1, channels), F32)
    image = jax.ShapeDtypeStruct(IMAGE, BF16)
    local = pl.BlockSpec(memory_space=pltpu.VMEM)
    far = pl.BlockSpec(memory_space=pltpu.HBM)
    near = pltpu.VMEM(IMAGE, BF16)
    sums = pltpu.VMEM((2 * HALF, 8, 128), BF16)
    results = pl.pallas_call(
        step_kernel,
        out_shape=[near, near, sums, sums],
        in_specs=[
            pl.BlockSpec(memory_space=pltpu.SMEM),
            far,
            far,
            far,
            local,
            far,
            local,
        ],
        out_specs=[local] * 4,
        scratch_shapes=step_scratch(),
        compiler_params=pltpu.CompilerParams(
            collective_id=0, has_side_effects=True, vmem_limit_bytes=63_600 << 10
        ),
    )(
        edge_map.reshape(4, 2).T,
        fields.reshape(IMAGE),
        cotangent.reshape(IMAGE),
        w_first,
        b_first.reshape(1, channels),
        w_second,
        b_second.reshape(1, channels),
    )
    outs = pl.pallas_call(
        functools.partial(store_kernel, float(samples) ** -0.5),
        out_shape=[image, image, kernel, bias, kernel, bias],
        in_specs=[local] * 4,
        out_specs=[far] * 6,
        scratch_shapes=[
            pltpu.VMEM(kernel.shape, F32),
            pltpu.VMEM(bias.shape, F32),
            pltpu.VMEM(kernel.shape, F32),
            pltpu.VMEM(bias.shape, F32),
            pltpu.SemaphoreType.DMA((6,)),
        ],
        compiler_params=pltpu.CompilerParams(vmem_limit_bytes=8 << 20),
    )(*results)
    return (
        outs[0].reshape(fields.shape),
        outs[1].reshape(fields.shape),
        outs[2].reshape(w_first.shape),
        outs[3].reshape(b_first.shape),
        outs[4].reshape(w_second.shape),
        outs[5].reshape(b_second.shape),
    )


def solution(mesh):
    in_specs = (
        P("member", "tile", None, None, None, None),
        P("member", "tile", None, None, None, None),
        P("tile", None, None),
        P(),
        P(),
        P(),
        P(),
    )
    out_specs = (
        P("member", "tile", None, None, None, None),
        P("member", "tile", None, None, None, None),
        P(),
        P(),
        P(),
        P(),
    )
    return jax.shard_map(
        per_device, mesh=mesh, in_specs=in_specs, out_specs=out_specs, check_vma=False
    )
```

```python
import functools

import jax
import jax.numpy as jnp
from jax import lax
from jax.experimental import pallas as pl
from jax.experimental.pallas import tpu as pltpu
from jax.sharding import PartitionSpec as P

ROW_TILES = 8
ROOT_HALF = 0.7071067811865476
INV_ROOT_TAU = 0.3989422804014327
BF16 = jnp.bfloat16
F32 = jnp.float32

PLANE = 16
DEPTH = 8
PIECE = 5
HALF = PLANE * PIECE
PART_ROWS = 2 * HALF * 8


def coordinates():
    tile = lax.axis_index("tile")
    member = lax.axis_index("member")
    core = lax.rem(tile, 2)
    spot = lax.rem(tile // 2, PLANE)
    floor = tile // (2 * PLANE)
    return tile, member, core, spot, floor


def sum_partners():
    tile, member, core, spot, floor = coordinates()
    mate = (tile - core + (1 - core), member)
    plane = [
        ((floor * PLANE + lax.rem(spot + step, PLANE)) * 2 + core, member)
        for step in range(1, PLANE)
    ]
    level = floor * 2 + member
    column = []
    for step in range(1, DEPTH):
        other = lax.rem(level + step, DEPTH)
        column.append((((other // 2) * PLANE + spot) * 2 + core, lax.rem(other, 2)))
    return mate, plane, column


def remote(source, target, send_sem, recv_sem, device):
    return pltpu.make_async_remote_copy(
        src_ref=source,
        dst_ref=target,
        send_sem=send_sem,
        recv_sem=recv_sem,
        device_id=device,
        device_id_type=pl.DeviceIdType.MESH,
    )


def sum_scratch():
    dma = pltpu.SemaphoreType.DMA
    return [
        pltpu.VMEM((2 * HALF, 8, 128), jnp.float32),
        pltpu.VMEM((2 * HALF, 8, 128), jnp.bfloat16),
        pltpu.VMEM((HALF, 8, 128), jnp.bfloat16),
        pltpu.VMEM((PLANE, PIECE, 8, 128), jnp.float32),
        pltpu.VMEM((PLANE, PIECE, 8, 128), jnp.bfloat16),
        pltpu.VMEM((PLANE, PIECE, 8, 128), jnp.bfloat16),
        pltpu.VMEM((DEPTH, PIECE, 8, 128), jnp.bfloat16),
        pltpu.VMEM((2, PLANE, PIECE, 8, 128), jnp.bfloat16),
        dma((2,)),
        dma((2,)),
        dma((2,)),
        dma((2,)),
        dma((2,)),
    ]


class GradientSum:
    def __init__(self, refs):
        (
            self.own,
            self.halves,
            self.from_mate,
            self.total,
            self.pieces,
            self.from_plane,
            self.from_column,
            self.gathered,
            self.mate_sem,
            self.plane_sem,
            self.column_sem,
            self.gather_sem,
            self.forward_sem,
        ) = refs
        tile, member, core, spot, floor = coordinates()
        self.core, self.spot, self.level = core, spot, floor * 2 + member
        self.mate, self.plane, self.column = sum_partners()

    def to_mate(self):
        return remote(
            self.halves.at[pl.ds((1 - self.core) * HALF, HALF)],
            self.from_mate,
            self.mate_sem.at[0],
            self.mate_sem.at[1],
            self.mate,
        )

    def to_plane(self, step):
        target = lax.rem(self.spot + step, PLANE)
        return remote(
            self.pieces.at[target],
            self.from_plane.at[self.spot],
            self.plane_sem.at[0],
            self.plane_sem.at[1],
            self.plane[step - 1],
        )

    def to_column(self, step):
        return remote(
            self.from_column.at[self.level],
            self.from_column.at[self.level],
            self.column_sem.at[0],
            self.column_sem.at[1],
            self.column[step - 1],
        )

    def to_gather(self, step):
        return remote(
            self.gathered.at[self.core, self.spot],
            self.gathered.at[self.core, self.spot],
            self.gather_sem.at[0],
            self.gather_sem.at[1],
            self.plane[step - 1],
        )

    def to_forward(self):
        return remote(
            self.gathered.at[self.core],
            self.gathered.at[self.core],
            self.forward_sem.at[0],
            self.forward_sem.at[1],
            self.mate,
        )

    def wait_all(self, buffer, count, sem):
        pltpu.make_async_copy(
            buffer.at[pl.ds(0, count)], buffer.at[pl.ds(0, count)], sem
        ).wait()

    def start(self):
        self.halves[...] = self.own[...].astype(jnp.bfloat16)
        self.to_mate().start()

    def spread_plane(self):
        self.to_mate().wait_recv()
        total = self.own[pl.ds(self.core * HALF, HALF)] + self.from_mate[...].astype(jnp.float32)
        total = total.reshape(PLANE, PIECE, 8, 128)
        self.total[...] = total
        self.pieces[...] = total.astype(jnp.bfloat16)
        for step in range(1, PLANE):
            self.to_plane(step).start()

    def spread_column(self):
        value = self.total[self.spot]
        self.wait_all(self.from_plane, PLANE - 1, self.plane_sem.at[1])
        for step in range(1, PLANE):
            origin = lax.rem(self.spot + PLANE - step, PLANE)
            value = value + self.from_plane[origin].astype(jnp.float32)
        self.from_column[self.level] = value.astype(jnp.bfloat16)
        for step in range(1, DEPTH):
            self.to_column(step).start()

    def gather_plane(self):
        self.wait_all(self.from_column, DEPTH - 1, self.column_sem.at[1])
        value = jnp.zeros((PIECE, 8, 128), jnp.float32)
        for level in range(DEPTH):
            value = value + self.from_column[level].astype(jnp.float32)
        self.gathered[self.core, self.spot] = value.astype(jnp.bfloat16)
        for step in range(1, PLANE):
            self.to_gather(step).start()

    def forward(self):
        self.wait_all(self.gathered.at[self.core], PLANE - 1, self.gather_sem.at[1])
        self.to_forward().start()

    def finish(self):
        self.to_forward().wait_recv()

    def drain(self):
        self.to_mate().wait_send()
        self.wait_all(self.pieces, PLANE - 1, self.plane_sem.at[0])
        self.wait_all(self.from_column, DEPTH - 1, self.column_sem.at[0])
        self.wait_all(self.gathered.at[self.core], PLANE - 1, self.gather_sem.at[0])
        self.to_forward().wait_send()


def dot(left, right):
    return jnp.dot(left, right, preferred_element_type=F32)


def dot_nt(left, right):
    return lax.dot_general(left, right, (((1,), (1,)), ((), ())), preferred_element_type=F32)


def dot_tn(left, right):
    return lax.dot_general(left, right, (((0,), (0,)), ((), ())), preferred_element_type=F32)


def iota(shape, axis):
    return lax.broadcasted_iota(jnp.int32, shape, axis)


def ones_where(mask):
    return jnp.where(mask, 1.0, 0.0).astype(BF16)


def border_pixel(side, place):
    return jnp.where(
        side == 0,
        place,
        jnp.where(side == 1, place * 32 + 31, jnp.where(side == 2, place + 992, place * 32)),
    )


def facing(edge_map, index):
    direction, place = index >> 5, index & 31
    side = jnp.zeros_like(index)
    flip = jnp.zeros_like(index)
    for candidate in range(4):
        side = jnp.where(direction == candidate, edge_map[0, candidate], side)
        flip = jnp.where(direction == candidate, edge_map[1, candidate], flip)
    return side, jnp.where(flip == 1, 31 - place, place)


def ring_taps(tap):
    row, lane = iota((128, 128), 0), iota((128, 128), 1)
    side, place = row >> 5, row & 31
    halo_side, halo_place = lane >> 5, lane & 31
    wanted = place + (tap - 1)
    whole = (halo_side == side) & (halo_place == wanted)
    along = (side == 0) | (side == 2)
    end = jnp.where(side == 0, 0, 31)
    low = ((halo_side == side) & (halo_place == 0)) | ((halo_side == 3) & (halo_place == end))
    high = ((halo_side == side) & (halo_place == 31)) | ((halo_side == 1) & (halo_place == end))
    half = along & (((wanted == -1) & low) | ((wanted == 32) & high))
    return jnp.where(whole, 1.0, jnp.where(half, 0.5, 0.0)).astype(BF16)


def side_tap(side, tap):
    return ((0, tap), (tap, 2), (2, tap), (tap, 0))[side]


def split_float(value):
    high = value.astype(BF16)
    low = (value - high.astype(F32)).astype(BF16)
    return jnp.concatenate([high, low], axis=0)


def make_tables(edge_map, t):
    row, lane = iota((128, 128), 0), iota((128, 128), 1)
    side, place = facing(edge_map, row)
    pixel = border_pixel(side, place)
    plain = border_pixel(row >> 5, row & 31)
    turn = ones_where(lane == side * 32 + place)
    t.turn[...] = turn
    for block in range(8):
        here = lane + block * 128
        t.pick[:, block * 128 : (block + 1) * 128] = ones_where(here == pixel)
        t.border[:, block * 128 : (block + 1) * 128] = ones_where(here == plain)
    lane_side, lane_place = facing(edge_map, lane)
    lane_pixel = border_pixel(lane_side, lane_place)
    lane_plain = border_pixel(lane >> 5, lane & 31)
    for block in range(8):
        here = row + block * 128
        rows = slice(block * 128, (block + 1) * 128)
        t.put_in[rows, :] = ones_where(here == lane_pixel)
        marks = ones_where(here == lane_plain)
        t.put[rows, 0:128] = marks
        t.put[rows, 128:256] = marks
    cross = dot_nt(t.border[...], t.border[...]).astype(BF16)
    t.cross[:, 0:128] = cross
    t.cross[:, 128:256] = cross
    t.cross_in[...] = dot_nt(t.border[...], t.pick[...]).astype(BF16)
    for tap in range(3):
        taps = ring_taps(tap)
        t.ring[tap * 128 : (tap + 1) * 128, :] = dot_nt(taps, turn).astype(BF16)
        back = dot_nt(turn, taps).astype(BF16)
        t.ring_back[:, tap * 128 : (tap + 1) * 128] = back
        t.ring_back[:, 384 + tap * 128 : 384 + (tap + 1) * 128] = back


def lay_weights(target, block):
    empty = jnp.zeros((384, 128), BF16)
    target[0, :, 128:256] = empty
    target[3, :, 0:128] = empty
    for row in range(3):
        for col in range(3):
            part = block(row, col)
            target[row, col * 128 : (col + 1) * 128, 0:128] = part
            target[row + 1, col * 128 : (col + 1) * 128, 128:256] = part


def lay_shifted(target, frame, pair, value):
    col = iota((64, 128), 0) & 31
    before = jnp.where(col == 0, 0.0, pltpu.roll(value, 1, 0))
    after = jnp.where(col == 31, 0.0, pltpu.roll(value, 63, 0))
    for tap, part in enumerate((before, value, after)):
        target[frame, pl.ds(1 + 2 * pair, 2), :, tap * 128 : (tap + 1) * 128] = part.astype(
            BF16
        ).reshape(2, 32, 128)


def lay_rows(target, frame, pair, value):
    part = value.reshape(2, 32, 128)
    for tap in range(3):
        target[frame, pl.ds(2 * pair + tap, 2), :, tap * 128 : (tap + 1) * 128] = part


def clear_rims(shifted):
    for frame in range(2):
        shifted[frame, 0] = jnp.zeros((32, 384), BF16)
        shifted[frame, 33] = jnp.zeros((32, 384), BF16)
        shifted[frame, 34] = jnp.zeros((32, 384), BF16)


def tile_conv(shifted, weights, result):
    for frame in range(2):
        total = None
        for row in range(4):
            rows = shifted[frame, row : row + 32].reshape(16, 2, 32, 384)[:, 0].reshape(512, 384)
            part = dot(rows, weights[row])
            total = part if total is None else total + part
        for pair in range(16):
            first = frame * 1024 + pair * 64
            rows = slice(pair * 32, (pair + 1) * 32)
            result[first : first + 32, :] = total[rows, 0:128]
            result[first + 32 : first + 64, :] = total[rows, 128:256]


def transpose_shifted(shifted, target):
    for frame in range(2):
        for tap in range(3):
            lanes = slice(tap * 128, (tap + 1) * 128)
            target[lanes, frame * 1024 : (frame + 1) * 1024] = (
                shifted[frame, 1:33, :, lanes].reshape(1024, 128).T
            )


def picked(table, image):
    parts = [
        dot(table[...], image[frame * 16 : (frame + 1) * 16].reshape(1024, 128))
        for frame in range(2)
    ]
    return jnp.concatenate(parts, axis=1).astype(BF16)


def halo_share(t, arrived, weights, ring_rows):
    around = dot(t.ring[...], arrived[...].reshape(128, 256)).astype(BF16)
    parts = []
    for side in range(4):
        for frame in range(2):
            lanes = slice(frame * 128, (frame + 1) * 128)
            ring_rows[side, frame * 32 : (frame + 1) * 32, :] = jnp.concatenate(
                [
                    around[tap * 128 + side * 32 : tap * 128 + (side + 1) * 32, lanes]
                    for tap in range(3)
                ],
                axis=1,
            )
        taps = jnp.concatenate([weights[side_tap(side, tap)] for tap in range(3)], axis=0)
        value = dot(ring_rows[side], taps)
        parts.append(jnp.concatenate([value[0:32], value[32:64]], axis=1))
    return split_float(jnp.concatenate(parts, axis=0))


def lay_border(border, border_rows):
    for side in range(4):
        here = border[side * 32 : (side + 1) * 32]
        border_rows[side] = jnp.concatenate([here[:, 0:128], here[:, 128:256]], axis=0)


def ring_gradient(t, weights, border_rows, leaving):
    rows = [[None] * 4 for tap in range(3)]
    for side in range(4):
        for tap in range(3):
            value = dot_nt(border_rows[side], weights[side_tap(side, tap)])
            rows[tap][side] = jnp.concatenate([value[0:32], value[32:64]], axis=1)
    stacked = jnp.concatenate([rows[tap][side] for tap in range(3) for side in range(4)], axis=0)
    leaving[...] = dot(t.ring_back[...], split_float(stacked)).astype(BF16).reshape(4, 32, 256)


def kernel_gradient(turned, spread_rows, ring_rows, border_rows, bias, block, own):
    total = None
    for frame in range(2):
        part = dot(
            turned[:, frame * 1024 : (frame + 1) * 1024],
            spread_rows[frame, 1:33].reshape(1024, 384),
        )
        total = part if total is None else total + part
    block[...] = total
    for side in range(4):
        part = dot_tn(ring_rows[side], border_rows[side])
        for tap in range(3):
            row, col = side_tap(side, tap)
            at = (slice(col * 128, (col + 1) * 128), slice(row * 128, (row + 1) * 128))
            block[at] += part[tap * 128 : (tap + 1) * 128]
    for row in range(3):
        for col in range(3):
            first = (row * 3 + col) * 16
            own[first : first + 16] = block[
                col * 128 : (col + 1) * 128, row * 128 : (row + 1) * 128
            ].reshape(16, 8, 128)
    own[144] = jnp.concatenate([bias, jnp.zeros((7, 128), F32)], axis=0)
    own[145:160] = jnp.zeros((15, 8, 128), F32)


def halo_partners():
    tile, member, core, spot, floor = coordinates()
    count = 2 * PLANE * (DEPTH // 2)
    steps = (count - ROW_TILES, 1, ROW_TILES, count - 1)
    return [(lax.rem(tile + step, count), member) for step in steps]


class Halo:
    def __init__(self, leaving, arrived, send_sem, recv_sem):
        self.leaving, self.arrived = leaving, arrived
        self.send_sem, self.recv_sem = send_sem, recv_sem
        self.partners = halo_partners()

    def copies(self, turn):
        return [
            remote(
                self.leaving.at[turn, way],
                self.arrived.at[turn, (way + 2) % 4],
                self.send_sem.at[turn, way],
                self.recv_sem.at[turn, (way + 2) % 4],
                self.partners[way],
            )
            for way in range(4)
        ]

    def start(self, turn):
        for copy in self.copies(turn):
            copy.start()

    def wait(self, turn):
        for copy in self.copies(turn):
            copy.wait_recv()

    def drain(self):
        for turn in range(4):
            for copy in self.copies(turn):
                copy.wait_send()


TABLES = {
    "pick": (128, 1024),
    "border": (128, 1024),
    "put_in": (1024, 128),
    "put": (1024, 256),
    "turn": (128, 128),
    "cross": (128, 256),
    "cross_in": (128, 128),
    "ring": (384, 128),
    "ring_back": (128, 768),
}
IMAGE = (32, 64, 128)
SHIFTED = (2, 36, 32, 384)
BUFFERS = {
    "source": (IMAGE, BF16),
    "upstream": (IMAGE, BF16),
    "first": ((3, 3, 128, 128), BF16),
    "second": ((3, 3, 128, 128), BF16),
    "first_fwd": ((4, 384, 256), BF16),
    "first_back": ((4, 384, 256), BF16),
    "second_fwd": ((4, 384, 256), BF16),
    "second_back": ((4, 384, 256), BF16),
    "shift_one": (SHIFTED, BF16),
    "shift_two": (SHIFTED, BF16),
    "shift_grad": (SHIFTED, BF16),
    "row_grad": ((2, 34, 32, 384), BF16),
    "turned_one": ((384, 2048), BF16),
    "turned_two": ((384, 2048), BF16),
    "hidden": ((2048, 128), F32),
    "hidden_border": ((128, 256), F32),
    "slope_border": ((128, 256), F32),
    "upstream_border": ((128, 256), BF16),
    "both": ((256, 256), BF16),
    "grad": (IMAGE, BF16),
    "share": ((16, 64, 256), F32),
    "slope": (IMAGE, F32),
    "ring_one": ((4, 64, 384), BF16),
    "ring_two": ((4, 64, 384), BF16),
    "border_grad": ((4, 64, 128), BF16),
    "block": ((384, 384), F32),
    "leaving": ((4, 4, 32, 256), BF16),
    "arrived": ((4, 4, 32, 256), BF16),
}


class Names:
    def __init__(self, names, refs):
        for name, ref in zip(names, refs):
            setattr(self, name, ref)


def step_scratch():
    dma = pltpu.SemaphoreType.DMA
    return (
        [pltpu.VMEM(shape, BF16) for shape in TABLES.values()]
        + [pltpu.VMEM(shape, kind) for shape, kind in BUFFERS.values()]
        + [dma((4, 4)), dma((4, 4)), dma((4,))]
        + sum_scratch()
        + sum_scratch()
    )


def gelu_parts(hidden):
    bell = 0.5 * (1.0 + lax.erf(hidden * ROOT_HALF))
    return hidden * bell, bell + hidden * jnp.exp(-0.5 * hidden * hidden) * INV_ROOT_TAU


def rows_of(index):
    return pl.ds(pl.multiple_of(index * 64, 64), 64)


def twice(bias):
    return jnp.concatenate([bias, bias], axis=1)


def border_of(image):
    frames = []
    for frame in range(2):
        first = frame * 1024
        frames.append(
            jnp.concatenate(
                [
                    image[first : first + 32, :],
                    image[pl.ds(first + 31, 32, stride=32), :],
                    image[first + 992 : first + 1024, :],
                    image[pl.ds(first, 32, stride=32), :],
                ],
                axis=0,
            )
        )
    return jnp.concatenate(frames, axis=1)


def each_pair(body, start=0):
    def step(pair, carry):
        for frame in range(2):
            carry = body(frame, pair, frame * 16 + pair, slice(frame * 128, (frame + 1) * 128), carry)
        return carry

    return lax.fori_loop(0, 16, step, start)


def fold_rows(value):
    return jnp.sum(value.reshape(8, 8, 128), axis=0)


def step_kernel(edge_map, fields, cotangent, w_first, b_first, w_second, b_second,
                response_out, field_grad_out, sum_one_out, sum_two_out, *scratch):
    tables, scratch = Names(TABLES, scratch), scratch[len(TABLES) :]
    v, scratch = Names(BUFFERS, scratch), scratch[len(BUFFERS) :]
    halo = Halo(v.leaving, v.arrived, scratch[0], scratch[1])
    local_sem, scratch = scratch[2], scratch[3:]
    count = len(sum_scratch())
    sum_one, sum_two = GradientSum(scratch[:count]), GradientSum(scratch[count:])

    mate, plane, column = sum_partners()
    partners = [*halo_partners(), mate, *plane, *column]
    barrier = pltpu.get_barrier_semaphore()
    for device in partners:
        pl.semaphore_signal(
            barrier, inc=1, device_id=device, device_id_type=pl.DeviceIdType.MESH
        )
    loads = [
        pltpu.make_async_copy(source, target, local_sem.at[index])
        for index, (source, target) in enumerate(
            ((fields, v.source), (w_first, v.first), (w_second, v.second), (cotangent, v.upstream))
        )
    ]
    for load in loads:
        load.start()
    make_tables(edge_map, tables)
    loads[0].wait()
    v.leaving[0] = picked(tables.pick, v.source).reshape(4, 32, 256)
    pl.semaphore_wait(barrier, len(partners))
    halo.start(0)

    for shifted in (v.shift_one, v.shift_two, v.shift_grad):
        clear_rims(shifted)
    for frame in range(2):
        v.row_grad[frame, 32:34, :, 0:128] = jnp.zeros((2, 32, 128), BF16)
        v.row_grad[frame, 0:2, :, 256:384] = jnp.zeros((2, 32, 128), BF16)

    def shift_source(frame, pair, index, lanes, carry):
        lay_shifted(v.shift_one, frame, pair, v.source[index].astype(F32))
        return carry

    each_pair(shift_source)
    loads[1].wait()
    lay_weights(v.first_fwd, lambda row, col: v.first[row, col])
    tile_conv(v.shift_one, v.first_fwd, v.hidden)
    v.hidden_border[...] = border_of(v.hidden) + twice(b_first[...])
    loads[2].wait()
    lay_weights(v.second_fwd, lambda row, col: v.second[row, col])
    loads[3].wait()
    v.upstream_border[...] = picked(tables.border, v.upstream)
    transpose_shifted(v.shift_one, v.turned_one)
    lay_weights(v.second_back, lambda row, col: v.second[2 - row, 2 - col].T)
    lay_weights(v.first_back, lambda row, col: v.first[2 - row, 2 - col].T)

    halo.wait(0)
    both = halo_share(tables, v.arrived.at[0], v.first, v.ring_one)
    v.both[...] = both
    value, slope = gelu_parts(v.hidden_border[...] + dot(tables.cross[...], both))
    v.leaving[1] = dot(tables.turn[...], value.astype(BF16)).astype(BF16).reshape(4, 32, 256)
    v.slope_border[...] = slope
    halo.start(1)
    v.share[...] = dot(tables.put[...], v.both[...]).reshape(16, 64, 256)

    def activate(frame, pair, index, lanes, carry):
        hidden = v.hidden[rows_of(index)] + v.share[pair, :, lanes] + b_first[...]
        value, slope = gelu_parts(hidden)
        v.slope[index] = slope
        lay_shifted(v.shift_two, frame, pair, value)
        return carry

    each_pair(activate)
    tile_conv(v.shift_two, v.second_fwd, v.hidden)
    v.hidden_border[...] = border_of(v.hidden) + twice(b_second[...])
    transpose_shifted(v.shift_two, v.turned_two)

    halo.wait(1)
    both = halo_share(tables, v.arrived.at[1], v.second, v.ring_two)
    v.both[...] = both
    value, slope = gelu_parts(v.hidden_border[...] + dot(tables.cross[...], both))
    border = (v.upstream_border[...].astype(F32) * slope).astype(BF16)
    lay_border(border, v.border_grad)
    ring_gradient(tables, v.second, v.border_grad, v.leaving.at[2])
    halo.start(2)
    v.share[...] = dot(tables.put[...], v.both[...]).reshape(16, 64, 256)

    def respond(frame, pair, index, lanes, carry):
        hidden = v.hidden[rows_of(index)] + v.share[pair, :, lanes] + b_second[...]
        value, slope = gelu_parts(hidden)
        response_out[index] = value.astype(BF16)
        grad = (v.upstream[index].astype(F32) * slope).astype(BF16)
        wide = grad.astype(F32)
        lay_shifted(v.shift_grad, frame, pair, wide)
        lay_rows(v.row_grad, frame, pair, grad)
        return carry + fold_rows(wide)

    bias = each_pair(respond, jnp.zeros((8, 128), F32))
    bias = jnp.sum(bias, axis=0, keepdims=True)
    tile_conv(v.shift_grad, v.second_back, v.hidden)
    v.hidden_border[...] = border_of(v.hidden)
    kernel_gradient(
        v.turned_two, v.row_grad, v.ring_two, v.border_grad, bias, v.block, sum_two.own
    )
    sum_two.start()

    sum_two.spread_plane()

    halo.wait(2)
    came = v.arrived[2].reshape(128, 256)
    border = v.hidden_border[...] + dot(tables.cross_in[...], came)
    border = (border * v.slope_border[...]).astype(BF16)
    lay_border(border, v.border_grad)
    v.share[...] = dot(tables.put_in[...], came).reshape(16, 64, 256)

    def descend(frame, pair, index, lanes, carry):
        grad = v.hidden[rows_of(index)] + v.share[pair, :, lanes]
        grad = (grad * v.slope[index]).astype(BF16)
        v.grad[index] = grad
        lay_rows(v.row_grad, frame, pair, grad)
        return carry + fold_rows(grad.astype(F32))

    bias = each_pair(descend, jnp.zeros((8, 128), F32))
    bias = jnp.sum(bias, axis=0, keepdims=True)
    kernel_gradient(
        v.turned_one, v.row_grad, v.ring_one, v.border_grad, bias, v.block, sum_one.own
    )
    sum_one.start()
    ring_gradient(tables, v.first, v.border_grad, v.leaving.at[3])
    halo.start(3)

    def shift_grad(frame, pair, index, lanes, carry):
        lay_shifted(v.shift_grad, frame, pair, v.grad[index].astype(F32))
        return carry

    sum_one.spread_plane()
    each_pair(shift_grad)
    sum_two.spread_column()
    tile_conv(v.shift_grad, v.first_back, v.hidden)
    halo.wait(3)
    v.share[...] = dot(tables.put_in[...], v.arrived[3].reshape(128, 256)).reshape(16, 64, 256)
    sum_one.spread_column()

    def finish(frame, pair, index, lanes, carry):
        field_grad_out[index] = (v.hidden[rows_of(index)] + v.share[pair, :, lanes]).astype(BF16)
        return carry

    each_pair(finish)
    sum_two.gather_plane()
    sum_one.gather_plane()
    halo.drain()
    sum_two.forward()
    sum_two.finish()
    sum_two_out[...] = sum_two.gathered[...].reshape(2 * HALF, 8, 128)
    sum_two.drain()
    sum_one.forward()
    sum_one.finish()
    sum_one_out[...] = sum_one.gathered[...].reshape(2 * HALF, 8, 128)
    sum_one.drain()


def store_kernel(scale, response, field_grad, sum_one, sum_two, response_out, field_grad_out,
                 kernel_one_out, bias_one_out, kernel_two_out, bias_two_out, kernel_one,
                 bias_one, kernel_two, bias_two, sems):
    stores = [
        pltpu.make_async_copy(response, response_out, sems.at[0]),
        pltpu.make_async_copy(field_grad, field_grad_out, sems.at[1]),
    ]
    for store in stores:
        store.start()
    for total, kernel, bias, kernel_out, bias_out in (
        (sum_one, kernel_one, bias_one, kernel_one_out, bias_one_out),
        (sum_two, kernel_two, bias_two, kernel_two_out, bias_two_out),
    ):
        kernel[...] = total[0:144].astype(F32) * scale
        bias[...] = total[144].astype(F32)[0:1] * scale
        for source, target in ((kernel, kernel_out), (bias, bias_out)):
            stores.append(pltpu.make_async_copy(source, target, sems.at[len(stores)]))
            stores[-1].start()
    for store in stores:
        store.wait()


def per_device(fields, cotangent, edge_map, w_first, b_first, w_second, b_second):
    frames, tile_side, channels = (fields.shape[2], fields.shape[3], fields.shape[5])
    samples = lax.axis_size("tile") * lax.axis_size("member") * frames * tile_side * tile_side
    kernel = jax.ShapeDtypeStruct((9 * channels // 8, 8, channels), F32)
    bias = jax.ShapeDtypeStruct((1, channels), F32)
    image = jax.ShapeDtypeStruct(IMAGE, BF16)
    local = pl.BlockSpec(memory_space=pltpu.VMEM)
    far = pl.BlockSpec(memory_space=pltpu.HBM)
    near = pltpu.VMEM(IMAGE, BF16)
    sums = pltpu.VMEM((2 * HALF, 8, 128), BF16)
    results = pl.pallas_call(
        step_kernel,
        out_shape=[near, near, sums, sums],
        in_specs=[
            pl.BlockSpec(memory_space=pltpu.SMEM),
            far,
            far,
            far,
            local,
            far,
            local,
        ],
        out_specs=[local] * 4,
        scratch_shapes=step_scratch(),
        compiler_params=pltpu.CompilerParams(
            collective_id=0, has_side_effects=True, vmem_limit_bytes=63_600 << 10
        ),
    )(
        edge_map.reshape(4, 2).T,
        fields.reshape(IMAGE),
        cotangent.reshape(IMAGE),
        w_first,
        b_first.reshape(1, channels),
        w_second,
        b_second.reshape(1, channels),
    )
    outs = pl.pallas_call(
        functools.partial(store_kernel, float(samples) ** -0.5),
        out_shape=[image, image, kernel, bias, kernel, bias],
        in_specs=[local] * 4,
        out_specs=[far] * 6,
        scratch_shapes=[
            pltpu.VMEM(kernel.shape, F32),
            pltpu.VMEM(bias.shape, F32),
            pltpu.VMEM(kernel.shape, F32),
            pltpu.VMEM(bias.shape, F32),
            pltpu.SemaphoreType.DMA((6,)),
        ],
        compiler_params=pltpu.CompilerParams(vmem_limit_bytes=8 << 20),
    )(*results)
    return (
        outs[0].reshape(fields.shape),
        outs[1].reshape(fields.shape),
        outs[2].reshape(w_first.shape),
        outs[3].reshape(b_first.shape),
        outs[4].reshape(w_second.shape),
        outs[5].reshape(b_second.shape),
    )


def solution(mesh):
    in_specs = (
        P("member", "tile", None, None, None, None),
        P("member", "tile", None, None, None, None),
        P("tile", None, None),
        P(),
        P(),
        P(),
        P(),
    )
    out_specs = (
        P("member", "tile", None, None, None, None),
        P("member", "tile", None, None, None, None),
        P(),
        P(),
        P(),
        P(),
    )
    return jax.shard_map(
        per_device, mesh=mesh, in_specs=in_specs, out_specs=out_specs, check_vma=False
    )
```

```python
import functools

import jax
import jax.numpy as jnp
from jax import lax
from jax.experimental import pallas as pl
from jax.experimental.pallas import tpu as pltpu
from jax.sharding import PartitionSpec as P

ROW_TILES = 8
ROOT_HALF = 0.7071067811865476
INV_ROOT_TAU = 0.3989422804014327
BF16 = jnp.bfloat16
F32 = jnp.float32

PLANE = 16
DEPTH = 8
PIECE = 5
HALF = PLANE * PIECE
PART_ROWS = 2 * HALF * 8


def coordinates():
    tile = lax.axis_index("tile")
    member = lax.axis_index("member")
    core = lax.rem(tile, 2)
    spot = lax.rem(tile // 2, PLANE)
    floor = tile // (2 * PLANE)
    return tile, member, core, spot, floor


def sum_partners():
    tile, member, core, spot, floor = coordinates()
    mate = (tile - core + (1 - core), member)
    plane = [
        ((floor * PLANE + lax.rem(spot + step, PLANE)) * 2 + core, member)
        for step in range(1, PLANE)
    ]
    level = floor * 2 + member
    column = []
    for step in range(1, DEPTH):
        other = lax.rem(level + step, DEPTH)
        column.append((((other // 2) * PLANE + spot) * 2 + core, lax.rem(other, 2)))
    return mate, plane, column


def remote(source, target, send_sem, recv_sem, device):
    return pltpu.make_async_remote_copy(
        src_ref=source,
        dst_ref=target,
        send_sem=send_sem,
        recv_sem=recv_sem,
        device_id=device,
        device_id_type=pl.DeviceIdType.MESH,
    )


def sum_scratch():
    dma = pltpu.SemaphoreType.DMA
    return [
        pltpu.VMEM((2 * HALF, 8, 128), jnp.float32),
        pltpu.VMEM((2 * HALF, 8, 128), jnp.bfloat16),
        pltpu.VMEM((HALF, 8, 128), jnp.bfloat16),
        pltpu.VMEM((PLANE, PIECE, 8, 128), jnp.float32),
        pltpu.VMEM((PLANE, PIECE, 8, 128), jnp.bfloat16),
        pltpu.VMEM((PLANE, PIECE, 8, 128), jnp.bfloat16),
        pltpu.VMEM((DEPTH, PIECE, 8, 128), jnp.bfloat16),
        pltpu.VMEM((2, PLANE, PIECE, 8, 128), jnp.bfloat16),
        dma((2,)),
        dma((2,)),
        dma((2,)),
        dma((2,)),
        dma((2,)),
    ]


class GradientSum:
    def __init__(self, refs):
        (
            self.own,
            self.halves,
            self.from_mate,
            self.total,
            self.pieces,
            self.from_plane,
            self.from_column,
            self.gathered,
            self.mate_sem,
            self.plane_sem,
            self.column_sem,
            self.gather_sem,
            self.forward_sem,
        ) = refs
        tile, member, core, spot, floor = coordinates()
        self.core, self.spot, self.level = core, spot, floor * 2 + member
        self.mate, self.plane, self.column = sum_partners()

    def to_mate(self):
        return remote(
            self.halves.at[pl.ds((1 - self.core) * HALF, HALF)],
            self.from_mate,
            self.mate_sem.at[0],
            self.mate_sem.at[1],
            self.mate,
        )

    def to_plane(self, step):
        target = lax.rem(self.spot + step, PLANE)
        return remote(
            self.pieces.at[target],
            self.from_plane.at[self.spot],
            self.plane_sem.at[0],
            self.plane_sem.at[1],
            self.plane[step - 1],
        )

    def to_column(self, step):
        return remote(
            self.from_column.at[self.level],
            self.from_column.at[self.level],
            self.column_sem.at[0],
            self.column_sem.at[1],
            self.column[step - 1],
        )

    def to_gather(self, step):
        return remote(
            self.gathered.at[self.core, self.spot],
            self.gathered.at[self.core, self.spot],
            self.gather_sem.at[0],
            self.gather_sem.at[1],
            self.plane[step - 1],
        )

    def to_forward(self):
        return remote(
            self.gathered.at[self.core],
            self.gathered.at[self.core],
            self.forward_sem.at[0],
            self.forward_sem.at[1],
            self.mate,
        )

    def wait_all(self, buffer, count, sem):
        pltpu.make_async_copy(
            buffer.at[pl.ds(0, count)], buffer.at[pl.ds(0, count)], sem
        ).wait()

    def start(self):
        self.halves[...] = self.own[...].astype(jnp.bfloat16)
        self.to_mate().start()

    def spread_plane(self):
        self.to_mate().wait_recv()
        total = self.own[pl.ds(self.core * HALF, HALF)] + self.from_mate[...].astype(jnp.float32)
        total = total.reshape(PLANE, PIECE, 8, 128)
        self.total[...] = total
        self.pieces[...] = total.astype(jnp.bfloat16)
        for step in range(1, PLANE):
            self.to_plane(step).start()

    def spread_column(self):
        value = self.total[self.spot]
        self.wait_all(self.from_plane, PLANE - 1, self.plane_sem.at[1])
        for step in range(1, PLANE):
            origin = lax.rem(self.spot + PLANE - step, PLANE)
            value = value + self.from_plane[origin].astype(jnp.float32)
        self.from_column[self.level] = value.astype(jnp.bfloat16)
        for step in range(1, DEPTH):
            self.to_column(step).start()

    def gather_plane(self):
        self.wait_all(self.from_column, DEPTH - 1, self.column_sem.at[1])
        value = jnp.zeros((PIECE, 8, 128), jnp.float32)
        for level in range(DEPTH):
            value = value + self.from_column[level].astype(jnp.float32)
        self.gathered[self.core, self.spot] = value.astype(jnp.bfloat16)
        for step in range(1, PLANE):
            self.to_gather(step).start()

    def forward(self):
        self.wait_all(self.gathered.at[self.core], PLANE - 1, self.gather_sem.at[1])
        self.to_forward().start()

    def finish(self):
        self.to_forward().wait_recv()

    def drain(self):
        self.to_mate().wait_send()
        self.wait_all(self.pieces, PLANE - 1, self.plane_sem.at[0])
        self.wait_all(self.from_column, DEPTH - 1, self.column_sem.at[0])
        self.wait_all(self.gathered.at[self.core], PLANE - 1, self.gather_sem.at[0])
        self.to_forward().wait_send()


def dot(left, right):
    return jnp.dot(left, right, preferred_element_type=F32)


def dot_nt(left, right):
    return lax.dot_general(left, right, (((1,), (1,)), ((), ())), preferred_element_type=F32)


def dot_tn(left, right):
    return lax.dot_general(left, right, (((0,), (0,)), ((), ())), preferred_element_type=F32)


def iota(shape, axis):
    return lax.broadcasted_iota(jnp.int32, shape, axis)


def ones_where(mask):
    return jnp.where(mask, 1.0, 0.0).astype(BF16)


def border_pixel(side, place):
    return jnp.where(
        side == 0,
        place,
        jnp.where(side == 1, place * 32 + 31, jnp.where(side == 2, place + 992, place * 32)),
    )


def facing(edge_map, index):
    direction, place = index >> 5, index & 31
    side = jnp.zeros_like(index)
    flip = jnp.zeros_like(index)
    for candidate in range(4):
        side = jnp.where(direction == candidate, edge_map[0, candidate], side)
        flip = jnp.where(direction == candidate, edge_map[1, candidate], flip)
    return side, jnp.where(flip == 1, 31 - place, place)


def ring_taps(tap):
    row, lane = iota((128, 128), 0), iota((128, 128), 1)
    side, place = row >> 5, row & 31
    halo_side, halo_place = lane >> 5, lane & 31
    wanted = place + (tap - 1)
    whole = (halo_side == side) & (halo_place == wanted)
    along = (side == 0) | (side == 2)
    end = jnp.where(side == 0, 0, 31)
    low = ((halo_side == side) & (halo_place == 0)) | ((halo_side == 3) & (halo_place == end))
    high = ((halo_side == side) & (halo_place == 31)) | ((halo_side == 1) & (halo_place == end))
    half = along & (((wanted == -1) & low) | ((wanted == 32) & high))
    return jnp.where(whole, 1.0, jnp.where(half, 0.5, 0.0)).astype(BF16)


def side_tap(side, tap):
    return ((0, tap), (tap, 2), (2, tap), (tap, 0))[side]


def split_float(value):
    high = value.astype(BF16)
    low = (value - high.astype(F32)).astype(BF16)
    return jnp.concatenate([high, low], axis=0)


def make_tables(edge_map, t):
    row, lane = iota((128, 128), 0), iota((128, 128), 1)
    side, place = facing(edge_map, row)
    pixel = border_pixel(side, place)
    plain = border_pixel(row >> 5, row & 31)
    turn = ones_where(lane == side * 32 + place)
    t.turn[...] = turn
    for block in range(8):
        here = lane + block * 128
        t.pick[:, block * 128 : (block + 1) * 128] = ones_where(here == pixel)
        t.border[:, block * 128 : (block + 1) * 128] = ones_where(here == plain)
    cross = dot_nt(t.border[...], t.border[...]).astype(BF16)
    t.cross[:, 0:128] = cross
    t.cross[:, 128:256] = cross
    t.cross_in[...] = dot_nt(t.border[...], t.pick[...]).astype(BF16)
    for tap in range(3):
        taps = ring_taps(tap)
        t.ring[tap * 128 : (tap + 1) * 128, :] = dot_nt(taps, turn).astype(BF16)
        back = dot_nt(turn, taps).astype(BF16)
        t.ring_back[:, tap * 128 : (tap + 1) * 128] = back
        t.ring_back[:, 384 + tap * 128 : 384 + (tap + 1) * 128] = back


def lay_weights(target, block):
    empty = jnp.zeros((384, 128), BF16)
    target[0, :, 128:256] = empty
    target[3, :, 0:128] = empty
    for row in range(3):
        for col in range(3):
            part = block(row, col)
            target[row, col * 128 : (col + 1) * 128, 0:128] = part
            target[row + 1, col * 128 : (col + 1) * 128, 128:256] = part


def lay_shifted(target, frame, pair, value):
    col = iota((64, 128), 0) & 31
    before = jnp.where(col == 0, 0.0, pltpu.roll(value, 1, 0))
    after = jnp.where(col == 31, 0.0, pltpu.roll(value, 63, 0))
    for tap, part in enumerate((before, value, after)):
        target[tap, frame, pl.ds(1 + 2 * pair, 2)] = part.astype(BF16).reshape(2, 32, 128)


def lay_rows(target, frame, pair, value):
    part = value.reshape(2, 32, 128)
    for tap in range(3):
        target[tap, frame, pl.ds(2 * pair + tap, 2)] = part


def clear_rims(shifted):
    for tap in range(3):
        for frame in range(2):
            shifted[tap, frame, 0] = jnp.zeros((32, 128), BF16)
            shifted[tap, frame, 33] = jnp.zeros((32, 128), BF16)
            shifted[tap, frame, 34] = jnp.zeros((32, 128), BF16)


def tile_conv(shifted, weights, result):
    for frame in range(2):
        total = None
        for row in range(4):
            rows = jnp.concatenate(
                [
                    shifted[tap, frame, row : row + 32]
                    .reshape(16, 2, 32, 128)[:, 0]
                    .reshape(512, 128)
                    for tap in range(3)
                ],
                axis=1,
            )
            part = dot(rows, weights[row])
            total = part if total is None else total + part
        for pair in range(16):
            first = frame * 1024 + pair * 64
            rows = slice(pair * 32, (pair + 1) * 32)
            result[first : first + 32, :] = total[rows, 0:128]
            result[first + 32 : first + 64, :] = total[rows, 128:256]


def transpose_shifted(shifted, target):
    for frame in range(2):
        for tap in range(3):
            target[tap * 128 : (tap + 1) * 128, frame * 1024 : (frame + 1) * 1024] = (
                shifted[tap, frame, 1:33].reshape(1024, 128).T
            )


def picked(table, image):
    parts = [
        dot(table[...], image[frame * 16 : (frame + 1) * 16].reshape(1024, 128))
        for frame in range(2)
    ]
    return jnp.concatenate(parts, axis=1).astype(BF16)


def halo_share(t, arrived, weights, ring_rows):
    around = dot(t.ring[...], arrived[...].reshape(128, 256)).astype(BF16)
    parts = []
    for side in range(4):
        for frame in range(2):
            lanes = slice(frame * 128, (frame + 1) * 128)
            ring_rows[side, frame * 32 : (frame + 1) * 32, :] = jnp.concatenate(
                [
                    around[tap * 128 + side * 32 : tap * 128 + (side + 1) * 32, lanes]
                    for tap in range(3)
                ],
                axis=1,
            )
        taps = jnp.concatenate([weights[side_tap(side, tap)] for tap in range(3)], axis=0)
        value = dot(ring_rows[side], taps)
        parts.append(jnp.concatenate([value[0:32], value[32:64]], axis=1))
    return split_float(jnp.concatenate(parts, axis=0))


def lay_border(border, border_rows):
    for side in range(4):
        here = border[side * 32 : (side + 1) * 32]
        border_rows[side] = jnp.concatenate([here[:, 0:128], here[:, 128:256]], axis=0)


def ring_gradient(t, weights, border_rows, leaving):
    rows = [[None] * 4 for tap in range(3)]
    for side in range(4):
        for tap in range(3):
            value = dot_nt(border_rows[side], weights[side_tap(side, tap)])
            rows[tap][side] = jnp.concatenate([value[0:32], value[32:64]], axis=1)
    stacked = jnp.concatenate([rows[tap][side] for tap in range(3) for side in range(4)], axis=0)
    leaving[...] = dot(t.ring_back[...], split_float(stacked)).astype(BF16).reshape(4, 32, 256)


def kernel_gradient(turned, spread_rows, ring_rows, border_rows, bias, own):
    total = None
    for frame in range(2):
        part = dot(
            turned[:, frame * 1024 : (frame + 1) * 1024],
            jnp.concatenate(
                [spread_rows[tap, frame, 1:33].reshape(1024, 128) for tap in range(3)], axis=1
            ),
        )
        total = part if total is None else total + part
    parts = [dot_tn(ring_rows[side], border_rows[side]) for side in range(4)]
    for row in range(3):
        for col in range(3):
            value = total[col * 128 : (col + 1) * 128, row * 128 : (row + 1) * 128]
            for side in range(4):
                for tap in range(3):
                    if side_tap(side, tap) == (row, col):
                        value = value + parts[side][tap * 128 : (tap + 1) * 128]
            first = (row * 3 + col) * 16
            own[first : first + 16] = value.reshape(16, 8, 128)
    own[144] = jnp.concatenate([bias, jnp.zeros((7, 128), F32)], axis=0)
    own[145:160] = jnp.zeros((15, 8, 128), F32)


def halo_partners():
    tile, member, core, spot, floor = coordinates()
    count = 2 * PLANE * (DEPTH // 2)
    steps = (count - ROW_TILES, 1, ROW_TILES, count - 1)
    return [(lax.rem(tile + step, count), member) for step in steps]


class Halo:
    def __init__(self, leaving, arrived, send_sem, recv_sem):
        self.leaving, self.arrived = leaving, arrived
        self.send_sem, self.recv_sem = send_sem, recv_sem
        self.partners = halo_partners()

    def copies(self, turn):
        return [
            remote(
                self.leaving.at[turn, way],
                self.arrived.at[turn, (way + 2) % 4],
                self.send_sem.at[turn, way],
                self.recv_sem.at[turn, (way + 2) % 4],
                self.partners[way],
            )
            for way in range(4)
        ]

    def start(self, turn):
        for copy in self.copies(turn):
            copy.start()

    def wait(self, turn):
        for copy in self.copies(turn):
            copy.wait_recv()

    def drain(self):
        for turn in range(4):
            for copy in self.copies(turn):
                copy.wait_send()


TABLES = {
    "pick": (128, 1024),
    "border": (128, 1024),
    "turn": (128, 128),
    "cross": (128, 256),
    "cross_in": (128, 128),
    "ring": (384, 128),
    "ring_back": (128, 768),
}
IMAGE = (32, 64, 128)
SHIFTED = (3, 2, 36, 32, 128)
BUFFERS = {
    "source": (IMAGE, BF16),
    "upstream": (IMAGE, BF16),
    "first": ((3, 3, 128, 128), BF16),
    "second": ((3, 3, 128, 128), BF16),
    "first_fwd": ((4, 384, 256), BF16),
    "first_back": ((4, 384, 256), BF16),
    "second_fwd": ((4, 384, 256), BF16),
    "second_back": ((4, 384, 256), BF16),
    "shift_one": (SHIFTED, BF16),
    "shift_two": (SHIFTED, BF16),
    "shift_grad": (SHIFTED, BF16),
    "row_grad": ((3, 2, 34, 32, 128), BF16),
    "turned_one": ((384, 2048), BF16),
    "turned_two": ((384, 2048), BF16),
    "hidden": ((2048, 128), F32),
    "hidden_border": ((128, 256), F32),
    "slope_border": ((128, 256), F32),
    "upstream_border": ((128, 256), BF16),
    "grad": (IMAGE, BF16),
    "slope": (IMAGE, F32),
    "ring_one": ((4, 64, 384), BF16),
    "ring_two": ((4, 64, 384), BF16),
    "border_grad": ((4, 64, 128), BF16),
    "leaving": ((4, 4, 32, 256), BF16),
    "arrived": ((4, 4, 32, 256), BF16),
}


class Names:
    def __init__(self, names, refs):
        for name, ref in zip(names, refs):
            setattr(self, name, ref)


def step_scratch():
    dma = pltpu.SemaphoreType.DMA
    return (
        [pltpu.VMEM(shape, BF16) for shape in TABLES.values()]
        + [pltpu.VMEM(shape, kind) for shape, kind in BUFFERS.values()]
        + [dma((4, 4)), dma((4, 4)), dma((4,))]
        + sum_scratch()
        + sum_scratch()
    )


def gelu_parts(hidden):
    bell = 0.5 * (1.0 + lax.erf(hidden * ROOT_HALF))
    return hidden * bell, bell + hidden * jnp.exp(-0.5 * hidden * hidden) * INV_ROOT_TAU


def rows_of(index):
    return pl.ds(pl.multiple_of(index * 64, 64), 64)


def twice(bias):
    return jnp.concatenate([bias, bias], axis=1)


def border_of(image):
    frames = []
    for frame in range(2):
        first = frame * 1024
        frames.append(
            jnp.concatenate(
                [
                    image[first : first + 32, :],
                    image[pl.ds(first + 31, 32, stride=32), :],
                    image[first + 992 : first + 1024, :],
                    image[pl.ds(first, 32, stride=32), :],
                ],
                axis=0,
            )
        )
    return jnp.concatenate(frames, axis=1)


def set_border(image, border):
    for frame in range(2):
        first = frame * 1024
        part = border[:, frame * 128 : (frame + 1) * 128]
        image[first : first + 32, :] = part[0:32]
        image[pl.ds(first + 31, 32, stride=32), :] = part[32:64]
        image[first + 992 : first + 1024, :] = part[64:96]
        image[pl.ds(first, 32, stride=32), :] = part[96:128]


def each_pair(body, start=0):
    def step(pair, carry):
        for frame in range(2):
            carry = body(frame, pair, frame * 16 + pair, slice(frame * 128, (frame + 1) * 128), carry)
        return carry

    return lax.fori_loop(0, 16, step, start)


def fold_rows(value):
    return jnp.sum(value.reshape(8, 8, 128), axis=0)


def step_kernel(edge_map, fields, cotangent, w_first, b_first, w_second, b_second,
                response_out, field_grad_out, sum_one_out, sum_two_out, *scratch):
    tables, scratch = Names(TABLES, scratch), scratch[len(TABLES) :]
    v, scratch = Names(BUFFERS, scratch), scratch[len(BUFFERS) :]
    halo = Halo(v.leaving, v.arrived, scratch[0], scratch[1])
    local_sem, scratch = scratch[2], scratch[3:]
    count = len(sum_scratch())
    sum_one, sum_two = GradientSum(scratch[:count]), GradientSum(scratch[count:])

    mate, plane, column = sum_partners()
    partners = [*column, *halo_partners(), *plane, mate]
    barrier = pltpu.get_barrier_semaphore()
    for device in partners:
        pl.semaphore_signal(
            barrier, inc=1, device_id=device, device_id_type=pl.DeviceIdType.MESH
        )
    loads = [
        pltpu.make_async_copy(source, target, local_sem.at[index])
        for index, (source, target) in enumerate(
            ((fields, v.source), (w_first, v.first), (w_second, v.second), (cotangent, v.upstream))
        )
    ]
    for load in loads:
        load.start()
    make_tables(edge_map, tables)
    loads[0].wait()
    v.leaving[0] = picked(tables.pick, v.source).reshape(4, 32, 256)
    pl.semaphore_wait(barrier, len(partners))
    halo.start(0)

    for shifted in (v.shift_one, v.shift_two, v.shift_grad):
        clear_rims(shifted)
    for frame in range(2):
        v.row_grad[0, frame, 32:34] = jnp.zeros((2, 32, 128), BF16)
        v.row_grad[2, frame, 0:2] = jnp.zeros((2, 32, 128), BF16)

    def shift_source(frame, pair, index, lanes, carry):
        lay_shifted(v.shift_one, frame, pair, v.source[index].astype(F32))
        return carry

    each_pair(shift_source)
    loads[1].wait()
    lay_weights(v.first_fwd, lambda row, col: v.first[row, col])
    tile_conv(v.shift_one, v.first_fwd, v.hidden)
    v.hidden_border[...] = border_of(v.hidden)
    loads[2].wait()
    lay_weights(v.second_fwd, lambda row, col: v.second[row, col])
    loads[3].wait()
    v.upstream_border[...] = picked(tables.border, v.upstream)
    transpose_shifted(v.shift_one, v.turned_one)
    lay_weights(v.second_back, lambda row, col: v.second[2 - row, 2 - col].T)
    lay_weights(v.first_back, lambda row, col: v.first[2 - row, 2 - col].T)

    halo.wait(0)
    both = halo_share(tables, v.arrived.at[0], v.first, v.ring_one)
    border = v.hidden_border[...] + dot(tables.cross[...], both)
    v.hidden_border[...] = border
    value, slope = gelu_parts(border + twice(b_first[...]))
    v.leaving[1] = dot(tables.turn[...], value.astype(BF16)).astype(BF16).reshape(4, 32, 256)
    v.slope_border[...] = slope
    halo.start(1)
    set_border(v.hidden, v.hidden_border[...])

    def activate(frame, pair, index, lanes, carry):
        hidden = v.hidden[rows_of(index)] + b_first[...]
        value, slope = gelu_parts(hidden)
        v.slope[index] = slope
        lay_shifted(v.shift_two, frame, pair, value)
        return carry

    each_pair(activate)
    tile_conv(v.shift_two, v.second_fwd, v.hidden)
    v.hidden_border[...] = border_of(v.hidden)
    transpose_shifted(v.shift_two, v.turned_two)

    halo.wait(1)
    both = halo_share(tables, v.arrived.at[1], v.second, v.ring_two)
    border = v.hidden_border[...] + dot(tables.cross[...], both)
    v.hidden_border[...] = border
    value, slope = gelu_parts(border + twice(b_second[...]))
    border = (v.upstream_border[...].astype(F32) * slope).astype(BF16)
    lay_border(border, v.border_grad)
    ring_gradient(tables, v.second, v.border_grad, v.leaving.at[2])
    halo.start(2)
    set_border(v.hidden, v.hidden_border[...])

    def respond(frame, pair, index, lanes, carry):
        hidden = v.hidden[rows_of(index)] + b_second[...]
        value, slope = gelu_parts(hidden)
        response_out[index] = value.astype(BF16)
        grad = (v.upstream[index].astype(F32) * slope).astype(BF16)
        wide = grad.astype(F32)
        lay_shifted(v.shift_grad, frame, pair, wide)
        lay_rows(v.row_grad, frame, pair, grad)
        return carry + fold_rows(wide)

    bias = each_pair(respond, jnp.zeros((8, 128), F32))
    bias = jnp.sum(bias, axis=0, keepdims=True)
    tile_conv(v.shift_grad, v.second_back, v.hidden)
    v.hidden_border[...] = border_of(v.hidden)
    kernel_gradient(
        v.turned_two, v.row_grad, v.ring_two, v.border_grad, bias, sum_two.own
    )
    sum_two.start()

    sum_two.spread_plane()

    halo.wait(2)
    came = v.arrived[2].reshape(128, 256)
    border = v.hidden_border[...] + dot(tables.cross_in[...], came)
    set_border(v.hidden, border)
    border = (border * v.slope_border[...]).astype(BF16)
    lay_border(border, v.border_grad)

    def descend(frame, pair, index, lanes, carry):
        grad = (v.hidden[rows_of(index)] * v.slope[index]).astype(BF16)
        v.grad[index] = grad
        lay_rows(v.row_grad, frame, pair, grad)
        return carry + fold_rows(grad.astype(F32))

    bias = each_pair(descend, jnp.zeros((8, 128), F32))
    bias = jnp.sum(bias, axis=0, keepdims=True)
    kernel_gradient(
        v.turned_one, v.row_grad, v.ring_one, v.border_grad, bias, sum_one.own
    )
    sum_one.start()
    ring_gradient(tables, v.first, v.border_grad, v.leaving.at[3])
    halo.start(3)

    def shift_grad(frame, pair, index, lanes, carry):
        lay_shifted(v.shift_grad, frame, pair, v.grad[index].astype(F32))
        return carry

    sum_one.spread_plane()
    each_pair(shift_grad)
    sum_two.spread_column()
    tile_conv(v.shift_grad, v.first_back, v.hidden)
    v.hidden_border[...] = border_of(v.hidden)
    halo.wait(3)
    came = v.arrived[3].reshape(128, 256)
    set_border(v.hidden, v.hidden_border[...] + dot(tables.cross_in[...], came))
    sum_one.spread_column()

    def finish(frame, pair, index, lanes, carry):
        field_grad_out[index] = v.hidden[rows_of(index)].astype(BF16)
        return carry

    each_pair(finish)
    sum_two.gather_plane()
    sum_one.gather_plane()
    halo.drain()
    sum_two.forward()
    sum_two.finish()
    sum_two_out[...] = sum_two.gathered[...].reshape(2 * HALF, 8, 128)
    sum_two.drain()
    sum_one.forward()
    sum_one.finish()
    sum_one_out[...] = sum_one.gathered[...].reshape(2 * HALF, 8, 128)
    sum_one.drain()


def store_kernel(scale, response, field_grad, sum_one, sum_two, response_out, field_grad_out,
                 kernel_one_out, bias_one_out, kernel_two_out, bias_two_out, kernel_one,
                 bias_one, kernel_two, bias_two, sems):
    stores = [
        pltpu.make_async_copy(response, response_out, sems.at[0]),
        pltpu.make_async_copy(field_grad, field_grad_out, sems.at[1]),
    ]
    for store in stores:
        store.start()
    for total, kernel, bias, kernel_out, bias_out in (
        (sum_one, kernel_one, bias_one, kernel_one_out, bias_one_out),
        (sum_two, kernel_two, bias_two, kernel_two_out, bias_two_out),
    ):
        kernel[...] = total[0:144].astype(F32) * scale
        bias[...] = total[144].astype(F32)[0:1] * scale
        for source, target in ((kernel, kernel_out), (bias, bias_out)):
            stores.append(pltpu.make_async_copy(source, target, sems.at[len(stores)]))
            stores[-1].start()
    for store in stores:
        store.wait()


def per_device(fields, cotangent, edge_map, w_first, b_first, w_second, b_second):
    frames, tile_side, channels = (fields.shape[2], fields.shape[3], fields.shape[5])
    samples = lax.axis_size("tile") * lax.axis_size("member") * frames * tile_side * tile_side
    kernel = jax.ShapeDtypeStruct((9 * channels // 8, 8, channels), F32)
    bias = jax.ShapeDtypeStruct((1, channels), F32)
    image = jax.ShapeDtypeStruct(IMAGE, BF16)
    local = pl.BlockSpec(memory_space=pltpu.VMEM)
    far = pl.BlockSpec(memory_space=pltpu.HBM)
    near = pltpu.VMEM(IMAGE, BF16)
    sums = pltpu.VMEM((2 * HALF, 8, 128), BF16)
    results = pl.pallas_call(
        step_kernel,
        out_shape=[near, near, sums, sums],
        in_specs=[
            pl.BlockSpec(memory_space=pltpu.SMEM),
            far,
            far,
            far,
            local,
            far,
            local,
        ],
        out_specs=[local] * 4,
        scratch_shapes=step_scratch(),
        compiler_params=pltpu.CompilerParams(
            collective_id=0, has_side_effects=True, vmem_limit_bytes=63_600 << 10
        ),
    )(
        edge_map.reshape(4, 2).T,
        fields.reshape(IMAGE),
        cotangent.reshape(IMAGE),
        w_first,
        b_first.reshape(1, channels),
        w_second,
        b_second.reshape(1, channels),
    )
    outs = pl.pallas_call(
        functools.partial(store_kernel, float(samples) ** -0.5),
        out_shape=[image, image, kernel, bias, kernel, bias],
        in_specs=[local] * 4,
        out_specs=[far] * 6,
        scratch_shapes=[
            pltpu.VMEM(kernel.shape, F32),
            pltpu.VMEM(bias.shape, F32),
            pltpu.VMEM(kernel.shape, F32),
            pltpu.VMEM(bias.shape, F32),
            pltpu.SemaphoreType.DMA((6,)),
        ],
        compiler_params=pltpu.CompilerParams(vmem_limit_bytes=8 << 20),
    )(*results)
    return (
        outs[0].reshape(fields.shape),
        outs[1].reshape(fields.shape),
        outs[2].reshape(w_first.shape),
        outs[3].reshape(b_first.shape),
        outs[4].reshape(w_second.shape),
        outs[5].reshape(b_second.shape),
    )


def solution(mesh):
    in_specs = (
        P("member", "tile", None, None, None, None),
        P("member", "tile", None, None, None, None),
        P("tile", None, None),
        P(),
        P(),
        P(),
        P(),
    )
    out_specs = (
        P("member", "tile", None, None, None, None),
        P("member", "tile", None, None, None, None),
        P(),
        P(),
        P(),
        P(),
    )
    return jax.shard_map(
        per_device, mesh=mesh, in_specs=in_specs, out_specs=out_specs, check_vma=False
    )
```

```python
import functools

import jax
import jax.numpy as jnp
from jax import lax
from jax.experimental import pallas as pl
from jax.experimental.pallas import tpu as pltpu
from jax.sharding import PartitionSpec as P

ROW_TILES = 8
ROOT_HALF = 0.7071067811865476
INV_ROOT_TAU = 0.3989422804014327
BF16 = jnp.bfloat16
F32 = jnp.float32

PLANE = 16
SIDE = 4
DEPTH = 8
PIECE = 5
HALF = PLANE * PIECE
PART_ROWS = 2 * HALF * 8


def coordinates():
    tile = lax.axis_index("tile")
    member = lax.axis_index("member")
    core = lax.rem(tile, 2)
    spot = lax.rem(tile // 2, PLANE)
    floor = tile // (2 * PLANE)
    return tile, member, core, spot, floor


def ring_hops(step, size):
    return min(step, size - step)


PLANE_STEPS = sorted(
    [(dx, dy) for dx in range(SIDE) for dy in range(SIDE) if (dx, dy) != (0, 0)],
    key=lambda step: -sum(ring_hops(part, SIDE) for part in step),
)
COLUMN_STEPS = sorted(range(1, DEPTH), key=lambda step: -ring_hops(step, DEPTH))


def moved(spot, step):
    across = lax.rem(spot // SIDE + step[0] + SIDE, SIDE)
    return across * SIDE + lax.rem(lax.rem(spot, SIDE) + step[1] + SIDE, SIDE)


def sum_partners():
    tile, member, core, spot, floor = coordinates()
    mate = (tile - core + (1 - core), member)
    plane = [
        ((floor * PLANE + moved(spot, step)) * 2 + core, member) for step in PLANE_STEPS
    ]
    level = floor * 2 + member
    column = []
    for step in COLUMN_STEPS:
        other = lax.rem(level + step, DEPTH)
        column.append((((other // 2) * PLANE + spot) * 2 + core, lax.rem(other, 2)))
    return mate, plane, column


def remote(source, target, send_sem, recv_sem, device):
    return pltpu.make_async_remote_copy(
        src_ref=source,
        dst_ref=target,
        send_sem=send_sem,
        recv_sem=recv_sem,
        device_id=device,
        device_id_type=pl.DeviceIdType.MESH,
    )


def sum_scratch():
    dma = pltpu.SemaphoreType.DMA
    return [
        pltpu.VMEM((2 * HALF, 8, 128), jnp.float32),
        pltpu.VMEM((2 * HALF, 8, 128), jnp.bfloat16),
        pltpu.VMEM((HALF, 8, 128), jnp.bfloat16),
        pltpu.VMEM((PLANE, PIECE, 8, 128), jnp.float32),
        pltpu.VMEM((PLANE, PIECE, 8, 128), jnp.bfloat16),
        pltpu.VMEM((PLANE, PIECE, 8, 128), jnp.bfloat16),
        pltpu.VMEM((DEPTH, PIECE, 8, 128), jnp.bfloat16),
        pltpu.VMEM((2, PLANE, PIECE, 8, 128), jnp.bfloat16),
        dma((2,)),
        dma((2,)),
        dma((2,)),
        dma((2,)),
        dma((2,)),
    ]


class GradientSum:
    def __init__(self, refs):
        (
            self.own,
            self.halves,
            self.from_mate,
            self.total,
            self.pieces,
            self.from_plane,
            self.from_column,
            self.gathered,
            self.mate_sem,
            self.plane_sem,
            self.column_sem,
            self.gather_sem,
            self.forward_sem,
        ) = refs
        tile, member, core, spot, floor = coordinates()
        self.core, self.spot, self.level = core, spot, floor * 2 + member
        self.mate, self.plane, self.column = sum_partners()

    def to_mate(self):
        return remote(
            self.halves.at[pl.ds((1 - self.core) * HALF, HALF)],
            self.from_mate,
            self.mate_sem.at[0],
            self.mate_sem.at[1],
            self.mate,
        )

    def to_plane(self, index):
        target = moved(self.spot, PLANE_STEPS[index])
        return remote(
            self.pieces.at[target],
            self.from_plane.at[self.spot],
            self.plane_sem.at[0],
            self.plane_sem.at[1],
            self.plane[index],
        )

    def to_column(self, index):
        return remote(
            self.from_column.at[self.level],
            self.from_column.at[self.level],
            self.column_sem.at[0],
            self.column_sem.at[1],
            self.column[index],
        )

    def to_gather(self, index):
        return remote(
            self.gathered.at[self.core, self.spot],
            self.gathered.at[self.core, self.spot],
            self.gather_sem.at[0],
            self.gather_sem.at[1],
            self.plane[index],
        )

    def to_forward(self):
        return remote(
            self.gathered.at[self.core],
            self.gathered.at[self.core],
            self.forward_sem.at[0],
            self.forward_sem.at[1],
            self.mate,
        )

    def wait_all(self, buffer, count, sem):
        pltpu.make_async_copy(
            buffer.at[pl.ds(0, count)], buffer.at[pl.ds(0, count)], sem
        ).wait()

    def start(self):
        self.halves[...] = self.own[...].astype(jnp.bfloat16)
        self.to_mate().start()

    def spread_plane(self):
        self.to_mate().wait_recv()
        total = self.own[pl.ds(self.core * HALF, HALF)] + self.from_mate[...].astype(jnp.float32)
        total = total.reshape(PLANE, PIECE, 8, 128)
        self.total[...] = total
        self.pieces[...] = total.astype(jnp.bfloat16)
        for index in range(PLANE - 1):
            self.to_plane(index).start()

    def spread_column(self):
        value = self.total[self.spot]
        self.wait_all(self.from_plane, PLANE - 1, self.plane_sem.at[1])
        for step in PLANE_STEPS:
            origin = moved(self.spot, step)
            value = value + self.from_plane[origin].astype(jnp.float32)
        self.from_column[self.level] = value.astype(jnp.bfloat16)
        for index in range(DEPTH - 1):
            self.to_column(index).start()

    def gather_plane(self):
        self.wait_all(self.from_column, DEPTH - 1, self.column_sem.at[1])
        value = jnp.zeros((PIECE, 8, 128), jnp.float32)
        for level in range(DEPTH):
            value = value + self.from_column[level].astype(jnp.float32)
        self.gathered[self.core, self.spot] = value.astype(jnp.bfloat16)
        for index in range(PLANE - 1):
            self.to_gather(index).start()

    def forward(self):
        self.wait_all(self.gathered.at[self.core], PLANE - 1, self.gather_sem.at[1])
        self.to_forward().start()

    def finish(self):
        self.to_forward().wait_recv()

    def drain(self):
        self.to_mate().wait_send()
        self.wait_all(self.pieces, PLANE - 1, self.plane_sem.at[0])
        self.wait_all(self.from_column, DEPTH - 1, self.column_sem.at[0])
        self.wait_all(self.gathered.at[self.core], PLANE - 1, self.gather_sem.at[0])
        self.to_forward().wait_send()


def dot(left, right):
    return jnp.dot(left, right, preferred_element_type=F32)


def dot_nt(left, right):
    return lax.dot_general(left, right, (((1,), (1,)), ((), ())), preferred_element_type=F32)


def dot_tn(left, right):
    return lax.dot_general(left, right, (((0,), (0,)), ((), ())), preferred_element_type=F32)


def iota(shape, axis):
    return lax.broadcasted_iota(jnp.int32, shape, axis)


def ones_where(mask):
    return jnp.where(mask, 1.0, 0.0).astype(BF16)


def border_pixel(side, place):
    return jnp.where(
        side == 0,
        place,
        jnp.where(side == 1, place * 32 + 31, jnp.where(side == 2, place + 992, place * 32)),
    )


def facing(edge_map, index):
    direction, place = index >> 5, index & 31
    side = jnp.zeros_like(index)
    flip = jnp.zeros_like(index)
    for candidate in range(4):
        side = jnp.where(direction == candidate, edge_map[0, candidate], side)
        flip = jnp.where(direction == candidate, edge_map[1, candidate], flip)
    return side, jnp.where(flip == 1, 31 - place, place)


def ring_taps(tap):
    row, lane = iota((128, 128), 0), iota((128, 128), 1)
    side, place = row >> 5, row & 31
    halo_side, halo_place = lane >> 5, lane & 31
    wanted = place + (tap - 1)
    whole = (halo_side == side) & (halo_place == wanted)
    along = (side == 0) | (side == 2)
    end = jnp.where(side == 0, 0, 31)
    low = ((halo_side == side) & (halo_place == 0)) | ((halo_side == 3) & (halo_place == end))
    high = ((halo_side == side) & (halo_place == 31)) | ((halo_side == 1) & (halo_place == end))
    half = along & (((wanted == -1) & low) | ((wanted == 32) & high))
    return jnp.where(whole, 1.0, jnp.where(half, 0.5, 0.0)).astype(BF16)


def side_tap(side, tap):
    return ((0, tap), (tap, 2), (2, tap), (tap, 0))[side]


def split_float(value):
    high = value.astype(BF16)
    low = (value - high.astype(F32)).astype(BF16)
    return jnp.concatenate([high, low], axis=0)


def make_tables(edge_map, t):
    row, lane = iota((128, 128), 0), iota((128, 128), 1)
    side, place = facing(edge_map, row)
    pixel = border_pixel(side, place)
    plain = border_pixel(row >> 5, row & 31)
    turn = ones_where(lane == side * 32 + place)
    t.turn[...] = turn
    for block in range(8):
        here = lane + block * 128
        t.pick[:, block * 128 : (block + 1) * 128] = ones_where(here == pixel)
        t.border[:, block * 128 : (block + 1) * 128] = ones_where(here == plain)
    cross = dot_nt(t.border[...], t.border[...]).astype(BF16)
    t.cross[:, 0:128] = cross
    t.cross[:, 128:256] = cross
    t.cross_in[...] = dot_nt(t.border[...], t.pick[...]).astype(BF16)
    for tap in range(3):
        taps = ring_taps(tap)
        t.ring[tap * 128 : (tap + 1) * 128, :] = dot_nt(taps, turn).astype(BF16)
        back = dot_nt(turn, taps).astype(BF16)
        t.ring_back[:, tap * 128 : (tap + 1) * 128] = back
        t.ring_back[:, 384 + tap * 128 : 384 + (tap + 1) * 128] = back


def lay_weights(target, block):
    empty = jnp.zeros((384, 128), BF16)
    target[0, :, 128:256] = empty
    target[3, :, 0:128] = empty
    for row in range(3):
        for col in range(3):
            part = block(row, col)
            target[row, col * 128 : (col + 1) * 128, 0:128] = part
            target[row + 1, col * 128 : (col + 1) * 128, 128:256] = part


def lay_shifted(target, frame, pair, value):
    col = iota((64, 128), 0) & 31
    before = jnp.where(col == 0, 0.0, pltpu.roll(value, 1, 0))
    after = jnp.where(col == 31, 0.0, pltpu.roll(value, 63, 0))
    for tap, part in enumerate((before, value, after)):
        target[tap, frame, pl.ds(1 + 2 * pair, 2)] = part.astype(BF16).reshape(2, 32, 128)


def lay_rows(target, frame, pair, value):
    part = value.reshape(2, 32, 128)
    for tap in range(3):
        target[tap, frame, pl.ds(2 * pair + tap, 2)] = part


def clear_rims(shifted):
    for tap in range(3):
        for frame in range(2):
            shifted[tap, frame, 0] = jnp.zeros((32, 128), BF16)
            shifted[tap, frame, 33] = jnp.zeros((32, 128), BF16)
            shifted[tap, frame, 34] = jnp.zeros((32, 128), BF16)


def tile_conv(shifted, weights, result):
    for frame in range(2):
        total = None
        for row in range(4):
            rows = jnp.concatenate(
                [
                    shifted[tap, frame, row : row + 32]
                    .reshape(16, 2, 32, 128)[:, 0]
                    .reshape(512, 128)
                    for tap in range(3)
                ],
                axis=1,
            )
            part = dot(rows, weights[row])
            total = part if total is None else total + part
        for pair in range(16):
            first = frame * 1024 + pair * 64
            rows = slice(pair * 32, (pair + 1) * 32)
            result[first : first + 32, :] = total[rows, 0:128]
            result[first + 32 : first + 64, :] = total[rows, 128:256]


def transpose_shifted(shifted, target):
    for frame in range(2):
        for tap in range(3):
            target[tap * 128 : (tap + 1) * 128, frame * 1024 : (frame + 1) * 1024] = (
                shifted[tap, frame, 1:33].reshape(1024, 128).T
            )


def picked(table, image):
    parts = [
        dot(table[...], image[frame * 16 : (frame + 1) * 16].reshape(1024, 128))
        for frame in range(2)
    ]
    return jnp.concatenate(parts, axis=1).astype(BF16)


def halo_share(t, arrived, weights, ring_rows):
    around = dot(t.ring[...], arrived[...].reshape(128, 256)).astype(BF16)
    parts = []
    for side in range(4):
        for frame in range(2):
            lanes = slice(frame * 128, (frame + 1) * 128)
            ring_rows[side, frame * 32 : (frame + 1) * 32, :] = jnp.concatenate(
                [
                    around[tap * 128 + side * 32 : tap * 128 + (side + 1) * 32, lanes]
                    for tap in range(3)
                ],
                axis=1,
            )
        taps = jnp.concatenate([weights[side_tap(side, tap)] for tap in range(3)], axis=0)
        value = dot(ring_rows[side], taps)
        parts.append(jnp.concatenate([value[0:32], value[32:64]], axis=1))
    return split_float(jnp.concatenate(parts, axis=0))


def lay_border(border, border_rows):
    for side in range(4):
        here = border[side * 32 : (side + 1) * 32]
        border_rows[side] = jnp.concatenate([here[:, 0:128], here[:, 128:256]], axis=0)


def ring_gradient(t, weights, border_rows, leaving):
    rows = [[None] * 4 for tap in range(3)]
    for side in range(4):
        for tap in range(3):
            value = dot_nt(border_rows[side], weights[side_tap(side, tap)])
            rows[tap][side] = jnp.concatenate([value[0:32], value[32:64]], axis=1)
    stacked = jnp.concatenate([rows[tap][side] for tap in range(3) for side in range(4)], axis=0)
    leaving[...] = dot(t.ring_back[...], split_float(stacked)).astype(BF16).reshape(4, 32, 256)


def kernel_gradient(turned, spread_rows, ring_rows, border_rows, bias, own):
    total = None
    for frame in range(2):
        part = dot(
            turned[:, frame * 1024 : (frame + 1) * 1024],
            jnp.concatenate(
                [spread_rows[tap, frame, 1:33].reshape(1024, 128) for tap in range(3)], axis=1
            ),
        )
        total = part if total is None else total + part
    parts = [dot_tn(ring_rows[side], border_rows[side]) for side in range(4)]
    for row in range(3):
        for col in range(3):
            value = total[col * 128 : (col + 1) * 128, row * 128 : (row + 1) * 128]
            for side in range(4):
                for tap in range(3):
                    if side_tap(side, tap) == (row, col):
                        value = value + parts[side][tap * 128 : (tap + 1) * 128]
            first = (row * 3 + col) * 16
            own[first : first + 16] = value.reshape(16, 8, 128)
    own[144] = jnp.concatenate([bias, jnp.zeros((7, 128), F32)], axis=0)
    own[145:160] = jnp.zeros((15, 8, 128), F32)


def halo_partners():
    tile, member, core, spot, floor = coordinates()
    count = 2 * PLANE * (DEPTH // 2)
    steps = (count - ROW_TILES, 1, ROW_TILES, count - 1)
    return [(lax.rem(tile + step, count), member) for step in steps]


class Halo:
    def __init__(self, leaving, arrived, send_sem, recv_sem):
        self.leaving, self.arrived = leaving, arrived
        self.send_sem, self.recv_sem = send_sem, recv_sem
        self.partners = halo_partners()

    def copies(self, turn):
        return [
            remote(
                self.leaving.at[turn, way],
                self.arrived.at[turn, (way + 2) % 4],
                self.send_sem.at[turn, way],
                self.recv_sem.at[turn, (way + 2) % 4],
                self.partners[way],
            )
            for way in range(4)
        ]

    def start(self, turn):
        for copy in self.copies(turn):
            copy.start()

    def wait(self, turn):
        for copy in self.copies(turn):
            copy.wait_recv()

    def drain(self):
        for turn in range(4):
            for copy in self.copies(turn):
                copy.wait_send()


TABLES = {
    "pick": (128, 1024),
    "border": (128, 1024),
    "turn": (128, 128),
    "cross": (128, 256),
    "cross_in": (128, 128),
    "ring": (384, 128),
    "ring_back": (128, 768),
}
IMAGE = (32, 64, 128)
SHIFTED = (3, 2, 36, 32, 128)
BUFFERS = {
    "source": (IMAGE, BF16),
    "upstream": (IMAGE, BF16),
    "first": ((3, 3, 128, 128), BF16),
    "second": ((3, 3, 128, 128), BF16),
    "first_fwd": ((4, 384, 256), BF16),
    "first_back": ((4, 384, 256), BF16),
    "second_fwd": ((4, 384, 256), BF16),
    "second_back": ((4, 384, 256), BF16),
    "shift_one": (SHIFTED, BF16),
    "shift_two": (SHIFTED, BF16),
    "shift_grad": (SHIFTED, BF16),
    "row_grad": ((3, 2, 34, 32, 128), BF16),
    "turned_one": ((384, 2048), BF16),
    "turned_two": ((384, 2048), BF16),
    "hidden": ((2048, 128), F32),
    "hidden_border": ((128, 256), F32),
    "slope_border": ((128, 256), F32),
    "upstream_border": ((128, 256), BF16),
    "grad": (IMAGE, BF16),
    "slope": (IMAGE, F32),
    "ring_one": ((4, 64, 384), BF16),
    "ring_two": ((4, 64, 384), BF16),
    "border_grad": ((4, 64, 128), BF16),
    "leaving": ((4, 4, 32, 256), BF16),
    "arrived": ((4, 4, 32, 256), BF16),
}


class Names:
    def __init__(self, names, refs):
        for name, ref in zip(names, refs):
            setattr(self, name, ref)


def step_scratch():
    dma = pltpu.SemaphoreType.DMA
    return (
        [pltpu.VMEM(shape, BF16) for shape in TABLES.values()]
        + [pltpu.VMEM(shape, kind) for shape, kind in BUFFERS.values()]
        + [dma((4, 4)), dma((4, 4)), dma((4,))]
        + sum_scratch()
        + sum_scratch()
    )


def gelu_parts(hidden):
    bell = 0.5 * (1.0 + lax.erf(hidden * ROOT_HALF))
    return hidden * bell, bell + hidden * jnp.exp(-0.5 * hidden * hidden) * INV_ROOT_TAU


def rows_of(index):
    return pl.ds(pl.multiple_of(index * 64, 64), 64)


def twice(bias):
    return jnp.concatenate([bias, bias], axis=1)


def border_of(image):
    frames = []
    for frame in range(2):
        first = frame * 1024
        frames.append(
            jnp.concatenate(
                [
                    image[first : first + 32, :],
                    image[pl.ds(first + 31, 32, stride=32), :],
                    image[first + 992 : first + 1024, :],
                    image[pl.ds(first, 32, stride=32), :],
                ],
                axis=0,
            )
        )
    return jnp.concatenate(frames, axis=1)


def set_border(image, border):
    for frame in range(2):
        first = frame * 1024
        part = border[:, frame * 128 : (frame + 1) * 128]
        image[first : first + 32, :] = part[0:32]
        image[pl.ds(first + 31, 32, stride=32), :] = part[32:64]
        image[first + 992 : first + 1024, :] = part[64:96]
        image[pl.ds(first, 32, stride=32), :] = part[96:128]


def each_pair(body, start=0):
    def step(pair, carry):
        for frame in range(2):
            carry = body(frame, pair, frame * 16 + pair, slice(frame * 128, (frame + 1) * 128), carry)
        return carry

    return lax.fori_loop(0, 16, step, start)


def fold_rows(value):
    return jnp.sum(value.reshape(8, 8, 128), axis=0)


def step_kernel(edge_map, fields, cotangent, w_first, b_first, w_second, b_second,
                response_out, field_grad_out, sum_one_out, sum_two_out, *scratch):
    tables, scratch = Names(TABLES, scratch), scratch[len(TABLES) :]
    v, scratch = Names(BUFFERS, scratch), scratch[len(BUFFERS) :]
    halo = Halo(v.leaving, v.arrived, scratch[0], scratch[1])
    local_sem, scratch = scratch[2], scratch[3:]
    count = len(sum_scratch())
    sum_one, sum_two = GradientSum(scratch[:count]), GradientSum(scratch[count:])

    mate, plane, column = sum_partners()
    partners = [*column, *halo_partners(), *plane, mate]
    barrier = pltpu.get_barrier_semaphore()
    for device in partners:
        pl.semaphore_signal(
            barrier, inc=1, device_id=device, device_id_type=pl.DeviceIdType.MESH
        )
    loads = [
        pltpu.make_async_copy(source, target, local_sem.at[index])
        for index, (source, target) in enumerate(
            ((fields, v.source), (w_first, v.first), (w_second, v.second), (cotangent, v.upstream))
        )
    ]
    for load in loads:
        load.start()
    make_tables(edge_map, tables)
    loads[0].wait()
    v.leaving[0] = picked(tables.pick, v.source).reshape(4, 32, 256)
    pl.semaphore_wait(barrier, len(partners))
    halo.start(0)

    for shifted in (v.shift_one, v.shift_two, v.shift_grad):
        clear_rims(shifted)
    for frame in range(2):
        v.row_grad[0, frame, 32:34] = jnp.zeros((2, 32, 128), BF16)
        v.row_grad[2, frame, 0:2] = jnp.zeros((2, 32, 128), BF16)

    def shift_source(frame, pair, index, lanes, carry):
        lay_shifted(v.shift_one, frame, pair, v.source[index].astype(F32))
        return carry

    each_pair(shift_source)
    loads[1].wait()
    lay_weights(v.first_fwd, lambda row, col: v.first[row, col])
    tile_conv(v.shift_one, v.first_fwd, v.hidden)
    v.hidden_border[...] = border_of(v.hidden)
    loads[2].wait()
    lay_weights(v.second_fwd, lambda row, col: v.second[row, col])
    loads[3].wait()
    v.upstream_border[...] = picked(tables.border, v.upstream)
    transpose_shifted(v.shift_one, v.turned_one)
    lay_weights(v.second_back, lambda row, col: v.second[2 - row, 2 - col].T)
    lay_weights(v.first_back, lambda row, col: v.first[2 - row, 2 - col].T)

    halo.wait(0)
    both = halo_share(tables, v.arrived.at[0], v.first, v.ring_one)
    border = v.hidden_border[...] + dot(tables.cross[...], both)
    v.hidden_border[...] = border
    value, slope = gelu_parts(border + twice(b_first[...]))
    v.leaving[1] = dot(tables.turn[...], value.astype(BF16)).astype(BF16).reshape(4, 32, 256)
    v.slope_border[...] = slope
    halo.start(1)
    set_border(v.hidden, v.hidden_border[...])

    def activate(frame, pair, index, lanes, carry):
        hidden = v.hidden[rows_of(index)] + b_first[...]
        value, slope = gelu_parts(hidden)
        v.slope[index] = slope
        lay_shifted(v.shift_two, frame, pair, value)
        return carry

    each_pair(activate)
    tile_conv(v.shift_two, v.second_fwd, v.hidden)
    v.hidden_border[...] = border_of(v.hidden)
    transpose_shifted(v.shift_two, v.turned_two)

    halo.wait(1)
    both = halo_share(tables, v.arrived.at[1], v.second, v.ring_two)
    border = v.hidden_border[...] + dot(tables.cross[...], both)
    v.hidden_border[...] = border
    value, slope = gelu_parts(border + twice(b_second[...]))
    border = (v.upstream_border[...].astype(F32) * slope).astype(BF16)
    lay_border(border, v.border_grad)
    ring_gradient(tables, v.second, v.border_grad, v.leaving.at[2])
    halo.start(2)
    set_border(v.hidden, v.hidden_border[...])

    def respond(frame, pair, index, lanes, carry):
        hidden = v.hidden[rows_of(index)] + b_second[...]
        value, slope = gelu_parts(hidden)
        response_out[index] = value.astype(BF16)
        grad = (v.upstream[index].astype(F32) * slope).astype(BF16)
        wide = grad.astype(F32)
        lay_shifted(v.shift_grad, frame, pair, wide)
        lay_rows(v.row_grad, frame, pair, grad)
        return carry + fold_rows(wide)

    bias = each_pair(respond, jnp.zeros((8, 128), F32))
    bias = jnp.sum(bias, axis=0, keepdims=True)
    tile_conv(v.shift_grad, v.second_back, v.hidden)
    v.hidden_border[...] = border_of(v.hidden)
    kernel_gradient(
        v.turned_two, v.row_grad, v.ring_two, v.border_grad, bias, sum_two.own
    )
    sum_two.start()

    sum_two.spread_plane()

    halo.wait(2)
    came = v.arrived[2].reshape(128, 256)
    border = v.hidden_border[...] + dot(tables.cross_in[...], came)
    set_border(v.hidden, border)
    border = (border * v.slope_border[...]).astype(BF16)
    lay_border(border, v.border_grad)

    def descend(frame, pair, index, lanes, carry):
        grad = (v.hidden[rows_of(index)] * v.slope[index]).astype(BF16)
        v.grad[index] = grad
        lay_rows(v.row_grad, frame, pair, grad)
        return carry + fold_rows(grad.astype(F32))

    bias = each_pair(descend, jnp.zeros((8, 128), F32))
    bias = jnp.sum(bias, axis=0, keepdims=True)
    kernel_gradient(
        v.turned_one, v.row_grad, v.ring_one, v.border_grad, bias, sum_one.own
    )
    sum_one.start()
    ring_gradient(tables, v.first, v.border_grad, v.leaving.at[3])
    halo.start(3)

    def shift_grad(frame, pair, index, lanes, carry):
        lay_shifted(v.shift_grad, frame, pair, v.grad[index].astype(F32))
        return carry

    sum_one.spread_plane()
    each_pair(shift_grad)
    sum_two.spread_column()
    tile_conv(v.shift_grad, v.first_back, v.hidden)
    v.hidden_border[...] = border_of(v.hidden)
    sum_one.spread_column()
    halo.wait(3)
    came = v.arrived[3].reshape(128, 256)
    set_border(v.hidden, v.hidden_border[...] + dot(tables.cross_in[...], came))

    def finish(frame, pair, index, lanes, carry):
        field_grad_out[index] = v.hidden[rows_of(index)].astype(BF16)
        return carry

    each_pair(finish)
    sum_two.gather_plane()
    sum_one.gather_plane()
    halo.drain()
    sum_two.forward()
    sum_two.finish()
    sum_two_out[...] = sum_two.gathered[...].reshape(2 * HALF, 8, 128)
    sum_two.drain()
    sum_one.forward()
    sum_one.finish()
    sum_one_out[...] = sum_one.gathered[...].reshape(2 * HALF, 8, 128)
    sum_one.drain()


def store_kernel(scale, response, field_grad, sum_one, sum_two, response_out, field_grad_out,
                 kernel_one_out, bias_one_out, kernel_two_out, bias_two_out, kernel_one,
                 bias_one, kernel_two, bias_two, sems):
    stores = [
        pltpu.make_async_copy(response, response_out, sems.at[0]),
        pltpu.make_async_copy(field_grad, field_grad_out, sems.at[1]),
    ]
    for store in stores:
        store.start()
    for total, kernel, bias, kernel_out, bias_out in (
        (sum_one, kernel_one, bias_one, kernel_one_out, bias_one_out),
        (sum_two, kernel_two, bias_two, kernel_two_out, bias_two_out),
    ):
        kernel[...] = total[0:144].astype(F32) * scale
        bias[...] = total[144].astype(F32)[0:1] * scale
        for source, target in ((kernel, kernel_out), (bias, bias_out)):
            stores.append(pltpu.make_async_copy(source, target, sems.at[len(stores)]))
            stores[-1].start()
    for store in stores:
        store.wait()


def per_device(fields, cotangent, edge_map, w_first, b_first, w_second, b_second):
    frames, tile_side, channels = (fields.shape[2], fields.shape[3], fields.shape[5])
    samples = lax.axis_size("tile") * lax.axis_size("member") * frames * tile_side * tile_side
    kernel = jax.ShapeDtypeStruct((9 * channels // 8, 8, channels), F32)
    bias = jax.ShapeDtypeStruct((1, channels), F32)
    image = jax.ShapeDtypeStruct(IMAGE, BF16)
    local = pl.BlockSpec(memory_space=pltpu.VMEM)
    far = pl.BlockSpec(memory_space=pltpu.HBM)
    near = pltpu.VMEM(IMAGE, BF16)
    sums = pltpu.VMEM((2 * HALF, 8, 128), BF16)
    results = pl.pallas_call(
        step_kernel,
        out_shape=[near, near, sums, sums],
        in_specs=[
            pl.BlockSpec(memory_space=pltpu.SMEM),
            far,
            far,
            far,
            local,
            far,
            local,
        ],
        out_specs=[local] * 4,
        scratch_shapes=step_scratch(),
        compiler_params=pltpu.CompilerParams(
            collective_id=0, has_side_effects=True, vmem_limit_bytes=63_600 << 10
        ),
    )(
        edge_map.reshape(4, 2).T,
        fields.reshape(IMAGE),
        cotangent.reshape(IMAGE),
        w_first,
        b_first.reshape(1, channels),
        w_second,
        b_second.reshape(1, channels),
    )
    outs = pl.pallas_call(
        functools.partial(store_kernel, float(samples) ** -0.5),
        out_shape=[image, image, kernel, bias, kernel, bias],
        in_specs=[local] * 4,
        out_specs=[far] * 6,
        scratch_shapes=[
            pltpu.VMEM(kernel.shape, F32),
            pltpu.VMEM(bias.shape, F32),
            pltpu.VMEM(kernel.shape, F32),
            pltpu.VMEM(bias.shape, F32),
            pltpu.SemaphoreType.DMA((6,)),
        ],
        compiler_params=pltpu.CompilerParams(vmem_limit_bytes=8 << 20),
    )(*results)
    return (
        outs[0].reshape(fields.shape),
        outs[1].reshape(fields.shape),
        outs[2].reshape(w_first.shape),
        outs[3].reshape(b_first.shape),
        outs[4].reshape(w_second.shape),
        outs[5].reshape(b_second.shape),
    )


def solution(mesh):
    in_specs = (
        P("member", "tile", None, None, None, None),
        P("member", "tile", None, None, None, None),
        P("tile", None, None),
        P(),
        P(),
        P(),
        P(),
    )
    out_specs = (
        P("member", "tile", None, None, None, None),
        P("member", "tile", None, None, None, None),
        P(),
        P(),
        P(),
        P(),
    )
    return jax.shard_map(
        per_device, mesh=mesh, in_specs=in_specs, out_specs=out_specs, check_vma=False
    )
```

```python
import functools

import jax
import jax.numpy as jnp
from jax import lax
from jax.experimental import pallas as pl
from jax.experimental.pallas import tpu as pltpu
from jax.sharding import PartitionSpec as P

ROW_TILES = 8
ROOT_HALF = 0.7071067811865476
INV_ROOT_TAU = 0.3989422804014327
BF16 = jnp.bfloat16
F32 = jnp.float32

PLANE = 16
SIDE = 4
DEPTH = 8
PIECE = 5
HALF = PLANE * PIECE
PART_ROWS = 2 * HALF * 8


def coordinates():
    tile = lax.axis_index("tile")
    member = lax.axis_index("member")
    core = lax.rem(tile, 2)
    spot = lax.rem(tile // 2, PLANE)
    floor = tile // (2 * PLANE)
    return tile, member, core, spot, floor


def ring_hops(step, size):
    return min(step, size - step)


PLANE_STEPS = sorted(
    [(dx, dy) for dx in range(SIDE) for dy in range(SIDE) if (dx, dy) != (0, 0)],
    key=lambda step: -sum(ring_hops(part, SIDE) for part in step),
)
COLUMN_STEPS = sorted(range(1, DEPTH), key=lambda step: -ring_hops(step, DEPTH))


def moved(spot, step):
    across = lax.rem(spot // SIDE + step[0] + SIDE, SIDE)
    return across * SIDE + lax.rem(lax.rem(spot, SIDE) + step[1] + SIDE, SIDE)


def sum_partners():
    tile, member, core, spot, floor = coordinates()
    mate = (tile - core + (1 - core), member)
    plane = [
        ((floor * PLANE + moved(spot, step)) * 2 + core, member) for step in PLANE_STEPS
    ]
    level = floor * 2 + member
    column = []
    for step in COLUMN_STEPS:
        other = lax.rem(level + step, DEPTH)
        column.append((((other // 2) * PLANE + spot) * 2 + core, lax.rem(other, 2)))
    return mate, plane, column


def remote(source, target, send_sem, recv_sem, device):
    return pltpu.make_async_remote_copy(
        src_ref=source,
        dst_ref=target,
        send_sem=send_sem,
        recv_sem=recv_sem,
        device_id=device,
        device_id_type=pl.DeviceIdType.MESH,
    )


def sum_scratch():
    dma = pltpu.SemaphoreType.DMA
    return [
        pltpu.VMEM((2 * HALF, 8, 128), jnp.float32),
        pltpu.VMEM((2 * HALF, 8, 128), jnp.bfloat16),
        pltpu.VMEM((HALF, 8, 128), jnp.bfloat16),
        pltpu.VMEM((PLANE, PIECE, 8, 128), jnp.float32),
        pltpu.VMEM((PLANE, PIECE, 8, 128), jnp.bfloat16),
        pltpu.VMEM((PLANE, PIECE, 8, 128), jnp.bfloat16),
        pltpu.VMEM((DEPTH, PIECE, 8, 128), jnp.bfloat16),
        pltpu.VMEM((2, PLANE, PIECE, 8, 128), jnp.bfloat16),
        dma((2,)),
        dma((2,)),
        dma((2,)),
        dma((2,)),
        dma((2,)),
    ]


class GradientSum:
    def __init__(self, refs):
        (
            self.own,
            self.halves,
            self.from_mate,
            self.total,
            self.pieces,
            self.from_plane,
            self.from_column,
            self.gathered,
            self.mate_sem,
            self.plane_sem,
            self.column_sem,
            self.gather_sem,
            self.forward_sem,
        ) = refs
        tile, member, core, spot, floor = coordinates()
        self.core, self.spot, self.level = core, spot, floor * 2 + member
        self.mate, self.plane, self.column = sum_partners()

    def to_mate(self):
        return remote(
            self.halves.at[pl.ds((1 - self.core) * HALF, HALF)],
            self.from_mate,
            self.mate_sem.at[0],
            self.mate_sem.at[1],
            self.mate,
        )

    def to_plane(self, index):
        target = moved(self.spot, PLANE_STEPS[index])
        return remote(
            self.pieces.at[target],
            self.from_plane.at[self.spot],
            self.plane_sem.at[0],
            self.plane_sem.at[1],
            self.plane[index],
        )

    def to_column(self, index):
        return remote(
            self.from_column.at[self.level],
            self.from_column.at[self.level],
            self.column_sem.at[0],
            self.column_sem.at[1],
            self.column[index],
        )

    def to_gather(self, index):
        return remote(
            self.gathered.at[self.core, self.spot],
            self.gathered.at[self.core, self.spot],
            self.gather_sem.at[0],
            self.gather_sem.at[1],
            self.plane[index],
        )

    def to_forward(self):
        return remote(
            self.gathered.at[self.core],
            self.gathered.at[self.core],
            self.forward_sem.at[0],
            self.forward_sem.at[1],
            self.mate,
        )

    def wait_all(self, buffer, count, sem):
        pltpu.make_async_copy(
            buffer.at[pl.ds(0, count)], buffer.at[pl.ds(0, count)], sem
        ).wait()

    def start(self):
        self.halves[...] = self.own[...].astype(jnp.bfloat16)
        self.to_mate().start()

    def spread_plane(self):
        self.to_mate().wait_recv()
        total = self.own[pl.ds(self.core * HALF, HALF)] + self.from_mate[...].astype(jnp.float32)
        total = total.reshape(PLANE, PIECE, 8, 128)
        self.total[...] = total
        self.pieces[...] = total.astype(jnp.bfloat16)
        for index in range(PLANE - 1):
            self.to_plane(index).start()

    def spread_column(self):
        value = self.total[self.spot]
        self.wait_all(self.from_plane, PLANE - 1, self.plane_sem.at[1])
        for step in PLANE_STEPS:
            origin = moved(self.spot, step)
            value = value + self.from_plane[origin].astype(jnp.float32)
        self.from_column[self.level] = value.astype(jnp.bfloat16)
        for index in range(DEPTH - 1):
            self.to_column(index).start()

    def gather_plane(self):
        self.wait_all(self.from_column, DEPTH - 1, self.column_sem.at[1])
        value = jnp.zeros((PIECE, 8, 128), jnp.float32)
        for level in range(DEPTH):
            value = value + self.from_column[level].astype(jnp.float32)
        self.gathered[self.core, self.spot] = value.astype(jnp.bfloat16)
        for index in range(PLANE - 1):
            self.to_gather(index).start()

    def forward(self):
        self.wait_all(self.gathered.at[self.core], PLANE - 1, self.gather_sem.at[1])
        self.to_forward().start()

    def finish(self):
        self.to_forward().wait_recv()

    def drain(self):
        self.to_mate().wait_send()
        self.wait_all(self.pieces, PLANE - 1, self.plane_sem.at[0])
        self.wait_all(self.from_column, DEPTH - 1, self.column_sem.at[0])
        self.wait_all(self.gathered.at[self.core], PLANE - 1, self.gather_sem.at[0])
        self.to_forward().wait_send()


def dot(left, right):
    return jnp.dot(left, right, preferred_element_type=F32)


def dot_nt(left, right):
    return lax.dot_general(left, right, (((1,), (1,)), ((), ())), preferred_element_type=F32)


def dot_tn(left, right):
    return lax.dot_general(left, right, (((0,), (0,)), ((), ())), preferred_element_type=F32)


def iota(shape, axis):
    return lax.broadcasted_iota(jnp.int32, shape, axis)


def ones_where(mask):
    return jnp.where(mask, 1.0, 0.0).astype(BF16)


def border_pixel(side, place):
    return jnp.where(
        side == 0,
        place,
        jnp.where(side == 1, place * 32 + 31, jnp.where(side == 2, place + 992, place * 32)),
    )


def facing(edge_map, index):
    direction, place = index >> 5, index & 31
    side = jnp.zeros_like(index)
    flip = jnp.zeros_like(index)
    for candidate in range(4):
        side = jnp.where(direction == candidate, edge_map[0, candidate], side)
        flip = jnp.where(direction == candidate, edge_map[1, candidate], flip)
    return side, jnp.where(flip == 1, 31 - place, place)


def ring_taps(tap):
    row, lane = iota((128, 128), 0), iota((128, 128), 1)
    side, place = row >> 5, row & 31
    halo_side, halo_place = lane >> 5, lane & 31
    wanted = place + (tap - 1)
    whole = (halo_side == side) & (halo_place == wanted)
    along = (side == 0) | (side == 2)
    end = jnp.where(side == 0, 0, 31)
    low = ((halo_side == side) & (halo_place == 0)) | ((halo_side == 3) & (halo_place == end))
    high = ((halo_side == side) & (halo_place == 31)) | ((halo_side == 1) & (halo_place == end))
    half = along & (((wanted == -1) & low) | ((wanted == 32) & high))
    return jnp.where(whole, 1.0, jnp.where(half, 0.5, 0.0)).astype(BF16)


def side_tap(side, tap):
    return ((0, tap), (tap, 2), (2, tap), (tap, 0))[side]


def split_float(value):
    high = value.astype(BF16)
    low = (value - high.astype(F32)).astype(BF16)
    return jnp.concatenate([high, low], axis=0)


def make_tables(edge_map, t):
    row, lane = iota((128, 128), 0), iota((128, 128), 1)
    side, place = facing(edge_map, row)
    pixel = border_pixel(side, place)
    plain = border_pixel(row >> 5, row & 31)
    turn = ones_where(lane == side * 32 + place)
    t.turn[...] = turn
    for block in range(8):
        here = lane + block * 128
        t.pick[:, block * 128 : (block + 1) * 128] = ones_where(here == pixel)
        t.border[:, block * 128 : (block + 1) * 128] = ones_where(here == plain)
    cross = dot_nt(t.border[...], t.border[...]).astype(BF16)
    t.cross[:, 0:128] = cross
    t.cross[:, 128:256] = cross
    t.cross_in[...] = dot_nt(t.border[...], t.pick[...]).astype(BF16)
    for tap in range(3):
        taps = ring_taps(tap)
        t.ring[tap * 128 : (tap + 1) * 128, :] = dot_nt(taps, turn).astype(BF16)
        back = dot_nt(turn, taps).astype(BF16)
        t.ring_back[:, tap * 128 : (tap + 1) * 128] = back
        t.ring_back[:, 384 + tap * 128 : 384 + (tap + 1) * 128] = back


def lay_weights(target, block):
    empty = jnp.zeros((384, 128), BF16)
    target[0, :, 128:256] = empty
    target[3, :, 0:128] = empty
    for row in range(3):
        for col in range(3):
            part = block(row, col)
            target[row, col * 128 : (col + 1) * 128, 0:128] = part
            target[row + 1, col * 128 : (col + 1) * 128, 128:256] = part


def lay_shifted(target, frame, pair, value):
    col = iota((64, 128), 0) & 31
    before = jnp.where(col == 0, 0.0, pltpu.roll(value, 1, 0))
    after = jnp.where(col == 31, 0.0, pltpu.roll(value, 63, 0))
    for tap, part in enumerate((before, value, after)):
        target[tap, frame, pl.ds(1 + 2 * pair, 2)] = part.astype(BF16).reshape(2, 32, 128)


def lay_rows(target, frame, pair, value):
    part = value.reshape(2, 32, 128)
    for tap in range(3):
        target[tap, frame, pl.ds(2 * pair + tap, 2)] = part


def clear_rims(shifted):
    for tap in range(3):
        for frame in range(2):
            shifted[tap, frame, 0] = jnp.zeros((32, 128), BF16)
            shifted[tap, frame, 33] = jnp.zeros((32, 128), BF16)
            shifted[tap, frame, 34] = jnp.zeros((32, 128), BF16)


def tile_conv(shifted, weights, result):
    for frame in range(2):
        total = None
        for row in range(4):
            rows = jnp.concatenate(
                [
                    shifted[tap, frame, row : row + 32]
                    .reshape(16, 2, 32, 128)[:, 0]
                    .reshape(512, 128)
                    for tap in range(3)
                ],
                axis=1,
            )
            part = dot(rows, weights[row])
            total = part if total is None else total + part
        for pair in range(16):
            first = frame * 1024 + pair * 64
            rows = slice(pair * 32, (pair + 1) * 32)
            result[first : first + 32, :] = total[rows, 0:128]
            result[first + 32 : first + 64, :] = total[rows, 128:256]


def transpose_shifted(shifted, target):
    for frame in range(2):
        for tap in range(3):
            target[tap * 128 : (tap + 1) * 128, frame * 1024 : (frame + 1) * 1024] = (
                shifted[tap, frame, 1:33].reshape(1024, 128).T
            )


def picked(table, image):
    parts = [
        dot(table[...], image[frame * 16 : (frame + 1) * 16].reshape(1024, 128))
        for frame in range(2)
    ]
    return jnp.concatenate(parts, axis=1).astype(BF16)


def halo_share(t, arrived, weights, ring_rows):
    around = dot(t.ring[...], arrived[...].reshape(128, 256)).astype(BF16)
    parts = []
    for side in range(4):
        for frame in range(2):
            lanes = slice(frame * 128, (frame + 1) * 128)
            ring_rows[side, frame * 32 : (frame + 1) * 32, :] = jnp.concatenate(
                [
                    around[tap * 128 + side * 32 : tap * 128 + (side + 1) * 32, lanes]
                    for tap in range(3)
                ],
                axis=1,
            )
        taps = jnp.concatenate([weights[side_tap(side, tap)] for tap in range(3)], axis=0)
        value = dot(ring_rows[side], taps)
        parts.append(jnp.concatenate([value[0:32], value[32:64]], axis=1))
    return split_float(jnp.concatenate(parts, axis=0))


def lay_border(border, border_rows):
    for side in range(4):
        here = border[side * 32 : (side + 1) * 32]
        border_rows[side] = jnp.concatenate([here[:, 0:128], here[:, 128:256]], axis=0)


def ring_gradient(t, weights, border_rows, leaving):
    rows = [[None] * 4 for tap in range(3)]
    for side in range(4):
        for tap in range(3):
            value = dot_nt(border_rows[side], weights[side_tap(side, tap)])
            rows[tap][side] = jnp.concatenate([value[0:32], value[32:64]], axis=1)
    stacked = jnp.concatenate([rows[tap][side] for tap in range(3) for side in range(4)], axis=0)
    leaving[...] = dot(t.ring_back[...], split_float(stacked)).astype(BF16).reshape(4, 32, 256)


def turn_ring(ring_rows, ring_turned):
    for side in range(4):
        ring_turned[side] = ring_rows[side].T


def kernel_gradient(turned, spread_rows, ring_turned, border_rows, bias, own):
    total = None
    for frame in range(2):
        part = dot(
            turned[:, frame * 1024 : (frame + 1) * 1024],
            jnp.concatenate(
                [spread_rows[tap, frame, 1:33].reshape(1024, 128) for tap in range(3)], axis=1
            ),
        )
        total = part if total is None else total + part
    parts = [dot(ring_turned[side], border_rows[side]) for side in range(4)]
    for row in range(3):
        for col in range(3):
            value = total[col * 128 : (col + 1) * 128, row * 128 : (row + 1) * 128]
            for side in range(4):
                for tap in range(3):
                    if side_tap(side, tap) == (row, col):
                        value = value + parts[side][tap * 128 : (tap + 1) * 128]
            first = (row * 3 + col) * 16
            own[first : first + 16] = value.reshape(16, 8, 128)
    own[144] = jnp.concatenate([bias, jnp.zeros((7, 128), F32)], axis=0)
    own[145:160] = jnp.zeros((15, 8, 128), F32)


def halo_partners():
    tile, member, core, spot, floor = coordinates()
    count = 2 * PLANE * (DEPTH // 2)
    steps = (count - ROW_TILES, 1, ROW_TILES, count - 1)
    return [(lax.rem(tile + step, count), member) for step in steps]


class Halo:
    def __init__(self, leaving, arrived, send_sem, recv_sem):
        self.leaving, self.arrived = leaving, arrived
        self.send_sem, self.recv_sem = send_sem, recv_sem
        self.partners = halo_partners()

    def copies(self, turn):
        return [
            remote(
                self.leaving.at[turn, way],
                self.arrived.at[turn, (way + 2) % 4],
                self.send_sem.at[turn, way],
                self.recv_sem.at[turn, (way + 2) % 4],
                self.partners[way],
            )
            for way in (1, 3, 0, 2)
        ]

    def start(self, turn):
        for copy in self.copies(turn):
            copy.start()

    def wait(self, turn):
        for copy in self.copies(turn):
            copy.wait_recv()

    def drain(self):
        for turn in range(4):
            for copy in self.copies(turn):
                copy.wait_send()


TABLES = {
    "pick": (128, 1024),
    "border": (128, 1024),
    "turn": (128, 128),
    "cross": (128, 256),
    "cross_in": (128, 128),
    "ring": (384, 128),
    "ring_back": (128, 768),
}
IMAGE = (32, 64, 128)
SHIFTED = (3, 2, 36, 32, 128)
BUFFERS = {
    "source": (IMAGE, BF16),
    "upstream": (IMAGE, BF16),
    "first": ((3, 3, 128, 128), BF16),
    "second": ((3, 3, 128, 128), BF16),
    "first_fwd": ((4, 384, 256), BF16),
    "first_back": ((4, 384, 256), BF16),
    "second_fwd": ((4, 384, 256), BF16),
    "second_back": ((4, 384, 256), BF16),
    "shift_one": (SHIFTED, BF16),
    "shift_two": (SHIFTED, BF16),
    "shift_grad": (SHIFTED, BF16),
    "row_grad": ((3, 2, 34, 32, 128), BF16),
    "turned_one": ((384, 2048), BF16),
    "turned_two": ((384, 2048), BF16),
    "hidden": ((2048, 128), F32),
    "hidden_border": ((128, 256), F32),
    "slope_border": ((128, 256), F32),
    "upstream_border": ((128, 256), BF16),
    "grad": (IMAGE, BF16),
    "slope": (IMAGE, F32),
    "ring_one": ((4, 64, 384), BF16),
    "ring_two": ((4, 64, 384), BF16),
    "ring_turned_one": ((4, 384, 64), BF16),
    "ring_turned_two": ((4, 384, 64), BF16),
    "border_grad": ((4, 64, 128), BF16),
    "leaving": ((4, 4, 32, 256), BF16),
    "arrived": ((4, 4, 32, 256), BF16),
}


class Names:
    def __init__(self, names, refs):
        for name, ref in zip(names, refs):
            setattr(self, name, ref)


def step_scratch():
    dma = pltpu.SemaphoreType.DMA
    return (
        [pltpu.VMEM(shape, BF16) for shape in TABLES.values()]
        + [pltpu.VMEM(shape, kind) for shape, kind in BUFFERS.values()]
        + [dma((4, 4)), dma((4, 4)), dma((4,))]
        + sum_scratch()
        + sum_scratch()
    )


def gelu_parts(hidden):
    bell = 0.5 * (1.0 + lax.erf(hidden * ROOT_HALF))
    return hidden * bell, bell + hidden * jnp.exp(-0.5 * hidden * hidden) * INV_ROOT_TAU


def rows_of(index):
    return pl.ds(pl.multiple_of(index * 64, 64), 64)


def twice(bias):
    return jnp.concatenate([bias, bias], axis=1)


def border_of(image):
    frames = []
    for frame in range(2):
        first = frame * 1024
        frames.append(
            jnp.concatenate(
                [
                    image[first : first + 32, :],
                    image[pl.ds(first + 31, 32, stride=32), :],
                    image[first + 992 : first + 1024, :],
                    image[pl.ds(first, 32, stride=32), :],
                ],
                axis=0,
            )
        )
    return jnp.concatenate(frames, axis=1)


def set_border(image, border):
    for frame in range(2):
        first = frame * 1024
        part = border[:, frame * 128 : (frame + 1) * 128]
        image[first : first + 32, :] = part[0:32]
        image[pl.ds(first + 31, 32, stride=32), :] = part[32:64]
        image[first + 992 : first + 1024, :] = part[64:96]
        image[pl.ds(first, 32, stride=32), :] = part[96:128]


def each_pair(body, start=0):
    def step(pair, carry):
        for frame in range(2):
            carry = body(frame, pair, frame * 16 + pair, slice(frame * 128, (frame + 1) * 128), carry)
        return carry

    return lax.fori_loop(0, 16, step, start)


def fold_rows(value):
    return jnp.sum(value.reshape(8, 8, 128), axis=0)


def step_kernel(edge_map, fields, cotangent, w_first, b_first, w_second, b_second,
                response_out, field_grad_out, sum_one_out, sum_two_out, *scratch):
    tables, scratch = Names(TABLES, scratch), scratch[len(TABLES) :]
    v, scratch = Names(BUFFERS, scratch), scratch[len(BUFFERS) :]
    halo = Halo(v.leaving, v.arrived, scratch[0], scratch[1])
    local_sem, scratch = scratch[2], scratch[3:]
    count = len(sum_scratch())
    sum_one, sum_two = GradientSum(scratch[:count]), GradientSum(scratch[count:])

    mate, plane, column = sum_partners()
    partners = [*column, *halo_partners(), *plane, mate]
    barrier = pltpu.get_barrier_semaphore()
    for device in partners:
        pl.semaphore_signal(
            barrier, inc=1, device_id=device, device_id_type=pl.DeviceIdType.MESH
        )
    loads = [
        pltpu.make_async_copy(source, target, local_sem.at[index])
        for index, (source, target) in enumerate(
            ((fields, v.source), (w_first, v.first), (w_second, v.second), (cotangent, v.upstream))
        )
    ]
    for load in loads:
        load.start()
    make_tables(edge_map, tables)
    loads[0].wait()
    v.leaving[0] = picked(tables.pick, v.source).reshape(4, 32, 256)
    pl.semaphore_wait(barrier, len(partners))
    halo.start(0)

    for shifted in (v.shift_one, v.shift_two, v.shift_grad):
        clear_rims(shifted)
    for frame in range(2):
        v.row_grad[0, frame, 32:34] = jnp.zeros((2, 32, 128), BF16)
        v.row_grad[2, frame, 0:2] = jnp.zeros((2, 32, 128), BF16)

    def shift_source(frame, pair, index, lanes, carry):
        lay_shifted(v.shift_one, frame, pair, v.source[index].astype(F32))
        return carry

    each_pair(shift_source)
    loads[1].wait()
    lay_weights(v.first_fwd, lambda row, col: v.first[row, col])
    tile_conv(v.shift_one, v.first_fwd, v.hidden)
    v.hidden_border[...] = border_of(v.hidden)
    loads[2].wait()
    lay_weights(v.second_fwd, lambda row, col: v.second[row, col])
    loads[3].wait()
    v.upstream_border[...] = picked(tables.border, v.upstream)
    transpose_shifted(v.shift_one, v.turned_one)
    lay_weights(v.second_back, lambda row, col: v.second[2 - row, 2 - col].T)
    lay_weights(v.first_back, lambda row, col: v.first[2 - row, 2 - col].T)

    halo.wait(0)
    both = halo_share(tables, v.arrived.at[0], v.first, v.ring_one)
    border = v.hidden_border[...] + dot(tables.cross[...], both)
    v.hidden_border[...] = border
    value, slope = gelu_parts(border + twice(b_first[...]))
    v.leaving[1] = dot(tables.turn[...], value.astype(BF16)).astype(BF16).reshape(4, 32, 256)
    v.slope_border[...] = slope
    halo.start(1)
    set_border(v.hidden, v.hidden_border[...])

    def activate(frame, pair, index, lanes, carry):
        hidden = v.hidden[rows_of(index)] + b_first[...]
        value, slope = gelu_parts(hidden)
        v.slope[index] = slope
        lay_shifted(v.shift_two, frame, pair, value)
        return carry

    each_pair(activate)
    tile_conv(v.shift_two, v.second_fwd, v.hidden)
    v.hidden_border[...] = border_of(v.hidden)
    transpose_shifted(v.shift_two, v.turned_two)
    turn_ring(v.ring_one, v.ring_turned_one)

    halo.wait(1)
    both = halo_share(tables, v.arrived.at[1], v.second, v.ring_two)
    border = v.hidden_border[...] + dot(tables.cross[...], both)
    v.hidden_border[...] = border
    value, slope = gelu_parts(border + twice(b_second[...]))
    border = (v.upstream_border[...].astype(F32) * slope).astype(BF16)
    lay_border(border, v.border_grad)
    ring_gradient(tables, v.second, v.border_grad, v.leaving.at[2])
    halo.start(2)
    set_border(v.hidden, v.hidden_border[...])

    def respond(frame, pair, index, lanes, carry):
        hidden = v.hidden[rows_of(index)] + b_second[...]
        value, slope = gelu_parts(hidden)
        response_out[index] = value.astype(BF16)
        grad = (v.upstream[index].astype(F32) * slope).astype(BF16)
        wide = grad.astype(F32)
        lay_shifted(v.shift_grad, frame, pair, wide)
        lay_rows(v.row_grad, frame, pair, grad)
        return carry + fold_rows(wide)

    bias = each_pair(respond, jnp.zeros((8, 128), F32))
    bias = jnp.sum(bias, axis=0, keepdims=True)
    tile_conv(v.shift_grad, v.second_back, v.hidden)
    turn_ring(v.ring_two, v.ring_turned_two)
    v.hidden_border[...] = border_of(v.hidden)
    kernel_gradient(
        v.turned_two, v.row_grad, v.ring_turned_two, v.border_grad, bias, sum_two.own
    )
    sum_two.start()

    sum_two.spread_plane()

    halo.wait(2)
    came = v.arrived[2].reshape(128, 256)
    border = v.hidden_border[...] + dot(tables.cross_in[...], came)
    set_border(v.hidden, border)
    border = (border * v.slope_border[...]).astype(BF16)
    lay_border(border, v.border_grad)

    def descend(frame, pair, index, lanes, carry):
        grad = (v.hidden[rows_of(index)] * v.slope[index]).astype(BF16)
        v.grad[index] = grad
        lay_rows(v.row_grad, frame, pair, grad)
        return carry + fold_rows(grad.astype(F32))

    bias = each_pair(descend, jnp.zeros((8, 128), F32))
    bias = jnp.sum(bias, axis=0, keepdims=True)
    kernel_gradient(
        v.turned_one, v.row_grad, v.ring_turned_one, v.border_grad, bias, sum_one.own
    )
    sum_one.start()
    ring_gradient(tables, v.first, v.border_grad, v.leaving.at[3])
    halo.start(3)

    def shift_grad(frame, pair, index, lanes, carry):
        lay_shifted(v.shift_grad, frame, pair, v.grad[index].astype(F32))
        return carry

    sum_one.spread_plane()
    each_pair(shift_grad)
    sum_two.spread_column()
    tile_conv(v.shift_grad, v.first_back, v.hidden)
    v.hidden_border[...] = border_of(v.hidden)
    sum_one.spread_column()
    halo.wait(3)
    came = v.arrived[3].reshape(128, 256)
    set_border(v.hidden, v.hidden_border[...] + dot(tables.cross_in[...], came))

    def finish(frame, pair, index, lanes, carry):
        field_grad_out[index] = v.hidden[rows_of(index)].astype(BF16)
        return carry

    each_pair(finish)
    sum_two.gather_plane()
    sum_one.gather_plane()
    halo.drain()
    sum_two.forward()
    sum_two.finish()
    sum_two_out[...] = sum_two.gathered[...].reshape(2 * HALF, 8, 128)
    sum_two.drain()
    sum_one.forward()
    for core in (sum_one.core, 1 - sum_one.core):
        if core is not sum_one.core:
            sum_one.finish()
        sum_one_out[pl.ds(core * HALF, HALF)] = sum_one.gathered[core].reshape(HALF, 8, 128)
    sum_one.drain()


def store_kernel(scale, response, field_grad, sum_one, sum_two, response_out, field_grad_out,
                 kernel_one_out, bias_one_out, kernel_two_out, bias_two_out, kernel_one,
                 bias_one, kernel_two, bias_two, sems):
    stores = [
        pltpu.make_async_copy(response, response_out, sems.at[0]),
        pltpu.make_async_copy(field_grad, field_grad_out, sems.at[1]),
    ]
    for store in stores:
        store.start()
    for total, kernel, bias, kernel_out, bias_out in (
        (sum_one, kernel_one, bias_one, kernel_one_out, bias_one_out),
        (sum_two, kernel_two, bias_two, kernel_two_out, bias_two_out),
    ):
        kernel[...] = total[0:144].astype(F32) * scale
        bias[...] = total[144].astype(F32)[0:1] * scale
        for source, target in ((kernel, kernel_out), (bias, bias_out)):
            stores.append(pltpu.make_async_copy(source, target, sems.at[len(stores)]))
            stores[-1].start()
    for store in stores:
        store.wait()


def per_device(fields, cotangent, edge_map, w_first, b_first, w_second, b_second):
    frames, tile_side, channels = (fields.shape[2], fields.shape[3], fields.shape[5])
    samples = lax.axis_size("tile") * lax.axis_size("member") * frames * tile_side * tile_side
    kernel = jax.ShapeDtypeStruct((9 * channels // 8, 8, channels), F32)
    bias = jax.ShapeDtypeStruct((1, channels), F32)
    image = jax.ShapeDtypeStruct(IMAGE, BF16)
    local = pl.BlockSpec(memory_space=pltpu.VMEM)
    far = pl.BlockSpec(memory_space=pltpu.HBM)
    near = pltpu.VMEM(IMAGE, BF16)
    sums = pltpu.VMEM((2 * HALF, 8, 128), BF16)
    results = pl.pallas_call(
        step_kernel,
        out_shape=[near, near, sums, sums],
        in_specs=[
            pl.BlockSpec(memory_space=pltpu.SMEM),
            far,
            far,
            far,
            local,
            far,
            local,
        ],
        out_specs=[local] * 4,
        scratch_shapes=step_scratch(),
        compiler_params=pltpu.CompilerParams(
            collective_id=0, has_side_effects=True, vmem_limit_bytes=63_600 << 10
        ),
    )(
        edge_map.reshape(4, 2).T,
        fields.reshape(IMAGE),
        cotangent.reshape(IMAGE),
        w_first,
        b_first.reshape(1, channels),
        w_second,
        b_second.reshape(1, channels),
    )
    outs = pl.pallas_call(
        functools.partial(store_kernel, float(samples) ** -0.5),
        out_shape=[image, image, kernel, bias, kernel, bias],
        in_specs=[local] * 4,
        out_specs=[far] * 6,
        scratch_shapes=[
            pltpu.VMEM(kernel.shape, F32),
            pltpu.VMEM(bias.shape, F32),
            pltpu.VMEM(kernel.shape, F32),
            pltpu.VMEM(bias.shape, F32),
            pltpu.SemaphoreType.DMA((6,)),
        ],
        compiler_params=pltpu.CompilerParams(vmem_limit_bytes=8 << 20),
    )(*results)
    return (
        outs[0].reshape(fields.shape),
        outs[1].reshape(fields.shape),
        outs[2].reshape(w_first.shape),
        outs[3].reshape(b_first.shape),
        outs[4].reshape(w_second.shape),
        outs[5].reshape(b_second.shape),
    )


def solution(mesh):
    in_specs = (
        P("member", "tile", None, None, None, None),
        P("member", "tile", None, None, None, None),
        P("tile", None, None),
        P(),
        P(),
        P(),
        P(),
    )
    out_specs = (
        P("member", "tile", None, None, None, None),
        P("member", "tile", None, None, None, None),
        P(),
        P(),
        P(),
        P(),
    )
    return jax.shard_map(
        per_device, mesh=mesh, in_specs=in_specs, out_specs=out_specs, check_vma=False
    )
```

```python
import functools

import jax
import jax.numpy as jnp
from jax import lax
from jax.experimental import pallas as pl
from jax.experimental.pallas import tpu as pltpu
from jax.sharding import PartitionSpec as P

ROW_TILES = 8
ROOT_HALF = 0.7071067811865476
INV_ROOT_TAU = 0.3989422804014327
BF16 = jnp.bfloat16
F32 = jnp.float32

PLANE = 16
SIDE = 4
DEPTH = 8
PIECE = 5
HALF = PLANE * PIECE
PART_ROWS = 2 * HALF * 8


def coordinates():
    tile = lax.axis_index("tile")
    member = lax.axis_index("member")
    core = lax.rem(tile, 2)
    spot = lax.rem(tile // 2, PLANE)
    floor = tile // (2 * PLANE)
    return tile, member, core, spot, floor


def ring_hops(step, size):
    return min(step, size - step)


PLANE_STEPS = sorted(
    [(dx, dy) for dx in range(SIDE) for dy in range(SIDE) if (dx, dy) != (0, 0)],
    key=lambda step: -sum(ring_hops(part, SIDE) for part in step),
)
COLUMN_STEPS = sorted(range(1, DEPTH), key=lambda step: -ring_hops(step, DEPTH))


def moved(spot, step):
    across = lax.rem(spot // SIDE + step[0] + SIDE, SIDE)
    return across * SIDE + lax.rem(lax.rem(spot, SIDE) + step[1] + SIDE, SIDE)


def sum_partners():
    tile, member, core, spot, floor = coordinates()
    mate = (tile - core + (1 - core), member)
    plane = [
        ((floor * PLANE + moved(spot, step)) * 2 + core, member) for step in PLANE_STEPS
    ]
    level = floor * 2 + member
    column = []
    for step in COLUMN_STEPS:
        other = lax.rem(level + step, DEPTH)
        column.append((((other // 2) * PLANE + spot) * 2 + core, lax.rem(other, 2)))
    return mate, plane, column


def remote(source, target, send_sem, recv_sem, device):
    return pltpu.make_async_remote_copy(
        src_ref=source,
        dst_ref=target,
        send_sem=send_sem,
        recv_sem=recv_sem,
        device_id=device,
        device_id_type=pl.DeviceIdType.MESH,
    )


def sum_scratch():
    dma = pltpu.SemaphoreType.DMA
    return [
        pltpu.VMEM((2 * HALF, 8, 128), jnp.float32),
        pltpu.VMEM((2 * HALF, 8, 128), jnp.bfloat16),
        pltpu.VMEM((HALF, 8, 128), jnp.bfloat16),
        pltpu.VMEM((PLANE, PIECE, 8, 128), jnp.float32),
        pltpu.VMEM((PLANE, PIECE, 8, 128), jnp.bfloat16),
        pltpu.VMEM((PLANE, PIECE, 8, 128), jnp.bfloat16),
        pltpu.VMEM((DEPTH, PIECE, 8, 128), jnp.bfloat16),
        pltpu.VMEM((2, PLANE, PIECE, 8, 128), jnp.bfloat16),
        dma((2,)),
        dma((2,)),
        dma((2,)),
        dma((2,)),
        dma((2,)),
    ]


class GradientSum:
    def __init__(self, refs):
        (
            self.own,
            self.halves,
            self.from_mate,
            self.total,
            self.pieces,
            self.from_plane,
            self.from_column,
            self.gathered,
            self.mate_sem,
            self.plane_sem,
            self.column_sem,
            self.gather_sem,
            self.forward_sem,
        ) = refs
        tile, member, core, spot, floor = coordinates()
        self.core, self.spot, self.level = core, spot, floor * 2 + member
        self.mate, self.plane, self.column = sum_partners()

    def to_mate(self):
        return remote(
            self.halves.at[pl.ds((1 - self.core) * HALF, HALF)],
            self.from_mate,
            self.mate_sem.at[0],
            self.mate_sem.at[1],
            self.mate,
        )

    def to_plane(self, index):
        target = moved(self.spot, PLANE_STEPS[index])
        return remote(
            self.pieces.at[target],
            self.from_plane.at[self.spot],
            self.plane_sem.at[0],
            self.plane_sem.at[1],
            self.plane[index],
        )

    def to_column(self, index):
        return remote(
            self.from_column.at[self.level],
            self.from_column.at[self.level],
            self.column_sem.at[0],
            self.column_sem.at[1],
            self.column[index],
        )

    def to_gather(self, index):
        return remote(
            self.gathered.at[self.core, self.spot],
            self.gathered.at[self.core, self.spot],
            self.gather_sem.at[0],
            self.gather_sem.at[1],
            self.plane[index],
        )

    def to_forward(self):
        return remote(
            self.gathered.at[self.core],
            self.gathered.at[self.core],
            self.forward_sem.at[0],
            self.forward_sem.at[1],
            self.mate,
        )

    def wait_all(self, buffer, count, sem):
        pltpu.make_async_copy(
            buffer.at[pl.ds(0, count)], buffer.at[pl.ds(0, count)], sem
        ).wait()

    def start(self):
        theirs = pl.ds((1 - self.core) * HALF, HALF)
        self.halves[theirs] = self.own[theirs].astype(jnp.bfloat16)
        self.to_mate().start()

    def spread_plane(self):
        self.to_mate().wait_recv()
        total = self.own[pl.ds(self.core * HALF, HALF)] + self.from_mate[...].astype(jnp.float32)
        total = total.reshape(PLANE, PIECE, 8, 128)
        self.total[...] = total
        self.pieces[...] = total.astype(jnp.bfloat16)
        for index in range(PLANE - 1):
            self.to_plane(index).start()

    def spread_column(self):
        value = self.total[self.spot]
        self.wait_all(self.from_plane, PLANE - 1, self.plane_sem.at[1])
        for step in PLANE_STEPS:
            origin = moved(self.spot, step)
            value = value + self.from_plane[origin].astype(jnp.float32)
        self.from_column[self.level] = value.astype(jnp.bfloat16)
        for index in range(DEPTH - 1):
            self.to_column(index).start()

    def gather_plane(self):
        self.wait_all(self.from_column, DEPTH - 1, self.column_sem.at[1])
        value = jnp.zeros((PIECE, 8, 128), jnp.float32)
        for level in range(DEPTH):
            value = value + self.from_column[level].astype(jnp.float32)
        self.gathered[self.core, self.spot] = value.astype(jnp.bfloat16)
        for index in range(PLANE - 1):
            self.to_gather(index).start()

    def forward(self):
        self.wait_all(self.gathered.at[self.core], PLANE - 1, self.gather_sem.at[1])
        self.to_forward().start()

    def finish(self):
        self.to_forward().wait_recv()

    def drain(self):
        self.to_mate().wait_send()
        self.wait_all(self.pieces, PLANE - 1, self.plane_sem.at[0])
        self.wait_all(self.from_column, DEPTH - 1, self.column_sem.at[0])
        self.wait_all(self.gathered.at[self.core], PLANE - 1, self.gather_sem.at[0])
        self.to_forward().wait_send()


def dot(left, right):
    return jnp.dot(left, right, preferred_element_type=F32)


def dot_nt(left, right):
    return lax.dot_general(left, right, (((1,), (1,)), ((), ())), preferred_element_type=F32)


def dot_tn(left, right):
    return lax.dot_general(left, right, (((0,), (0,)), ((), ())), preferred_element_type=F32)


def iota(shape, axis):
    return lax.broadcasted_iota(jnp.int32, shape, axis)


def ones_where(mask):
    return jnp.where(mask, 1.0, 0.0).astype(BF16)


def border_pixel(side, place):
    return jnp.where(
        side == 0,
        place,
        jnp.where(side == 1, place * 32 + 31, jnp.where(side == 2, place + 992, place * 32)),
    )


def facing(edge_map, index):
    direction, place = index >> 5, index & 31
    side = jnp.zeros_like(index)
    flip = jnp.zeros_like(index)
    for candidate in range(4):
        side = jnp.where(direction == candidate, edge_map[0, candidate], side)
        flip = jnp.where(direction == candidate, edge_map[1, candidate], flip)
    return side, jnp.where(flip == 1, 31 - place, place)


def ring_taps(tap):
    row, lane = iota((128, 128), 0), iota((128, 128), 1)
    side, place = row >> 5, row & 31
    halo_side, halo_place = lane >> 5, lane & 31
    wanted = place + (tap - 1)
    whole = (halo_side == side) & (halo_place == wanted)
    along = (side == 0) | (side == 2)
    end = jnp.where(side == 0, 0, 31)
    low = ((halo_side == side) & (halo_place == 0)) | ((halo_side == 3) & (halo_place == end))
    high = ((halo_side == side) & (halo_place == 31)) | ((halo_side == 1) & (halo_place == end))
    half = along & (((wanted == -1) & low) | ((wanted == 32) & high))
    return jnp.where(whole, 1.0, jnp.where(half, 0.5, 0.0)).astype(BF16)


def side_tap(side, tap):
    return ((0, tap), (tap, 2), (2, tap), (tap, 0))[side]


def split_float(value):
    high = value.astype(BF16)
    low = (value - high.astype(F32)).astype(BF16)
    return jnp.concatenate([high, low], axis=0)


def make_tables(edge_map, t):
    row, lane = iota((128, 128), 0), iota((128, 128), 1)
    side, place = facing(edge_map, row)
    pixel = border_pixel(side, place)
    plain = border_pixel(row >> 5, row & 31)
    turn = ones_where(lane == side * 32 + place)
    t.turn[...] = turn
    for block in range(8):
        here = lane + block * 128
        t.pick[:, block * 128 : (block + 1) * 128] = ones_where(here == pixel)
        t.border[:, block * 128 : (block + 1) * 128] = ones_where(here == plain)
    cross = dot_nt(t.border[...], t.border[...]).astype(BF16)
    t.cross[:, 0:128] = cross
    t.cross[:, 128:256] = cross
    t.cross_in[...] = dot_nt(t.border[...], t.pick[...]).astype(BF16)
    for tap in range(3):
        taps = ring_taps(tap)
        t.ring[tap * 128 : (tap + 1) * 128, :] = dot_nt(taps, turn).astype(BF16)
        back = dot_nt(turn, taps).astype(BF16)
        t.ring_back[:, tap * 128 : (tap + 1) * 128] = back
        t.ring_back[:, 384 + tap * 128 : 384 + (tap + 1) * 128] = back


def lay_weights(target, block):
    empty = jnp.zeros((384, 128), BF16)
    target[0, :, 128:256] = empty
    target[3, :, 0:128] = empty
    for row in range(3):
        for col in range(3):
            part = block(row, col)
            target[row, col * 128 : (col + 1) * 128, 0:128] = part
            target[row + 1, col * 128 : (col + 1) * 128, 128:256] = part


def lay_shifted(target, frame, pair, value):
    col = iota((64, 128), 0) & 31
    before = jnp.where(col == 0, 0.0, pltpu.roll(value, 1, 0))
    after = jnp.where(col == 31, 0.0, pltpu.roll(value, 63, 0))
    for tap, part in enumerate((before, value, after)):
        target[tap, frame, pl.ds(1 + 2 * pair, 2)] = part.astype(BF16).reshape(2, 32, 128)


def lay_rows(target, frame, pair, value):
    part = value.reshape(2, 32, 128)
    for tap in range(3):
        target[tap, frame, pl.ds(2 * pair + tap, 2)] = part


def clear_rims(shifted):
    for tap in range(3):
        for frame in range(2):
            shifted[tap, frame, 0] = jnp.zeros((32, 128), BF16)
            shifted[tap, frame, 33] = jnp.zeros((32, 128), BF16)
            shifted[tap, frame, 34] = jnp.zeros((32, 128), BF16)


def tile_conv(shifted, weights, result):
    for frame in range(2):
        total = None
        for row in range(4):
            rows = jnp.concatenate(
                [
                    shifted[tap, frame, row : row + 32]
                    .reshape(16, 2, 32, 128)[:, 0]
                    .reshape(512, 128)
                    for tap in range(3)
                ],
                axis=1,
            )
            part = dot(rows, weights[row])
            total = part if total is None else total + part
        for pair in range(16):
            first = frame * 1024 + pair * 64
            rows = slice(pair * 32, (pair + 1) * 32)
            result[first : first + 32, :] = total[rows, 0:128]
            result[first + 32 : first + 64, :] = total[rows, 128:256]


def transpose_shifted(shifted, target):
    for frame in range(2):
        for tap in range(3):
            target[tap * 128 : (tap + 1) * 128, frame * 1024 : (frame + 1) * 1024] = (
                shifted[tap, frame, 1:33].reshape(1024, 128).T
            )


def picked(table, image):
    parts = [
        dot(table[...], image[frame * 16 : (frame + 1) * 16].reshape(1024, 128))
        for frame in range(2)
    ]
    return jnp.concatenate(parts, axis=1).astype(BF16)


def halo_share(t, arrived, weights, ring_rows):
    around = dot(t.ring[...], arrived[...].reshape(128, 256)).astype(BF16)
    parts = []
    for side in range(4):
        for frame in range(2):
            lanes = slice(frame * 128, (frame + 1) * 128)
            ring_rows[side, frame * 32 : (frame + 1) * 32, :] = jnp.concatenate(
                [
                    around[tap * 128 + side * 32 : tap * 128 + (side + 1) * 32, lanes]
                    for tap in range(3)
                ],
                axis=1,
            )
        taps = jnp.concatenate([weights[side_tap(side, tap)] for tap in range(3)], axis=0)
        value = dot(ring_rows[side], taps)
        parts.append(jnp.concatenate([value[0:32], value[32:64]], axis=1))
    return split_float(jnp.concatenate(parts, axis=0))


def lay_border(border, border_rows):
    for side in range(4):
        here = border[side * 32 : (side + 1) * 32]
        border_rows[side] = jnp.concatenate([here[:, 0:128], here[:, 128:256]], axis=0)


def ring_gradient(t, weights, border_rows, leaving):
    rows = [[None] * 4 for tap in range(3)]
    for side in range(4):
        for tap in range(3):
            value = dot_nt(border_rows[side], weights[side_tap(side, tap)])
            rows[tap][side] = jnp.concatenate([value[0:32], value[32:64]], axis=1)
    stacked = jnp.concatenate([rows[tap][side] for tap in range(3) for side in range(4)], axis=0)
    leaving[...] = dot(t.ring_back[...], split_float(stacked)).astype(BF16).reshape(4, 32, 256)


def turn_ring(ring_rows, ring_turned):
    for side in range(4):
        ring_turned[side] = ring_rows[side].T


def kernel_gradient(turned, spread_rows, ring_turned, border_rows, bias, own):
    total = None
    for frame in range(2):
        part = dot(
            turned[:, frame * 1024 : (frame + 1) * 1024],
            jnp.concatenate(
                [spread_rows[tap, frame, 1:33].reshape(1024, 128) for tap in range(3)], axis=1
            ),
        )
        total = part if total is None else total + part
    parts = [dot(ring_turned[side], border_rows[side]) for side in range(4)]
    for row in range(3):
        for col in range(3):
            value = total[col * 128 : (col + 1) * 128, row * 128 : (row + 1) * 128]
            for side in range(4):
                for tap in range(3):
                    if side_tap(side, tap) == (row, col):
                        value = value + parts[side][tap * 128 : (tap + 1) * 128]
            first = (row * 3 + col) * 16
            own[first : first + 16] = value.reshape(16, 8, 128)
    own[144] = jnp.concatenate([bias, jnp.zeros((7, 128), F32)], axis=0)
    own[145:160] = jnp.zeros((15, 8, 128), F32)


def halo_partners():
    tile, member, core, spot, floor = coordinates()
    count = 2 * PLANE * (DEPTH // 2)
    steps = (count - ROW_TILES, 1, ROW_TILES, count - 1)
    return [(lax.rem(tile + step, count), member) for step in steps]


class Halo:
    def __init__(self, leaving, arrived, send_sem, recv_sem):
        self.leaving, self.arrived = leaving, arrived
        self.send_sem, self.recv_sem = send_sem, recv_sem
        self.partners = halo_partners()

    def copies(self, turn):
        return [
            remote(
                self.leaving.at[turn, way],
                self.arrived.at[turn, (way + 2) % 4],
                self.send_sem.at[turn, way],
                self.recv_sem.at[turn, (way + 2) % 4],
                self.partners[way],
            )
            for way in (1, 3, 0, 2)
        ]

    def start(self, turn):
        for copy in self.copies(turn):
            copy.start()

    def wait(self, turn):
        for copy in self.copies(turn):
            copy.wait_recv()

    def drain(self):
        for turn in range(4):
            for copy in self.copies(turn):
                copy.wait_send()


TABLES = {
    "pick": (128, 1024),
    "border": (128, 1024),
    "turn": (128, 128),
    "cross": (128, 256),
    "cross_in": (128, 128),
    "ring": (384, 128),
    "ring_back": (128, 768),
}
IMAGE = (32, 64, 128)
SHIFTED = (3, 2, 36, 32, 128)
BUFFERS = {
    "source": (IMAGE, BF16),
    "upstream": (IMAGE, BF16),
    "first": ((3, 3, 128, 128), BF16),
    "second": ((3, 3, 128, 128), BF16),
    "first_fwd": ((4, 384, 256), BF16),
    "first_back": ((4, 384, 256), BF16),
    "second_fwd": ((4, 384, 256), BF16),
    "second_back": ((4, 384, 256), BF16),
    "shift_one": (SHIFTED, BF16),
    "shift_two": (SHIFTED, BF16),
    "shift_grad": (SHIFTED, BF16),
    "row_grad": ((3, 2, 34, 32, 128), BF16),
    "turned_one": ((384, 2048), BF16),
    "turned_two": ((384, 2048), BF16),
    "hidden": ((2048, 128), F32),
    "hidden_border": ((128, 256), F32),
    "slope_border": ((128, 256), F32),
    "upstream_border": ((128, 256), BF16),
    "grad": (IMAGE, BF16),
    "slope": (IMAGE, F32),
    "ring_one": ((4, 64, 384), BF16),
    "ring_two": ((4, 64, 384), BF16),
    "ring_turned_one": ((4, 384, 64), BF16),
    "ring_turned_two": ((4, 384, 64), BF16),
    "border_grad": ((4, 64, 128), BF16),
    "leaving": ((4, 4, 32, 256), BF16),
    "arrived": ((4, 4, 32, 256), BF16),
}


class Names:
    def __init__(self, names, refs):
        for name, ref in zip(names, refs):
            setattr(self, name, ref)


def step_scratch():
    dma = pltpu.SemaphoreType.DMA
    return (
        [pltpu.VMEM(shape, BF16) for shape in TABLES.values()]
        + [pltpu.VMEM(shape, kind) for shape, kind in BUFFERS.values()]
        + [dma((4, 4)), dma((4, 4)), dma((4,))]
        + sum_scratch()
        + sum_scratch()
    )


def gelu_parts(hidden):
    bell = 0.5 * (1.0 + lax.erf(hidden * ROOT_HALF))
    return hidden * bell, bell + hidden * jnp.exp(-0.5 * hidden * hidden) * INV_ROOT_TAU


def rows_of(index):
    return pl.ds(pl.multiple_of(index * 64, 64), 64)


def twice(bias):
    return jnp.concatenate([bias, bias], axis=1)


def border_of(image):
    frames = []
    for frame in range(2):
        first = frame * 1024
        frames.append(
            jnp.concatenate(
                [
                    image[first : first + 32, :],
                    image[pl.ds(first + 31, 32, stride=32), :],
                    image[first + 992 : first + 1024, :],
                    image[pl.ds(first, 32, stride=32), :],
                ],
                axis=0,
            )
        )
    return jnp.concatenate(frames, axis=1)


def set_border(image, border):
    for frame in range(2):
        first = frame * 1024
        part = border[:, frame * 128 : (frame + 1) * 128]
        image[first : first + 32, :] = part[0:32]
        image[pl.ds(first + 31, 32, stride=32), :] = part[32:64]
        image[first + 992 : first + 1024, :] = part[64:96]
        image[pl.ds(first, 32, stride=32), :] = part[96:128]


def each_pair(body, start=0):
    def step(pair, carry):
        for frame in range(2):
            carry = body(frame, pair, frame * 16 + pair, slice(frame * 128, (frame + 1) * 128), carry)
        return carry

    return lax.fori_loop(0, 16, step, start)


def fold_rows(value):
    return jnp.sum(value.reshape(8, 8, 128), axis=0)


def step_kernel(edge_map, fields, cotangent, w_first, b_first, w_second, b_second,
                response_out, field_grad_out, sum_one_out, sum_two_out, *scratch):
    tables, scratch = Names(TABLES, scratch), scratch[len(TABLES) :]
    v, scratch = Names(BUFFERS, scratch), scratch[len(BUFFERS) :]
    halo = Halo(v.leaving, v.arrived, scratch[0], scratch[1])
    local_sem, scratch = scratch[2], scratch[3:]
    count = len(sum_scratch())
    sum_one, sum_two = GradientSum(scratch[:count]), GradientSum(scratch[count:])

    mate, plane, column = sum_partners()
    partners = [*halo_partners(), *column, *plane, mate]
    barrier = pltpu.get_barrier_semaphore()
    for device in partners:
        pl.semaphore_signal(
            barrier, inc=1, device_id=device, device_id_type=pl.DeviceIdType.MESH
        )
    loads = [
        pltpu.make_async_copy(source, target, local_sem.at[index])
        for index, (source, target) in enumerate(
            ((fields, v.source), (w_first, v.first), (w_second, v.second), (cotangent, v.upstream))
        )
    ]
    for load in loads:
        load.start()
    make_tables(edge_map, tables)
    loads[0].wait()
    v.leaving[0] = picked(tables.pick, v.source).reshape(4, 32, 256)
    pl.semaphore_wait(barrier, len(partners))
    halo.start(0)

    for shifted in (v.shift_one, v.shift_two, v.shift_grad):
        clear_rims(shifted)
    for frame in range(2):
        v.row_grad[0, frame, 32:34] = jnp.zeros((2, 32, 128), BF16)
        v.row_grad[2, frame, 0:2] = jnp.zeros((2, 32, 128), BF16)

    def shift_source(frame, pair, index, lanes, carry):
        lay_shifted(v.shift_one, frame, pair, v.source[index].astype(F32))
        return carry

    each_pair(shift_source)
    loads[1].wait()
    lay_weights(v.first_fwd, lambda row, col: v.first[row, col])
    tile_conv(v.shift_one, v.first_fwd, v.hidden)
    v.hidden_border[...] = border_of(v.hidden)
    loads[2].wait()
    lay_weights(v.second_fwd, lambda row, col: v.second[row, col])
    loads[3].wait()
    v.upstream_border[...] = picked(tables.border, v.upstream)
    transpose_shifted(v.shift_one, v.turned_one)
    lay_weights(v.second_back, lambda row, col: v.second[2 - row, 2 - col].T)
    lay_weights(v.first_back, lambda row, col: v.first[2 - row, 2 - col].T)

    halo.wait(0)
    both = halo_share(tables, v.arrived.at[0], v.first, v.ring_one)
    border = v.hidden_border[...] + dot(tables.cross[...], both)
    v.hidden_border[...] = border
    value, slope = gelu_parts(border + twice(b_first[...]))
    v.leaving[1] = dot(tables.turn[...], value.astype(BF16)).astype(BF16).reshape(4, 32, 256)
    v.slope_border[...] = slope
    halo.start(1)
    set_border(v.hidden, v.hidden_border[...])

    def activate(frame, pair, index, lanes, carry):
        hidden = v.hidden[rows_of(index)] + b_first[...]
        value, slope = gelu_parts(hidden)
        v.slope[index] = slope
        lay_shifted(v.shift_two, frame, pair, value)
        return carry

    each_pair(activate)
    tile_conv(v.shift_two, v.second_fwd, v.hidden)
    v.hidden_border[...] = border_of(v.hidden)
    transpose_shifted(v.shift_two, v.turned_two)
    turn_ring(v.ring_one, v.ring_turned_one)

    halo.wait(1)
    both = halo_share(tables, v.arrived.at[1], v.second, v.ring_two)
    border = v.hidden_border[...] + dot(tables.cross[...], both)
    v.hidden_border[...] = border
    value, slope = gelu_parts(border + twice(b_second[...]))
    border = (v.upstream_border[...].astype(F32) * slope).astype(BF16)
    lay_border(border, v.border_grad)
    ring_gradient(tables, v.second, v.border_grad, v.leaving.at[2])
    halo.start(2)
    set_border(v.hidden, v.hidden_border[...])

    def respond(frame, pair, index, lanes, carry):
        hidden = v.hidden[rows_of(index)] + b_second[...]
        value, slope = gelu_parts(hidden)
        response_out[index] = value.astype(BF16)
        grad = (v.upstream[index].astype(F32) * slope).astype(BF16)
        wide = grad.astype(F32)
        lay_shifted(v.shift_grad, frame, pair, wide)
        lay_rows(v.row_grad, frame, pair, grad)
        return carry + fold_rows(wide)

    bias = each_pair(respond, jnp.zeros((8, 128), F32))
    bias = jnp.sum(bias, axis=0, keepdims=True)
    tile_conv(v.shift_grad, v.second_back, v.hidden)
    turn_ring(v.ring_two, v.ring_turned_two)
    v.hidden_border[...] = border_of(v.hidden)
    kernel_gradient(
        v.turned_two, v.row_grad, v.ring_turned_two, v.border_grad, bias, sum_two.own
    )
    sum_two.start()

    sum_two.spread_plane()

    halo.wait(2)
    came = v.arrived[2].reshape(128, 256)
    border = v.hidden_border[...] + dot(tables.cross_in[...], came)
    set_border(v.hidden, border)
    border = (border * v.slope_border[...]).astype(BF16)
    lay_border(border, v.border_grad)

    def descend(frame, pair, index, lanes, carry):
        grad = (v.hidden[rows_of(index)] * v.slope[index]).astype(BF16)
        v.grad[index] = grad
        lay_rows(v.row_grad, frame, pair, grad)
        return carry + fold_rows(grad.astype(F32))

    bias = each_pair(descend, jnp.zeros((8, 128), F32))
    bias = jnp.sum(bias, axis=0, keepdims=True)
    kernel_gradient(
        v.turned_one, v.row_grad, v.ring_turned_one, v.border_grad, bias, sum_one.own
    )
    sum_one.start()
    ring_gradient(tables, v.first, v.border_grad, v.leaving.at[3])
    halo.start(3)

    def shift_grad(frame, pair, index, lanes, carry):
        lay_shifted(v.shift_grad, frame, pair, v.grad[index].astype(F32))
        return carry

    sum_one.spread_plane()
    each_pair(shift_grad)
    sum_two.spread_column()
    tile_conv(v.shift_grad, v.first_back, v.hidden)
    v.hidden_border[...] = border_of(v.hidden)
    sum_one.spread_column()
    halo.wait(3)
    came = v.arrived[3].reshape(128, 256)
    set_border(v.hidden, v.hidden_border[...] + dot(tables.cross_in[...], came))

    def finish(frame, pair, index, lanes, carry):
        field_grad_out[index] = v.hidden[rows_of(index)].astype(BF16)
        return carry

    each_pair(finish)
    sum_two.gather_plane()
    sum_one.gather_plane()
    halo.drain()
    sum_two.forward()
    sum_two.finish()
    sum_two_out[...] = sum_two.gathered[...].reshape(2 * HALF, 8, 128)
    sum_two.drain()
    sum_one.forward()
    for core in (sum_one.core, 1 - sum_one.core):
        if core is not sum_one.core:
            sum_one.finish()
        sum_one_out[pl.ds(core * HALF, HALF)] = sum_one.gathered[core].reshape(HALF, 8, 128)
    sum_one.drain()


def store_kernel(scale, response, field_grad, sum_one, sum_two, response_out, field_grad_out,
                 kernel_one_out, bias_one_out, kernel_two_out, bias_two_out, kernel_one,
                 bias_one, kernel_two, bias_two, sems):
    stores = [
        pltpu.make_async_copy(response, response_out, sems.at[0]),
        pltpu.make_async_copy(field_grad, field_grad_out, sems.at[1]),
    ]
    for store in stores:
        store.start()
    for total, kernel, bias, kernel_out, bias_out in (
        (sum_one, kernel_one, bias_one, kernel_one_out, bias_one_out),
        (sum_two, kernel_two, bias_two, kernel_two_out, bias_two_out),
    ):
        kernel[...] = total[0:144].astype(F32) * scale
        bias[...] = total[144].astype(F32)[0:1] * scale
        for source, target in ((kernel, kernel_out), (bias, bias_out)):
            stores.append(pltpu.make_async_copy(source, target, sems.at[len(stores)]))
            stores[-1].start()
    for store in stores:
        store.wait()


def per_device(fields, cotangent, edge_map, w_first, b_first, w_second, b_second):
    frames, tile_side, channels = (fields.shape[2], fields.shape[3], fields.shape[5])
    samples = lax.axis_size("tile") * lax.axis_size("member") * frames * tile_side * tile_side
    kernel = jax.ShapeDtypeStruct((9 * channels // 8, 8, channels), F32)
    bias = jax.ShapeDtypeStruct((1, channels), F32)
    image = jax.ShapeDtypeStruct(IMAGE, BF16)
    local = pl.BlockSpec(memory_space=pltpu.VMEM)
    far = pl.BlockSpec(memory_space=pltpu.HBM)
    near = pltpu.VMEM(IMAGE, BF16)
    sums = pltpu.VMEM((2 * HALF, 8, 128), BF16)
    results = pl.pallas_call(
        step_kernel,
        out_shape=[near, near, sums, sums],
        in_specs=[
            pl.BlockSpec(memory_space=pltpu.SMEM),
            far,
            far,
            far,
            local,
            far,
            local,
        ],
        out_specs=[local] * 4,
        scratch_shapes=step_scratch(),
        compiler_params=pltpu.CompilerParams(
            collective_id=0, has_side_effects=True, vmem_limit_bytes=63_600 << 10
        ),
    )(
        edge_map.reshape(4, 2).T,
        fields.reshape(IMAGE),
        cotangent.reshape(IMAGE),
        w_first,
        b_first.reshape(1, channels),
        w_second,
        b_second.reshape(1, channels),
    )
    outs = pl.pallas_call(
        functools.partial(store_kernel, float(samples) ** -0.5),
        out_shape=[image, image, kernel, bias, kernel, bias],
        in_specs=[local] * 4,
        out_specs=[far] * 6,
        scratch_shapes=[
            pltpu.VMEM(kernel.shape, F32),
            pltpu.VMEM(bias.shape, F32),
            pltpu.VMEM(kernel.shape, F32),
            pltpu.VMEM(bias.shape, F32),
            pltpu.SemaphoreType.DMA((6,)),
        ],
        compiler_params=pltpu.CompilerParams(vmem_limit_bytes=8 << 20),
    )(*results)
    return (
        outs[0].reshape(fields.shape),
        outs[1].reshape(fields.shape),
        outs[2].reshape(w_first.shape),
        outs[3].reshape(b_first.shape),
        outs[4].reshape(w_second.shape),
        outs[5].reshape(b_second.shape),
    )


def solution(mesh):
    in_specs = (
        P("member", "tile", None, None, None, None),
        P("member", "tile", None, None, None, None),
        P("tile", None, None),
        P(),
        P(),
        P(),
        P(),
    )
    out_specs = (
        P("member", "tile", None, None, None, None),
        P("member", "tile", None, None, None, None),
        P(),
        P(),
        P(),
        P(),
    )
    return jax.shard_map(
        per_device, mesh=mesh, in_specs=in_specs, out_specs=out_specs, check_vma=False
    )
```
